256 devices in a mesh: depth: 16 (over x, z_lo), plane: 16 (over z_hi, y, core).
Axes of the slice: x: 4, y: 4, z: 8 (z_hi: 2, z_lo: 4; z = z_hi * 4 + z_lo), core: 2. Of those that a mesh axis runs over, the one named last changes fastest.
Arguments:
- spectrum: bfloat16 [32, 2, 1024, 2048], P('depth', None, 'plane'), may hold values from -6 to 6
- colour_table: float32 [4, 4, 16], replicated, may hold values from 0 to 1
- map_index: int32 [32], P('depth'), may hold values from 0 to 3
Outputs:
- final_image: float32 [4, 2048, 2048], P(None, 'plane', 'depth')
The draws below stay inside these ranges and needn't reach their ends.
Inputs may be any that keep to these rules, and one draw needn't show every extreme that they name: `map_index`: which of the 4 colour maps each depth plane uses.
All inputs are finite; a program needn't handle non-finite values.
Results may differ from the reference program's by a relative error of at most 0.0034.
Values may be sent and summed in bfloat16 or wider, within the bound.
A program may use at most 64 MiB of HBM per device.

```python
import math
import jax
import jax.numpy as jnp
from jax import lax

NX = 2048
NY = 2048
NCTRL = 16
NMAPS = 4
KY = 1024
NZ = 32


def with_ends(array, rng, least, high):
    longest = array.shape.index(max(array.shape))
    spots = []
    for shift in (0, 1):
        where = [jax.random.randint(jax.random.fold_in(rng, axis), (), 0, length) for axis, length in enumerate(array.shape)]
        where[longest] = (where[longest] + shift) % array.shape[longest]
        spots.append(tuple(where))
    return array.at[spots[0]].set(least).at[spots[1]].set(high)


def level_of(rng, dims, shards, low, top_value):
    loudness, own = 1.0, jax.random.fold_in(rng, 6)
    for dim, blocks in shards:
        draws = jnp.exp(jax.random.uniform(jax.random.fold_in(own, dim), (blocks,), jnp.float32, low / len(shards), top_value / len(shards)))
        loudness = loudness * jnp.repeat(draws, dims[dim] // blocks).reshape([-1 if axis == dim else 1 for axis in range(len(dims))])
    return loudness


def centred(stream_key, shape, width, bound, cuts=(), kind=jnp.bfloat16):
    entries = width * jax.random.normal(stream_key, shape, jnp.float32)
    if cuts:
        entries = entries * level_of(stream_key, shape, cuts, -0.22, 0.18)
    return jnp.clip(entries, -bound, bound).astype(kind)


def setup_inputs(seed: int = 0) -> dict:
    key_list = jax.random.split(jax.random.key(seed), 4)
    return {
        "spectrum": centred(key_list[0], (NZ, 2, KY, NX), 1.0, 6.0, ((0, 16), (2, 16))),
        "colour_table": jnp.clip(jax.random.uniform(key_list[1], (NMAPS, 4, NCTRL), jnp.float32, 0.0, 1.0), 0.0, 1.0),
        "map_index": with_ends(jax.random.randint(key_list[2], (NZ,), 0, NMAPS), jax.random.fold_in(key_list[2], 1), 0, NMAPS - 1).astype(jnp.int32),
    }


SPREAD = 3.0
OPACITY = 0.06

def angle_grid(row_count, col_count, length):
    row_index = jnp.arange(row_count, dtype=jnp.int32)[:, None]
    col_index = jnp.arange(col_count, dtype=jnp.int32)[None, :]
    residue = (row_index * col_index % length).astype(jnp.int32)
    return residue.astype(jnp.float32) * (2.0 * math.pi / length)

def x_table_make():
    angles = angle_grid(NX, NX, NX)
    return (jnp.concatenate([jnp.cos(angles), jnp.sin(angles)], axis=1) * (1.0 / math.sqrt(NX))).astype(jnp.bfloat16)

def y_table_make():
    angles = angle_grid(NY // 2, NY, NY)
    return (jnp.stack([jnp.cos(angles), -jnp.sin(angles)]) * math.sqrt(2.0 / NY)).astype(jnp.bfloat16)

def composite(nearer, farther, channel_axis):
    color_near = lax.slice_in_dim(nearer, 0, 3, axis=channel_axis)
    trans_near = lax.slice_in_dim(nearer, 3, 4, axis=channel_axis)
    color_far = lax.slice_in_dim(farther, 0, 3, axis=channel_axis)
    trans_far = lax.slice_in_dim(farther, 3, 4, axis=channel_axis)
    return jnp.concatenate([color_near + trans_near * color_far, trans_near * trans_far], axis=channel_axis)

def pick_colours(colour_table, which_map):
    onehot = (which_map[:, None] == jnp.arange(NMAPS, dtype=jnp.int32)[None, :]).astype(jnp.float32)
    return jnp.einsum('zm,mqj->zqj', onehot, colour_table, precision=lax.Precision.HIGHEST)

def shade_planes(density, colours):
    position = jnp.clip((density + SPREAD) * ((NCTRL - 1) / (2.0 * SPREAD)), 0.0, NCTRL - 1.0)
    knot_points = jnp.arange(NCTRL, dtype=jnp.float32)
    weights = jnp.maximum(0.0, 1.0 - jnp.abs(position[:, None] - knot_points[None, :, None, None]))
    values = jnp.einsum('zjxy,zqj->zqxy', weights, colours, precision=lax.Precision.HIGHEST)
    opacity = OPACITY * values[:, 3]
    emission = values[:, :3] * opacity[:, None]
    return jnp.concatenate([emission, (1.0 - opacity)[:, None]], axis=1)

def reference(spectrum, colour_table, map_index):
    x_table = x_table_make()
    y_table = y_table_make().astype(jnp.float32)
    half = NY // 2

    def one_plane(running, inputs):
        spec_plane, which_map = inputs
        flat_spec = spec_plane.reshape(2 * half, NX)
        products = jnp.dot(flat_spec, x_table, preferred_element_type=jnp.float32).reshape(2, half, 2, NX)
        real_part = products[0, :, 0] - products[1, :, 1]
        imag_part = products[0, :, 1] + products[1, :, 0]
        grid_rows = jnp.stack([real_part, imag_part]).astype(jnp.bfloat16)
        density = jnp.einsum('ckx,cky->xy', grid_rows.astype(jnp.float32), y_table, precision=lax.Precision.HIGHEST)
        colours = pick_colours(colour_table, which_map[None])
        plane_layer = shade_planes(density[None], colours)[0]
        return (composite(running, plane_layer, 0), None)
    start = jnp.concatenate([jnp.zeros((3, NX, NY), jnp.float32), jnp.ones((1, NX, NY), jnp.float32)], axis=0)
    final_image, unused = lax.scan(one_plane, start, (spectrum, map_index))
    return final_image
```

```python
import functools
import math

import jax
import jax.numpy as jnp
import numpy as np
from jax import lax
from jax.experimental import pallas as pl
from jax.experimental.pallas import tpu as pltpu
from jax.sharding import PartitionSpec as P

NX = 2048
NY = 2048
NCTRL = 16
NMAPS = 4
SPREAD = 3.0
OPACITY = 0.06
LANES = 128
FINE = 16
CHUNKS = 2
MESH = pl.DeviceIdType.MESH


def base_tables():
    fine = 2.0 * np.pi * np.outer(np.arange(FINE), np.arange(NX)) / NX
    coarse = 2.0 * np.pi * (np.outer(np.arange(128), np.arange(128)) % 128) / 128.0
    fine_pair = np.stack([np.cos(fine), np.sin(fine)]).astype(np.float32)
    coarse_pair = np.stack([np.cos(coarse), np.sin(coarse)]).astype(np.float32)
    return fine_pair, coarse_pair


def kernel(
    spec_ref, colour_ref, map_ref, fine_ref, coarse_ref, out_ref,
    swap_ref, cos_ref, sin_ref, send1, recv1, ytab, lhs, ctab, dens, send2, recv2,
    send_sem, recv1_sem, recv2_sem, tab_sem, *, comm
):
    if comm:
        depth_id = lax.axis_index("depth")
        plane_id = lax.axis_index("plane")
    else:
        depth_id = jnp.int32(5)
        plane_id = jnp.int32(6)
    my_x, my_zl = depth_id // 4, depth_id % 4
    my_zh, my_j = plane_id // 8, plane_id % 8
    my_z = my_zh * 4 + my_zl

    def same_x(z, j):
        return {"depth": my_x * 4 + z % 4, "plane": (z // 4) * 8 + j}

    def same_plane(x, zl):
        return {"depth": x * 4 + zl, "plane": plane_id}

    if comm:
        barrier = pltpu.get_barrier_semaphore()

        def greet_gather(i, carry):
            z, j = (my_z + i // 8) % 8, (my_j + i % 8) % 8
            pl.semaphore_signal(barrier, inc=1, device_id=same_x(z, j), device_id_type=MESH)
            return carry

        def greet_depth(i, carry):
            x, zl = (my_x + 1 + i // 4) % 4, i % 4
            pl.semaphore_signal(barrier, inc=1, device_id=same_plane(x, zl), device_id_type=MESH)
            return carry

        lax.fori_loop(1, 64, greet_gather, 0)
        lax.fori_loop(0, 12, greet_depth, 0)

    for z in range(2):
        swap_ref[z * 128 : z * 128 + 64, :] = -spec_ref[z, 1]
        swap_ref[z * 128 + 64 : z * 128 + 128, :] = spec_ref[z, 0]

    for z in range(2):
        values = colour_ref[map_ref[z]]
        values = jnp.concatenate([values, jnp.zeros((4, LANES - NCTRL), jnp.float32)], axis=1)
        row = lax.broadcasted_iota(jnp.int32, (4, LANES), 0)
        values = jnp.where(row == 3, values * OPACITY, values)
        slopes = pltpu.roll(values, LANES - 1, 1) - values
        ctab[my_zl, z] = jnp.concatenate([values, slopes], axis=0)

    if comm:
        pl.semaphore_wait(barrier, 75)
        for k in range(1, 4):
            pltpu.make_async_remote_copy(
                src_ref=ctab.at[my_zl], dst_ref=ctab.at[my_zl], send_sem=send_sem.at[2 * CHUNKS],
                recv_sem=tab_sem, device_id=same_plane(my_x, (my_zl + k) % 4), device_id_type=MESH,
            ).start()

    x_scale = 1.0 / math.sqrt(NX)
    y_scale = math.sqrt(2.0 / NY)

    def coarse_row(index, scale):
        bc = coarse_ref[0, pl.ds(index, 1), :] * scale
        bs = coarse_ref[1, pl.ds(index, 1), :] * scale
        return jnp.broadcast_to(bc, (FINE, LANES)), jnp.broadcast_to(bs, (FINE, LANES))

    def transform_x(step, carry):
        chunk, k = step // 8, step % 8
        z = (my_z + 4 + ((k + 1) // 2) * (1 - 2 * (k % 2))) % 8
        first = (z // 4) * 64 + 2 * (z % 4) + chunk
        for j in range(8):
            bc, bs = coarse_row(first + 8 * j, x_scale)
            for b in range(NX // LANES):
                cols = slice(b * LANES, (b + 1) * LANES)
                ec, es = fine_ref[0, :, cols], fine_ref[1, :, cols]
                cos_ref[j * FINE : (j + 1) * FINE, cols] = (bc * ec - bs * es).astype(jnp.bfloat16)
                sin_ref[j * FINE : (j + 1) * FINE, cols] = (bs * ec + bc * es).astype(jnp.bfloat16)
        nt = (((1,), (1,)), ((), ()))
        spec = spec_ref[...].reshape(256, NX)
        rows = lax.dot_general(cos_ref[...], spec, nt, preferred_element_type=jnp.float32)
        rows += lax.dot_general(sin_ref[...], swap_ref[...], nt, preferred_element_type=jnp.float32)
        rows = rows.astype(jnp.bfloat16).reshape(8, FINE, 256)
        send1[chunk, k] = rows
        if comm:
            def send(i, c):
                j = (my_j + i) % 8

                @pl.when(jnp.logical_or(k != 7, i != 0))
                def _():
                    pltpu.make_async_remote_copy(
                        src_ref=send1.at[chunk, k, j], dst_ref=recv1.at[chunk, my_zl * 16 + plane_id],
                        send_sem=send_sem.at[chunk], recv_sem=recv1_sem.at[chunk],
                        device_id=same_x(z, j), device_id_type=MESH,
                    ).start()

                return c

            lax.fori_loop(0, 8, send, 0)

        @pl.when(k == 7)
        def _():
            recv1[chunk, my_zl * 16 + plane_id] = send1[chunk, k, my_j]

        return carry

    lax.fori_loop(0, 8 * CHUNKS, transform_x, 0)

    def make_y(a, carry):
        bc, bs = coarse_row(a, y_scale)
        base = pl.multiple_of((a // 4) * 128 + (a % 4) * FINE, FINE)
        for b in range(NY // LANES):
            cols = slice(b * LANES, (b + 1) * LANES)
            ec, es = fine_ref[0, :, cols], fine_ref[1, :, cols]
            part = slice((b % 2) * LANES, (b % 2 + 1) * LANES)
            ytab[b // 2, pl.ds(base, FINE), part] = (bc * ec - bs * es).astype(jnp.bfloat16)
            ytab[b // 2, pl.ds(base + 64, FINE), part] = (-(bs * ec + bc * es)).astype(jnp.bfloat16)
        return carry

    lax.fori_loop(0, 64, make_y, 0)

    if comm:
        pltpu.make_async_remote_copy(
            src_ref=ctab.at[pl.ds(0, 3)], dst_ref=ctab.at[pl.ds(0, 3)], send_sem=send_sem.at[2 * CHUNKS],
            recv_sem=tab_sem, device_id=same_plane(my_x, (my_zl + 1) % 4), device_id_type=MESH,
        ).wait_recv()

    for chunk in range(CHUNKS):
        if comm:
            pltpu.make_async_remote_copy(
                src_ref=recv1.at[chunk, pl.ds(0, 63)], dst_ref=recv1.at[chunk, pl.ds(0, 63)],
                send_sem=send_sem.at[chunk], recv_sem=recv1_sem.at[chunk],
                device_id=same_x((my_z + 1) % 8, my_j), device_id_type=MESH,
            ).wait_recv()
        for zl in range(4):
            for z in range(2):
                for p in range(16):
                    lhs[(2 * zl + z) * FINE : (2 * zl + z + 1) * FINE, p * LANES : (p + 1) * LANES] = (
                        recv1[chunk, zl * 16 + p, :, z * LANES : (z + 1) * LANES]
                    )

        def columns(step, carry, chunk=chunk):
            block = (depth_id // 2 + 1 + step) % 8
            dens[...] = jnp.dot(lhs[...], ytab[block], preferred_element_type=jnp.float32)
            tiles = [(r, c) for c in range(2) for r in range(2)]
            colour = {t: [jnp.zeros((8, LANES), jnp.float32) for _ in range(3)] for t in tiles}
            clear = {t: jnp.ones((8, LANES), jnp.float32) for t in tiles}
            for z in range(8):
                maps = [
                    jnp.broadcast_to(ctab[z // 2, z % 2, q : q + 1, :], (8, LANES)) for q in range(8)
                ]
                for r, c in tiles:
                    d = dens[z * FINE + 8 * r : z * FINE + 8 * r + 8, c * LANES : (c + 1) * LANES]
                    position = jnp.clip((d + SPREAD) * ((NCTRL - 1) / (2.0 * SPREAD)), 0.0, NCTRL - 1.0)
                    index = position.astype(jnp.int32)
                    frac = position - index.astype(jnp.float32)
                    value = [
                        jnp.take_along_axis(maps[q], index, axis=1, mode="promise_in_bounds")
                        + frac * jnp.take_along_axis(maps[q + 4], index, axis=1, mode="promise_in_bounds")
                        for q in range(4)
                    ]
                    weight = clear[r, c] * value[3]
                    colour[r, c] = [colour[r, c][q] + weight * value[q] for q in range(3)]
                    clear[r, c] = clear[r, c] - weight
            for c in range(2):
                d = block * 2 + c
                for q in range(4):
                    both = jnp.concatenate(
                        [colour[r, c][q] if q < 3 else 1.0 - clear[r, c] for r in range(2)], axis=0
                    )
                    send2[chunk, d, q] = both.astype(jnp.bfloat16)
                x, zl = d // 4, d % 4
                if comm:
                    @pl.when(d != depth_id)
                    def _():
                        pltpu.make_async_remote_copy(
                            src_ref=send2.at[chunk, d], dst_ref=recv2.at[chunk, depth_id],
                            send_sem=send_sem.at[CHUNKS + chunk], recv_sem=recv2_sem.at[chunk],
                            device_id=same_plane(x, zl), device_id_type=MESH,
                        ).start()
            return carry

        lax.fori_loop(0, 8, columns, 0)
        recv2[chunk, depth_id] = send2[chunk, depth_id]

    for chunk in range(CHUNKS):
        if comm:
            pltpu.make_async_remote_copy(
                src_ref=recv2.at[chunk, pl.ds(0, 15)], dst_ref=recv2.at[chunk, pl.ds(0, 15)],
                send_sem=send_sem.at[CHUNKS + chunk], recv_sem=recv2_sem.at[chunk],
                device_id=same_plane((my_x + 1) % 4, my_zl), device_id_type=MESH,
            ).wait_recv()
        for zl in range(4):
            rows = slice(zl * 32 + chunk * FINE, zl * 32 + (chunk + 1) * FINE)
            total = [recv2[chunk, zl, q].astype(jnp.float32) for q in range(3)]
            clear = 1.0 - recv2[chunk, zl, 3].astype(jnp.float32)
            for x in range(1, 4):
                for q in range(3):
                    total[q] = total[q] + clear * recv2[chunk, 4 * x + zl, q].astype(jnp.float32)
                clear = clear * (1.0 - recv2[chunk, 4 * x + zl, 3].astype(jnp.float32))
            for q in range(3):
                out_ref[q, rows, :] = total[q]
            out_ref[3, rows, :] = clear

    if comm:
        for chunk in range(CHUNKS):
            pltpu.make_async_remote_copy(
                src_ref=recv1.at[chunk, pl.ds(0, 63)], dst_ref=recv1.at[chunk, pl.ds(0, 63)],
                send_sem=send_sem.at[chunk], recv_sem=recv1_sem.at[chunk],
                device_id=same_x((my_z + 1) % 8, my_j), device_id_type=MESH,
            ).wait_send()
            pltpu.make_async_remote_copy(
                src_ref=recv2.at[chunk, pl.ds(0, 15)], dst_ref=recv2.at[chunk, pl.ds(0, 15)],
                send_sem=send_sem.at[CHUNKS + chunk], recv_sem=recv2_sem.at[chunk],
                device_id=same_plane((my_x + 1) % 4, my_zl), device_id_type=MESH,
            ).wait_send()
        pltpu.make_async_remote_copy(
            src_ref=ctab.at[pl.ds(0, 3)], dst_ref=ctab.at[pl.ds(0, 3)], send_sem=send_sem.at[2 * CHUNKS],
            recv_sem=tab_sem, device_id=same_plane(my_x, (my_zl + 1) % 4), device_id_type=MESH,
        ).wait_send()


def render(spectrum, colour_table, map_index, comm=True):
    fine_pair, coarse_pair = base_tables()
    vmem = pl.BlockSpec(memory_space=pltpu.VMEM)
    bf16, f32 = jnp.bfloat16, jnp.float32
    return pl.pallas_call(
        functools.partial(kernel, comm=comm),
        out_shape=jax.ShapeDtypeStruct((4, 128, 128), f32),
        in_specs=[vmem, vmem, pl.BlockSpec(memory_space=pltpu.SMEM), vmem, vmem],
        out_specs=vmem,
        scratch_shapes=[
            pltpu.VMEM((256, NX), bf16),
            pltpu.VMEM((128, NX), bf16),
            pltpu.VMEM((128, NX), bf16),
            pltpu.VMEM((CHUNKS, 8, 8, FINE, 256), bf16),
            pltpu.VMEM((CHUNKS, 64, FINE, 256), bf16),
            pltpu.VMEM((8, NY, 256), bf16),
            pltpu.VMEM((128, NY), bf16),
            pltpu.VMEM((4, 2, 8, LANES), f32),
            pltpu.VMEM((128, 256), f32),
            pltpu.VMEM((CHUNKS, 16, 4, FINE, LANES), bf16),
            pltpu.VMEM((CHUNKS, 16, 4, FINE, LANES), bf16),
            pltpu.SemaphoreType.DMA((2 * CHUNKS + 1,)),
            pltpu.SemaphoreType.DMA((CHUNKS,)),
            pltpu.SemaphoreType.DMA((CHUNKS,)),
            pltpu.SemaphoreType.DMA,
        ],
        compiler_params=pltpu.CompilerParams(
            vmem_limit_bytes=40 << 20,
            **(dict(collective_id=0, has_side_effects=True) if comm else {}),
        ),
        name="render",
    )(spectrum, colour_table, map_index, jnp.asarray(fine_pair), jnp.asarray(coarse_pair))


def solution(mesh):
    return jax.shard_map(
        render,
        mesh=mesh,
        in_specs=(P("depth", None, "plane", None), P(), P("depth")),
        out_specs=P(None, "plane", "depth"),
        check_vma=False,
    )
```

```python
import functools
import math

import jax
import jax.numpy as jnp
import numpy as np
from jax import lax
from jax.experimental import pallas as pl
from jax.experimental.pallas import tpu as pltpu
from jax.sharding import PartitionSpec as P

NX = 2048
NY = 2048
NCTRL = 16
NMAPS = 4
SPREAD = 3.0
OPACITY = 0.06
LANES = 128
FINE = 16
CHUNKS = 2
MESH = pl.DeviceIdType.MESH


def base_tables():
    fine = 2.0 * np.pi * np.outer(np.arange(FINE), np.arange(NX)) / NX
    coarse = 2.0 * np.pi * (np.outer(np.arange(128), np.arange(128)) % 128) / 128.0
    fine_pair = np.stack([np.cos(fine), np.sin(fine)]).astype(np.float32)
    coarse_pair = np.stack([np.cos(coarse), np.sin(coarse)]).astype(np.float32)
    return fine_pair, coarse_pair


def kernel(
    spec_hbm, colour_hbm, map_hbm, fine_hbm, coarse_hbm, out_ref,
    spec_ref, colour_ref, map_ref, fine_ref, coarse_ref,
    swap_ref, cos_ref, sin_ref, send1, recv1, ytab, lhs, ctab, dens, send2, recv2, send3,
    in_sem, send_sem, recv1_sem, recv2_sem, recv3_sem, tab_sem, *, comm
):
    if comm:
        depth_id = lax.axis_index("depth")
        plane_id = lax.axis_index("plane")
    else:
        depth_id = jnp.int32(5)
        plane_id = jnp.int32(6)
    my_x, my_zl = depth_id // 4, depth_id % 4
    my_zh, my_j = plane_id // 8, plane_id % 8
    my_z = my_zh * 4 + my_zl

    fetches = [
        pltpu.make_async_copy(src, dst, in_sem.at[i])
        for i, (src, dst) in enumerate(
            [(spec_hbm, spec_ref), (fine_hbm, fine_ref), (coarse_hbm, coarse_ref),
             (colour_hbm, colour_ref), (map_hbm, map_ref)]
        )
    ]
    for fetch in fetches:
        fetch.start()

    def same_x(z, j):
        return {"depth": my_x * 4 + z % 4, "plane": (z // 4) * 8 + j}

    def same_plane(x, zl):
        return {"depth": x * 4 + zl, "plane": plane_id}

    if comm:
        barrier = pltpu.get_barrier_semaphore()

        def greet_gather(i, carry):
            z, j = (my_z + i // 8) % 8, (my_j + i % 8) % 8
            pl.semaphore_signal(barrier, inc=1, device_id=same_x(z, j), device_id_type=MESH)
            return carry

        def greet_depth(i, carry):
            pl.semaphore_signal(
                barrier, inc=1, device_id=same_plane((my_x + i) % 4, my_zl), device_id_type=MESH
            )
            return carry

        lax.fori_loop(1, 64, greet_gather, 0)
        lax.fori_loop(1, 4, greet_depth, 0)

    for fetch in fetches:
        fetch.wait()

    for z in range(2):
        swap_ref[z * 128 : z * 128 + 64, :] = -spec_ref[z, 1]
        swap_ref[z * 128 + 64 : z * 128 + 128, :] = spec_ref[z, 0]

    for z in range(2):
        values = colour_ref[map_ref[z]]
        values = jnp.concatenate([values, jnp.zeros((4, LANES - NCTRL), jnp.float32)], axis=1)
        row = lax.broadcasted_iota(jnp.int32, (4, LANES), 0)
        values = jnp.where(row == 3, values * OPACITY, values)
        slopes = pltpu.roll(values, LANES - 1, 1) - values
        ctab[my_zl, z] = jnp.concatenate([values, slopes], axis=0)

    if comm:
        pl.semaphore_wait(barrier, 66)
        for k in range(1, 4):
            pltpu.make_async_remote_copy(
                src_ref=ctab.at[my_zl], dst_ref=ctab.at[my_zl], send_sem=send_sem.at[3 * CHUNKS],
                recv_sem=tab_sem, device_id=same_plane(my_x, (my_zl + k) % 4), device_id_type=MESH,
            ).start()

    x_scale = 1.0 / math.sqrt(NX)
    y_scale = math.sqrt(2.0 / NY)

    def coarse_row(index, scale):
        bc = coarse_ref[0, pl.ds(index, 1), :] * scale
        bs = coarse_ref[1, pl.ds(index, 1), :] * scale
        return jnp.broadcast_to(bc, (FINE, LANES)), jnp.broadcast_to(bs, (FINE, LANES))

    def transform_x(step, carry):
        chunk, k = step // 8, step % 8
        z = (my_z + 4 + ((k + 1) // 2) * (1 - 2 * (k % 2))) % 8
        first = (z // 4) * 64 + 2 * (z % 4) + chunk
        for j in range(8):
            bc, bs = coarse_row(first + 8 * j, x_scale)
            for b in range(NX // LANES):
                cols = slice(b * LANES, (b + 1) * LANES)
                ec, es = fine_ref[0, :, cols], fine_ref[1, :, cols]
                cos_ref[j * FINE : (j + 1) * FINE, cols] = (bc * ec - bs * es).astype(jnp.bfloat16)
                sin_ref[j * FINE : (j + 1) * FINE, cols] = (bs * ec + bc * es).astype(jnp.bfloat16)
        nt = (((1,), (1,)), ((), ()))
        spec = spec_ref[...].reshape(256, NX)
        rows = lax.dot_general(cos_ref[...], spec, nt, preferred_element_type=jnp.float32)
        rows += lax.dot_general(sin_ref[...], swap_ref[...], nt, preferred_element_type=jnp.float32)
        rows = rows.astype(jnp.bfloat16).reshape(8, FINE, 256)
        send1[chunk, k] = rows
        if comm:
            def send(i, c):
                j = (my_j + i) % 8

                @pl.when(jnp.logical_or(k != 7, i != 0))
                def _():
                    pltpu.make_async_remote_copy(
                        src_ref=send1.at[chunk, k, j], dst_ref=recv1.at[chunk, my_zl * 16 + plane_id],
                        send_sem=send_sem.at[chunk], recv_sem=recv1_sem.at[chunk],
                        device_id=same_x(z, j), device_id_type=MESH,
                    ).start()

                return c

            lax.fori_loop(0, 8, send, 0)

        @pl.when(k == 7)
        def _():
            recv1[chunk, my_zl * 16 + plane_id] = send1[chunk, k, my_j]

        return carry

    lax.fori_loop(0, 8 * CHUNKS, transform_x, 0)

    def make_y(a, carry):
        bc, bs = coarse_row(a, y_scale)
        base = pl.multiple_of((a // 4) * 128 + (a % 4) * FINE, FINE)
        for b in range(NY // LANES):
            cols = slice(b * LANES, (b + 1) * LANES)
            ec, es = fine_ref[0, :, cols], fine_ref[1, :, cols]
            part = slice((b % 2) * LANES, (b % 2 + 1) * LANES)
            ytab[b // 2, pl.ds(base, FINE), part] = (bc * ec - bs * es).astype(jnp.bfloat16)
            ytab[b // 2, pl.ds(base + 64, FINE), part] = (-(bs * ec + bc * es)).astype(jnp.bfloat16)
        return carry

    lax.fori_loop(0, 64, make_y, 0)

    if comm:
        pltpu.make_async_remote_copy(
            src_ref=ctab.at[pl.ds(0, 3)], dst_ref=ctab.at[pl.ds(0, 3)], send_sem=send_sem.at[3 * CHUNKS],
            recv_sem=tab_sem, device_id=same_plane(my_x, (my_zl + 1) % 4), device_id_type=MESH,
        ).wait_recv()

    for chunk in range(CHUNKS):
        if comm:
            pltpu.make_async_remote_copy(
                src_ref=recv1.at[chunk, pl.ds(0, 63)], dst_ref=recv1.at[chunk, pl.ds(0, 63)],
                send_sem=send_sem.at[chunk], recv_sem=recv1_sem.at[chunk],
                device_id=same_x((my_z + 1) % 8, my_j), device_id_type=MESH,
            ).wait_recv()
        for zl in range(4):
            for z in range(2):
                for p in range(16):
                    lhs[(2 * zl + z) * FINE : (2 * zl + z + 1) * FINE, p * LANES : (p + 1) * LANES] = (
                        recv1[chunk, zl * 16 + p, :, z * LANES : (z + 1) * LANES]
                    )

        def columns(step, carry, chunk=chunk):
            x = (my_x + 1 + step // 2) % 4
            half = step % 2
            block = 2 * x + half
            dens[...] = jnp.dot(lhs[...], ytab[block], preferred_element_type=jnp.float32)
            tiles = [(r, c) for c in range(2) for r in range(2)]
            colour = {t: [jnp.zeros((8, LANES), jnp.float32) for _ in range(3)] for t in tiles}
            clear = {t: jnp.ones((8, LANES), jnp.float32) for t in tiles}
            for z in range(8):
                maps = [
                    jnp.broadcast_to(ctab[z // 2, z % 2, q : q + 1, :], (8, LANES)) for q in range(8)
                ]
                for r, c in tiles:
                    d = dens[z * FINE + 8 * r : z * FINE + 8 * r + 8, c * LANES : (c + 1) * LANES]
                    position = jnp.clip((d + SPREAD) * ((NCTRL - 1) / (2.0 * SPREAD)), 0.0, NCTRL - 1.0)
                    index = position.astype(jnp.int32)
                    frac = position - index.astype(jnp.float32)
                    value = [
                        jnp.take_along_axis(maps[q], index, axis=1, mode="promise_in_bounds")
                        + frac * jnp.take_along_axis(maps[q + 4], index, axis=1, mode="promise_in_bounds")
                        for q in range(4)
                    ]
                    weight = clear[r, c] * value[3]
                    colour[r, c] = [colour[r, c][q] + weight * value[q] for q in range(3)]
                    clear[r, c] = clear[r, c] - weight
            for c in range(2):
                for q in range(4):
                    both = jnp.concatenate(
                        [colour[r, c][q] if q < 3 else 1.0 - clear[r, c] for r in range(2)], axis=0
                    )
                    send2[chunk, x, half, q, :, c * LANES : (c + 1) * LANES] = both.astype(jnp.bfloat16)
            if comm:
                @pl.when(step < 6)
                def _():
                    pltpu.make_async_remote_copy(
                        src_ref=send2.at[chunk, x, half], dst_ref=recv2.at[chunk, my_x, half],
                        send_sem=send_sem.at[CHUNKS + chunk], recv_sem=recv2_sem.at[chunk],
                        device_id=same_plane(x, my_zl), device_id_type=MESH,
                    ).start()
            return carry

        lax.fori_loop(0, 8, columns, 0)
        recv2[chunk, my_x] = send2[chunk, my_x]
        if comm:
            pltpu.make_async_remote_copy(
                src_ref=recv2.at[chunk, pl.ds(0, 3)], dst_ref=recv2.at[chunk, pl.ds(0, 3)],
                send_sem=send_sem.at[CHUNKS + chunk], recv_sem=recv2_sem.at[chunk],
                device_id=same_plane((my_x + 1) % 4, my_zl), device_id_type=MESH,
            ).wait_recv()
        rows = pl.ds(pl.multiple_of(my_zl * 32 + chunk * FINE, FINE), FINE)
        for zl in range(4):
            half, cols = zl // 2, slice((zl % 2) * LANES, (zl % 2 + 1) * LANES)
            total = [recv2[chunk, 0, half, q, :, cols].astype(jnp.float32) for q in range(3)]
            clear = 1.0 - recv2[chunk, 0, half, 3, :, cols].astype(jnp.float32)
            for x in range(1, 4):
                for q in range(3):
                    total[q] = total[q] + clear * recv2[chunk, x, half, q, :, cols].astype(jnp.float32)
                clear = clear * (1.0 - recv2[chunk, x, half, 3, :, cols].astype(jnp.float32))
            for q in range(4):
                send3[chunk, zl, q] = total[q] if q < 3 else clear
            if comm:
                @pl.when(my_zl != zl)
                def _():
                    pltpu.make_async_remote_copy(
                        src_ref=send3.at[chunk, zl], dst_ref=out_ref.at[:, rows, :],
                        send_sem=send_sem.at[2 * CHUNKS + chunk], recv_sem=recv3_sem.at[chunk],
                        device_id=same_plane(my_x, zl), device_id_type=MESH,
                    ).start()
        out_ref[:, rows, :] = send3[chunk, my_zl]

    if comm:
        for chunk in range(CHUNKS):
            pltpu.make_async_remote_copy(
                src_ref=recv1.at[chunk, pl.ds(0, 63)], dst_ref=recv1.at[chunk, pl.ds(0, 63)],
                send_sem=send_sem.at[chunk], recv_sem=recv1_sem.at[chunk],
                device_id=same_x((my_z + 1) % 8, my_j), device_id_type=MESH,
            ).wait_send()
            pltpu.make_async_remote_copy(
                src_ref=recv2.at[chunk, pl.ds(0, 3)], dst_ref=recv2.at[chunk, pl.ds(0, 3)],
                send_sem=send_sem.at[CHUNKS + chunk], recv_sem=recv2_sem.at[chunk],
                device_id=same_plane((my_x + 1) % 4, my_zl), device_id_type=MESH,
            ).wait_send()
            last = pltpu.make_async_remote_copy(
                src_ref=send3.at[chunk, pl.ds(0, 3)], dst_ref=send3.at[chunk, pl.ds(0, 3)],
                send_sem=send_sem.at[2 * CHUNKS + chunk], recv_sem=recv3_sem.at[chunk],
                device_id=same_plane(my_x, (my_zl + 1) % 4), device_id_type=MESH,
            )
            last.wait_send()
            last.wait_recv()
        pltpu.make_async_remote_copy(
            src_ref=ctab.at[pl.ds(0, 3)], dst_ref=ctab.at[pl.ds(0, 3)], send_sem=send_sem.at[3 * CHUNKS],
            recv_sem=tab_sem, device_id=same_plane(my_x, (my_zl + 1) % 4), device_id_type=MESH,
        ).wait_send()


def render(spectrum, colour_table, map_index, comm=True):
    fine_pair, coarse_pair = base_tables()
    vmem = pl.BlockSpec(memory_space=pltpu.VMEM)
    bf16, f32 = jnp.bfloat16, jnp.float32
    return pl.pallas_call(
        functools.partial(kernel, comm=comm),
        out_shape=jax.ShapeDtypeStruct((4, 128, 128), f32),
        in_specs=[pl.BlockSpec(memory_space=pltpu.HBM)] * 5,
        out_specs=vmem,
        scratch_shapes=[
            pltpu.VMEM((2, 2, 64, NX), bf16),
            pltpu.VMEM((NMAPS, 4, NCTRL), f32),
            pltpu.SMEM((2,), jnp.int32),
            pltpu.VMEM((2, FINE, NX), f32),
            pltpu.VMEM((2, 128, LANES), f32),
            pltpu.VMEM((256, NX), bf16),
            pltpu.VMEM((128, NX), bf16),
            pltpu.VMEM((128, NX), bf16),
            pltpu.VMEM((CHUNKS, 8, 8, FINE, 256), bf16),
            pltpu.VMEM((CHUNKS, 64, FINE, 256), bf16),
            pltpu.VMEM((8, NY, 256), bf16),
            pltpu.VMEM((128, NY), bf16),
            pltpu.VMEM((4, 2, 8, LANES), f32),
            pltpu.VMEM((128, 256), f32),
            pltpu.VMEM((CHUNKS, 4, 2, 4, FINE, 2 * LANES), bf16),
            pltpu.VMEM((CHUNKS, 4, 2, 4, FINE, 2 * LANES), bf16),
            pltpu.VMEM((CHUNKS, 4, 4, FINE, LANES), f32),
            pltpu.SemaphoreType.DMA((5,)),
            pltpu.SemaphoreType.DMA((3 * CHUNKS + 1,)),
            pltpu.SemaphoreType.DMA((CHUNKS,)),
            pltpu.SemaphoreType.DMA((CHUNKS,)),
            pltpu.SemaphoreType.DMA((CHUNKS,)),
            pltpu.SemaphoreType.DMA,
        ],
        compiler_params=pltpu.CompilerParams(
            vmem_limit_bytes=60 << 20,
            **(dict(collective_id=0, has_side_effects=True) if comm else {}),
        ),
        name="render",
    )(spectrum, colour_table, map_index, jnp.asarray(fine_pair), jnp.asarray(coarse_pair))


def solution(mesh):
    return jax.shard_map(
        render,
        mesh=mesh,
        in_specs=(P("depth", None, "plane", None), P(), P("depth")),
        out_specs=P(None, "plane", "depth"),
        check_vma=False,
    )
```

```python
import functools
import math

import jax
import jax.numpy as jnp
import numpy as np
from jax import lax
from jax.experimental import pallas as pl
from jax.experimental.pallas import tpu as pltpu
from jax.sharding import PartitionSpec as P

NX = 2048
NY = 2048
NCTRL = 16
NMAPS = 4
SPREAD = 3.0
OPACITY = 0.06
LANES = 128
FINE = 16
CHUNKS = 2
MESH = pl.DeviceIdType.MESH


def base_tables():
    fine = 2.0 * np.pi * np.outer(np.arange(FINE), np.arange(NX)) / NX
    coarse = 2.0 * np.pi * (np.outer(np.arange(128), np.arange(128)) % 128) / 128.0
    fine_pair = np.stack([np.cos(fine), np.sin(fine)]).astype(np.float32)
    odd_even = 2.0 * np.pi * np.outer(np.arange(2 * FINE), np.arange(NY // 2)) / NY
    fine_y = np.stack([np.cos(odd_even), np.sin(odd_even)]).reshape(2, FINE, 2, NY // 2)
    fine_y = np.ascontiguousarray(fine_y.transpose(2, 0, 1, 3)).astype(np.float32)
    coarse_pair = np.stack([np.cos(coarse), np.sin(coarse)]).astype(np.float32)
    return fine_pair, fine_y, coarse_pair


def kernel(
    spec_hbm, colour_hbm, map_hbm, fine_hbm, fine_y_hbm, coarse_hbm, out_ref,
    spec_ref, colour_ref, map_ref, fine_ref, fine_y_ref, coarse_ref,
    turned_ref, swapped_ref, cos_ref, sin_ref, send1, recv1, ytab, lhs, ctab, dens, send2, recv2, send3,
    in_sem, send_sem, recv1_sem, recv2_sem, recv3_sem, tab_sem, *, comm
):
    if comm:
        depth_id = lax.axis_index("depth")
        plane_id = lax.axis_index("plane")
    else:
        depth_id = jnp.int32(5)
        plane_id = jnp.int32(6)
    my_x, my_zl = depth_id // 4, depth_id % 4
    my_zh, my_j = plane_id // 8, plane_id % 8
    my_z = my_zh * 4 + my_zl

    fetches = [
        pltpu.make_async_copy(src, dst, in_sem.at[i])
        for i, (src, dst) in enumerate(
            [(spec_hbm, spec_ref), (fine_hbm, fine_ref), (coarse_hbm, coarse_ref),
             (colour_hbm, colour_ref), (map_hbm, map_ref), (fine_y_hbm, fine_y_ref)]
        )
    ]
    for fetch in fetches:
        fetch.start()

    def same_x(z, j):
        return {"depth": my_x * 4 + z % 4, "plane": (z // 4) * 8 + j}

    def same_plane(x, zl):
        return {"depth": x * 4 + zl, "plane": plane_id}

    if comm:
        barrier = pltpu.get_barrier_semaphore()

        def greet_gather(i, carry):
            z, j = (my_z + i // 8) % 8, (my_j + i % 8) % 8
            pl.semaphore_signal(barrier, inc=1, device_id=same_x(z, j), device_id_type=MESH)
            return carry

        def greet_depth(i, carry):
            pl.semaphore_signal(
                barrier, inc=1, device_id=same_plane((my_x + i) % 4, my_zl), device_id_type=MESH
            )
            return carry

        lax.fori_loop(1, 64, greet_gather, 0)
        lax.fori_loop(1, 4, greet_depth, 0)

    for fetch in fetches[:5]:
        fetch.wait()

    source = lax.broadcasted_iota(jnp.int32, (256, 256), 0)
    column = lax.broadcasted_iota(jnp.int32, (256, 256), 1)
    part = (column // 32) % 2
    parity = (column // 64 + plane_id) % 2
    base = (column // 128) * 128 + (column % 32) * 2 + parity
    straight = jnp.where(source == base + 64 * part, 1.0, 0.0).astype(jnp.bfloat16)
    crossed = jnp.where(
        source == base + 64 * (1 - part), jnp.where(part == 0, -1.0, 1.0), 0.0
    ).astype(jnp.bfloat16)
    tn = (((0,), (0,)), ((), ()))
    spec = spec_ref[...].reshape(256, NX)
    turned_ref[...] = lax.dot_general(spec, straight, tn, preferred_element_type=jnp.float32).astype(jnp.bfloat16)
    swapped_ref[...] = lax.dot_general(spec, crossed, tn, preferred_element_type=jnp.float32).astype(jnp.bfloat16)

    for z in range(2):
        values = colour_ref[map_ref[z]]
        values = jnp.concatenate([values, jnp.zeros((4, LANES - NCTRL), jnp.float32)], axis=1)
        row = lax.broadcasted_iota(jnp.int32, (4, LANES), 0)
        values = jnp.where(row == 3, values * OPACITY, values)
        slopes = pltpu.roll(values, LANES - 1, 1) - values
        ctab[my_zl, z] = jnp.concatenate([values, slopes], axis=0)

    x_scale = 1.0 / math.sqrt(NX)
    y_scale = math.sqrt(2.0 / NY)

    def coarse_row(index, scale):
        bc = coarse_ref[0, pl.ds(index, 1), :] * scale
        bs = coarse_ref[1, pl.ds(index, 1), :] * scale
        return jnp.broadcast_to(bc, (FINE, LANES)), jnp.broadcast_to(bs, (FINE, LANES))

    def group_z(k):
        return (my_z + 4 + ((k + 1) // 2) * (1 - 2 * (k % 2))) % 8

    def transform_x(step):
        chunk, k = step // 8, step % 8
        z = group_z(k)
        first = (z // 4) * 64 + 2 * (z % 4) + chunk
        for j in range(8):
            bc, bs = coarse_row(first + 8 * j, x_scale)
            for b in range(NX // LANES):
                cols = slice(b * LANES, (b + 1) * LANES)
                ec, es = fine_ref[0, :, cols], fine_ref[1, :, cols]
                cos_ref[j * FINE : (j + 1) * FINE, cols] = (bc * ec - bs * es).astype(jnp.bfloat16)
                sin_ref[j * FINE : (j + 1) * FINE, cols] = (bs * ec + bc * es).astype(jnp.bfloat16)
        rows = jnp.dot(cos_ref[...], turned_ref[...], preferred_element_type=jnp.float32)
        rows += jnp.dot(sin_ref[...], swapped_ref[...], preferred_element_type=jnp.float32)
        rows = rows.astype(jnp.bfloat16).reshape(8, FINE, 256)
        send1[chunk, k] = rows

    def send_x(step):
        chunk, k = step // 8, step % 8
        z = group_z(k)
        if comm:
            def send(i, c):
                j = (my_j + i) % 8

                @pl.when(jnp.logical_or(k != 7, i != 0))
                def _():
                    pltpu.make_async_remote_copy(
                        src_ref=send1.at[chunk, k, j], dst_ref=recv1.at[chunk, my_zl * 16 + plane_id],
                        send_sem=send_sem.at[chunk], recv_sem=recv1_sem.at[chunk],
                        device_id=same_x(z, j), device_id_type=MESH,
                    ).start()

                return c

            lax.fori_loop(0, 8, send, 0)

    transform_x(0)
    if comm:
        pl.semaphore_wait(barrier, 66)
    send_x(0)
    if comm:
        for k in range(1, 4):
            pltpu.make_async_remote_copy(
                src_ref=ctab.at[my_zl], dst_ref=ctab.at[my_zl], send_sem=send_sem.at[3 * CHUNKS],
                recv_sem=tab_sem, device_id=same_plane(my_x, (my_zl + k) % 4), device_id_type=MESH,
            ).start()

    def x_step(step, carry):
        transform_x(step)
        send_x(step)
        return carry

    lax.fori_loop(1, 8 * CHUNKS, x_step, 0)
    for chunk in range(CHUNKS):
        recv1[chunk, my_zl * 16 + plane_id] = send1[chunk, 7, my_j]
    fetches[5].wait()

    def make_y(i, carry):
        parity, p, quarter = i // 32, (i % 32) // 2, i % 2
        bc, bs = coarse_row(4 * p + 2 * quarter, y_scale)
        base = (p // 2) * LANES + ((p + parity) % 2) * 64 + quarter * FINE
        base = pl.multiple_of(base, FINE)
        for b in range(NY // 2 // LANES):
            cols = slice(b * LANES, (b + 1) * LANES)
            ec, es = fine_y_ref[parity, 0, :, cols], fine_y_ref[parity, 1, :, cols]
            part = slice((b % 2) * LANES, (b % 2 + 1) * LANES)
            ytab[parity, b // 2, pl.ds(base, FINE), part] = (bc * ec - bs * es).astype(jnp.bfloat16)
            ytab[parity, b // 2, pl.ds(base + 32, FINE), part] = (-(bs * ec + bc * es)).astype(jnp.bfloat16)
        return carry

    lax.fori_loop(0, 64, make_y, 0)

    if comm:
        pltpu.make_async_remote_copy(
            src_ref=ctab.at[pl.ds(0, 3)], dst_ref=ctab.at[pl.ds(0, 3)], send_sem=send_sem.at[3 * CHUNKS],
            recv_sem=tab_sem, device_id=same_plane(my_x, (my_zl + 1) % 4), device_id_type=MESH,
        ).wait_recv()

    low = lax.broadcasted_iota(jnp.int32, (FINE, LANES), 1) < 64

    def transform_y(block, slot):
        even = jnp.dot(lhs[0], ytab[0, block], preferred_element_type=jnp.float32)
        odd = jnp.dot(lhs[1], ytab[1, block], preferred_element_type=jnp.float32)
        dens[slot, 0] = even + odd
        dens[slot, 1] = even - odd

    def shade(chunk, x, half, slot, side):
        tiles = [(r, c) for c in range(2) for r in range(2)]
        colour = {t: [jnp.zeros((8, LANES), jnp.float32) for _ in range(3)] for t in tiles}
        clear = {t: jnp.ones((8, LANES), jnp.float32) for t in tiles}
        for z in range(8):
            maps = [jnp.broadcast_to(ctab[z // 2, z % 2, q : q + 1, :], (8, LANES)) for q in range(8)]
            for r, c in tiles:
                d = dens[slot, side, z * FINE + 8 * r : z * FINE + 8 * r + 8, c * LANES : (c + 1) * LANES]
                position = jnp.clip((d + SPREAD) * ((NCTRL - 1) / (2.0 * SPREAD)), 0.0, NCTRL - 1.0)
                index = position.astype(jnp.int32)
                frac = position - index.astype(jnp.float32)
                value = [
                    jnp.take_along_axis(maps[q], index, axis=1, mode="promise_in_bounds")
                    + frac * jnp.take_along_axis(maps[q + 4], index, axis=1, mode="promise_in_bounds")
                    for q in range(4)
                ]
                weight = clear[r, c] * value[3]
                colour[r, c] = [colour[r, c][q] + weight * value[q] for q in range(3)]
                clear[r, c] = clear[r, c] - weight
        for c in range(2):
            for q in range(4):
                both = jnp.concatenate(
                    [colour[r, c][q] if q < 3 else 1.0 - clear[r, c] for r in range(2)], axis=0
                )
                send2[chunk, x, half, q, :, c * LANES : (c + 1) * LANES] = both.astype(jnp.bfloat16)

    def slab(chunk, carry):
        if comm:
            pltpu.make_async_remote_copy(
                src_ref=recv1.at[chunk, pl.ds(0, 63)], dst_ref=recv1.at[chunk, pl.ds(0, 63)],
                send_sem=send_sem.at[chunk], recv_sem=recv1_sem.at[chunk],
                device_id=same_x((my_z + 1) % 8, my_j), device_id_type=MESH,
            ).wait_recv()
        for zl in range(4):
            for z in range(2):
                for pair in range(8):
                    first = recv1[chunk, zl * 16 + 2 * pair, :, z * LANES : (z + 1) * LANES]
                    second = recv1[chunk, zl * 16 + 2 * pair + 1, :, z * LANES : (z + 1) * LANES]
                    rows = slice((2 * zl + z) * FINE, (2 * zl + z + 1) * FINE)
                    cols = slice(pair * LANES, (pair + 1) * LANES)
                    lhs[0, rows, cols] = jnp.where(low, first, second)
                    lhs[1, rows, cols] = jnp.where(low, second, first)

        pairs = [(my_x + 1) % 2, (my_x + 1) % 2, my_x % 2, my_x % 2]
        transform_y(2 * pairs[0], 0)
        for step in range(4):
            half = step % 2
            if step < 3:
                transform_y(2 * pairs[step + 1] + (step + 1) % 2, (step + 1) % 2)
            for side in range(2):
                shade(chunk, pairs[step] + 2 * side, half, step % 2, side)
            if comm:
                for side in range(2):
                    x = pairs[step] + 2 * side

                    @pl.when(x != my_x)
                    def _(x=x, half=half):
                        pltpu.make_async_remote_copy(
                            src_ref=send2.at[chunk, x, half], dst_ref=recv2.at[chunk, my_x, half],
                            send_sem=send_sem.at[CHUNKS + chunk], recv_sem=recv2_sem.at[chunk],
                            device_id=same_plane(x, my_zl), device_id_type=MESH,
                        ).start()

        recv2[chunk, my_x] = send2[chunk, my_x]
        if comm:
            pltpu.make_async_remote_copy(
                src_ref=recv2.at[chunk, pl.ds(0, 3)], dst_ref=recv2.at[chunk, pl.ds(0, 3)],
                send_sem=send_sem.at[CHUNKS + chunk], recv_sem=recv2_sem.at[chunk],
                device_id=same_plane((my_x + 1) % 4, my_zl), device_id_type=MESH,
            ).wait_recv()
        rows = pl.ds(pl.multiple_of(my_zl * 32 + chunk * FINE, FINE), FINE)
        for zl in range(4):
            half, cols = zl // 2, slice((zl % 2) * LANES, (zl % 2 + 1) * LANES)
            total = [recv2[chunk, 0, half, q, :, cols].astype(jnp.float32) for q in range(3)]
            clear = 1.0 - recv2[chunk, 0, half, 3, :, cols].astype(jnp.float32)
            for x in range(1, 4):
                for q in range(3):
                    total[q] = total[q] + clear * recv2[chunk, x, half, q, :, cols].astype(jnp.float32)
                clear = clear * (1.0 - recv2[chunk, x, half, 3, :, cols].astype(jnp.float32))
            for q in range(4):
                send3[chunk, zl, q] = total[q] if q < 3 else clear
            if comm:
                @pl.when(my_zl != zl)
                def _(zl=zl):
                    pltpu.make_async_remote_copy(
                        src_ref=send3.at[chunk, zl], dst_ref=out_ref.at[:, rows, :],
                        send_sem=send_sem.at[2 * CHUNKS + chunk], recv_sem=recv3_sem.at[chunk],
                        device_id=same_plane(my_x, zl), device_id_type=MESH,
                    ).start()
        out_ref[:, rows, :] = send3[chunk, my_zl]
        return carry

    lax.fori_loop(0, CHUNKS, slab, 0)

    if comm:
        for chunk in range(CHUNKS):
            pltpu.make_async_remote_copy(
                src_ref=recv1.at[chunk, pl.ds(0, 63)], dst_ref=recv1.at[chunk, pl.ds(0, 63)],
                send_sem=send_sem.at[chunk], recv_sem=recv1_sem.at[chunk],
                device_id=same_x((my_z + 1) % 8, my_j), device_id_type=MESH,
            ).wait_send()
            pltpu.make_async_remote_copy(
                src_ref=recv2.at[chunk, pl.ds(0, 3)], dst_ref=recv2.at[chunk, pl.ds(0, 3)],
                send_sem=send_sem.at[CHUNKS + chunk], recv_sem=recv2_sem.at[chunk],
                device_id=same_plane((my_x + 1) % 4, my_zl), device_id_type=MESH,
            ).wait_send()
            last = pltpu.make_async_remote_copy(
                src_ref=send3.at[chunk, pl.ds(0, 3)], dst_ref=send3.at[chunk, pl.ds(0, 3)],
                send_sem=send_sem.at[2 * CHUNKS + chunk], recv_sem=recv3_sem.at[chunk],
                device_id=same_plane(my_x, (my_zl + 1) % 4), device_id_type=MESH,
            )
            last.wait_send()
            last.wait_recv()
        pltpu.make_async_remote_copy(
            src_ref=ctab.at[pl.ds(0, 3)], dst_ref=ctab.at[pl.ds(0, 3)], send_sem=send_sem.at[3 * CHUNKS],
            recv_sem=tab_sem, device_id=same_plane(my_x, (my_zl + 1) % 4), device_id_type=MESH,
        ).wait_send()


def render(spectrum, colour_table, map_index, comm=True):
    fine_pair, fine_y, coarse_pair = base_tables()
    vmem = pl.BlockSpec(memory_space=pltpu.VMEM)
    bf16, f32 = jnp.bfloat16, jnp.float32
    return pl.pallas_call(
        functools.partial(kernel, comm=comm),
        out_shape=jax.ShapeDtypeStruct((4, 128, 128), f32),
        in_specs=[pl.BlockSpec(memory_space=pltpu.HBM)] * 6,
        out_specs=vmem,
        scratch_shapes=[
            pltpu.VMEM((2, 2, 64, NX), bf16),
            pltpu.VMEM((NMAPS, 4, NCTRL), f32),
            pltpu.SMEM((2,), jnp.int32),
            pltpu.VMEM((2, FINE, NX), f32),
            pltpu.VMEM((2, 2, FINE, NY // 2), f32),
            pltpu.VMEM((2, 128, LANES), f32),
            pltpu.VMEM((NX, 256), bf16),
            pltpu.VMEM((NX, 256), bf16),
            pltpu.VMEM((128, NX), bf16),
            pltpu.VMEM((128, NX), bf16),
            pltpu.VMEM((CHUNKS, 8, 8, FINE, 256), bf16),
            pltpu.VMEM((CHUNKS, 64, FINE, 256), bf16),
            pltpu.VMEM((2, 4, NY // 2, 256), bf16),
            pltpu.VMEM((2, 128, NY // 2), bf16),
            pltpu.VMEM((4, 2, 8, LANES), f32),
            pltpu.VMEM((2, 2, 128, 256), f32),
            pltpu.VMEM((CHUNKS, 4, 2, 4, FINE, 2 * LANES), bf16),
            pltpu.VMEM((CHUNKS, 4, 2, 4, FINE, 2 * LANES), bf16),
            pltpu.VMEM((CHUNKS, 4, 4, FINE, LANES), f32),
            pltpu.SemaphoreType.DMA((6,)),
            pltpu.SemaphoreType.DMA((3 * CHUNKS + 1,)),
            pltpu.SemaphoreType.DMA((CHUNKS,)),
            pltpu.SemaphoreType.DMA((CHUNKS,)),
            pltpu.SemaphoreType.DMA((CHUNKS,)),
            pltpu.SemaphoreType.DMA,
        ],
        compiler_params=pltpu.CompilerParams(
            vmem_limit_bytes=60 << 20,
            **(dict(collective_id=0, has_side_effects=True) if comm else {}),
        ),
        name="render",
    )(spectrum, colour_table, map_index, jnp.asarray(fine_pair), jnp.asarray(fine_y), jnp.asarray(coarse_pair))


def solution(mesh):
    return jax.shard_map(
        render,
        mesh=mesh,
        in_specs=(P("depth", None, "plane", None), P(), P("depth")),
        out_specs=P(None, "plane", "depth"),
        check_vma=False,
    )
```

```python
import functools
import math

import jax
import jax.numpy as jnp
import numpy as np
from jax import lax
from jax.experimental import pallas as pl
from jax.experimental.pallas import tpu as pltpu
from jax.sharding import PartitionSpec as P

NX = 2048
NY = 2048
NCTRL = 16
NMAPS = 4
SPREAD = 3.0
OPACITY = 0.06
LANES = 128
FINE = 16
CHUNKS = 2
MESH = pl.DeviceIdType.MESH


def base_tables():
    fine = 2.0 * np.pi * np.outer(np.arange(FINE), np.arange(NX)) / NX
    coarse = 2.0 * np.pi * (np.outer(np.arange(128), np.arange(128)) % 128) / 128.0
    fine_pair = np.stack([np.cos(fine), np.sin(fine)]).astype(np.float32)
    odd_even = 2.0 * np.pi * np.outer(np.arange(2 * FINE), np.arange(NY // 2)) / NY
    fine_y = np.stack([np.cos(odd_even), np.sin(odd_even)]).reshape(2, FINE, 2, NY // 2)
    fine_y = np.ascontiguousarray(fine_y.transpose(2, 0, 1, 3)).astype(np.float32)
    coarse_pair = np.stack([np.cos(coarse), np.sin(coarse)]).astype(np.float32)
    return fine_pair, fine_y, coarse_pair


def kernel(
    spec_hbm, colour_hbm, map_hbm, fine_hbm, fine_y_hbm, coarse_hbm, out_ref,
    spec_ref, colour_ref, map_ref, fine_ref, fine_y_ref, coarse_ref,
    turned_ref, swapped_ref, cos_ref, sin_ref, send1, recv1, ytab, lhs, ctab, dens, send2, recv2, send3,
    in_sem, send_sem, recv1_sem, recv2_sem, recv3_sem, tab_sem, *, comm
):
    if comm:
        depth_id = lax.axis_index("depth")
        plane_id = lax.axis_index("plane")
    else:
        depth_id = jnp.int32(5)
        plane_id = jnp.int32(6)
    my_x, my_zl = depth_id // 4, depth_id % 4
    my_zh, my_j = plane_id // 8, plane_id % 8
    my_z = my_zh * 4 + my_zl

    fetches = [
        pltpu.make_async_copy(src, dst, in_sem.at[i])
        for i, (src, dst) in enumerate(
            [(spec_hbm, spec_ref), (fine_hbm, fine_ref), (coarse_hbm, coarse_ref),
             (colour_hbm, colour_ref), (map_hbm, map_ref), (fine_y_hbm, fine_y_ref)]
        )
    ]
    for fetch in fetches:
        fetch.start()

    def same_x(z, j):
        return {"depth": my_x * 4 + z % 4, "plane": (z // 4) * 8 + j}

    def same_plane(x, zl):
        return {"depth": x * 4 + zl, "plane": plane_id}

    if comm:
        barrier = pltpu.get_barrier_semaphore()

        def greet_gather(i, carry):
            z, j = (my_z + i // 8) % 8, (my_j + i % 8) % 8
            pl.semaphore_signal(barrier, inc=1, device_id=same_x(z, j), device_id_type=MESH)
            return carry

        def greet_depth(i, carry):
            pl.semaphore_signal(
                barrier, inc=1, device_id=same_plane((my_x + i) % 4, my_zl), device_id_type=MESH
            )
            return carry

        lax.fori_loop(1, 64, greet_gather, 0)
        lax.fori_loop(1, 4, greet_depth, 0)

    for fetch in fetches[:5]:
        fetch.wait()

    source = lax.broadcasted_iota(jnp.int32, (256, 256), 0)
    column = lax.broadcasted_iota(jnp.int32, (256, 256), 1)
    part = (column // 32) % 2
    parity = (column // 64 + plane_id) % 2
    base = (column // 128) * 128 + (column % 32) * 2 + parity
    straight = jnp.where(source == base + 64 * part, 1.0, 0.0).astype(jnp.bfloat16)
    crossed = jnp.where(
        source == base + 64 * (1 - part), jnp.where(part == 0, -1.0, 1.0), 0.0
    ).astype(jnp.bfloat16)
    tn = (((0,), (0,)), ((), ()))
    spec = spec_ref[...].reshape(256, NX)
    turned_ref[...] = lax.dot_general(spec, straight, tn, preferred_element_type=jnp.float32).astype(jnp.bfloat16)
    swapped_ref[...] = lax.dot_general(spec, crossed, tn, preferred_element_type=jnp.float32).astype(jnp.bfloat16)

    for z in range(2):
        values = colour_ref[map_ref[z]]
        values = jnp.concatenate([values, jnp.zeros((4, LANES - NCTRL), jnp.float32)], axis=1)
        row = lax.broadcasted_iota(jnp.int32, (4, LANES), 0)
        values = jnp.where(row == 3, values * OPACITY, values)
        slopes = pltpu.roll(values, LANES - 1, 1) - values
        ctab[my_zl, z] = jnp.concatenate([values, slopes], axis=0)

    x_scale = 1.0 / math.sqrt(NX)
    y_scale = math.sqrt(2.0 / NY)

    def coarse_row(index, scale):
        bc = coarse_ref[0, pl.ds(index, 1), :] * scale
        bs = coarse_ref[1, pl.ds(index, 1), :] * scale
        return jnp.broadcast_to(bc, (FINE, LANES)), jnp.broadcast_to(bs, (FINE, LANES))

    def pair_z(k):
        return (my_z + 4 - k) % 8, (my_z + 4 + k + 4 * ((4 - k) // 4)) % 8

    def transform_x(step):
        chunk, k = step // 4, step % 4
        for i, z in enumerate(pair_z(k)):
            first = (z // 4) * 64 + 2 * (z % 4) + chunk
            for j in range(8):
                bc, bs = coarse_row(first + 8 * j, x_scale)
                rows = slice((8 * i + j) * FINE, (8 * i + j + 1) * FINE)
                for b in range(NX // LANES):
                    cols = slice(b * LANES, (b + 1) * LANES)
                    ec, es = fine_ref[0, :, cols], fine_ref[1, :, cols]
                    cos_ref[rows, cols] = (bc * ec - bs * es).astype(jnp.bfloat16)
                    sin_ref[rows, cols] = (bs * ec + bc * es).astype(jnp.bfloat16)
        rows = jnp.dot(cos_ref[...], turned_ref[...], preferred_element_type=jnp.float32)
        rows += jnp.dot(sin_ref[...], swapped_ref[...], preferred_element_type=jnp.float32)
        rows = rows.astype(jnp.bfloat16).reshape(2, 8, FINE, 256)
        send1[chunk, k] = rows

    def send_x(step):
        chunk, k = step // 4, step % 4
        zs = pair_z(k)
        if comm:
            def send(i, c):
                j = (my_j + i) % 8
                for side, z in enumerate(zs):
                    copy = pltpu.make_async_remote_copy(
                        src_ref=send1.at[chunk, k, side, j], dst_ref=recv1.at[chunk, my_zl * 16 + plane_id],
                        send_sem=send_sem.at[chunk], recv_sem=recv1_sem.at[chunk],
                        device_id=same_x(z, j), device_id_type=MESH,
                    )
                    if side == 0:
                        copy.start()
                    else:
                        pl.when(jnp.logical_or(k != 0, i != 0))(copy.start)
                return c

            lax.fori_loop(0, 8, send, 0)

    transform_x(0)
    if comm:
        pl.semaphore_wait(barrier, 66)
    send_x(0)
    if comm:
        for k in range(1, 4):
            pltpu.make_async_remote_copy(
                src_ref=ctab.at[my_zl], dst_ref=ctab.at[my_zl], send_sem=send_sem.at[3 * CHUNKS],
                recv_sem=tab_sem, device_id=same_plane(my_x, (my_zl + k) % 4), device_id_type=MESH,
            ).start()

    def x_step(step, carry):
        transform_x(step)
        send_x(step)
        return carry

    lax.fori_loop(1, 4 * CHUNKS, x_step, 0)
    for chunk in range(CHUNKS):
        recv1[chunk, my_zl * 16 + plane_id] = send1[chunk, 0, 1, my_j]
    fetches[5].wait()

    def make_y(i, carry):
        parity, p, quarter = i // 32, (i % 32) // 2, i % 2
        bc, bs = coarse_row(4 * p + 2 * quarter, y_scale)
        base = (p // 2) * LANES + ((p + parity) % 2) * 64 + quarter * FINE
        base = pl.multiple_of(base, FINE)
        for b in range(NY // 2 // LANES):
            cols = slice(b * LANES, (b + 1) * LANES)
            ec, es = fine_y_ref[parity, 0, :, cols], fine_y_ref[parity, 1, :, cols]
            part = slice((b % 2) * LANES, (b % 2 + 1) * LANES)
            ytab[parity, b // 2, pl.ds(base, FINE), part] = (bc * ec - bs * es).astype(jnp.bfloat16)
            ytab[parity, b // 2, pl.ds(base + 32, FINE), part] = (-(bs * ec + bc * es)).astype(jnp.bfloat16)
        return carry

    lax.fori_loop(0, 64, make_y, 0)

    if comm:
        pltpu.make_async_remote_copy(
            src_ref=ctab.at[pl.ds(0, 3)], dst_ref=ctab.at[pl.ds(0, 3)], send_sem=send_sem.at[3 * CHUNKS],
            recv_sem=tab_sem, device_id=same_plane(my_x, (my_zl + 1) % 4), device_id_type=MESH,
        ).wait_recv()

    low = lax.broadcasted_iota(jnp.int32, (FINE, LANES), 1) < 64

    def transform_y(block, slot, piece):
        parity, depth = piece // 4, slice((piece % 4) * 256, (piece % 4 + 1) * 256)
        part = jnp.dot(lhs[parity, :, depth], ytab[parity, block, depth, :], preferred_element_type=jnp.float32)
        dens[slot, parity] = part if piece % 4 == 0 else dens[slot, parity] + part

    def shade(chunk, x, half, slot, side, following):
        tiles = [(r, c) for c in range(2) for r in range(2)]
        colour = {t: [jnp.zeros((8, LANES), jnp.float32) for _ in range(3)] for t in tiles}
        clear = {t: jnp.ones((8, LANES), jnp.float32) for t in tiles}
        for z in range(8):
            if following is not None and z % 2 == 0:
                transform_y(*following, 4 * side + z // 2)
            maps = [jnp.broadcast_to(ctab[z // 2, z % 2, q : q + 1, :], (8, LANES)) for q in range(8)]
            for r, c in tiles:
                at = (slice(z * FINE + 8 * r, z * FINE + 8 * r + 8), slice(c * LANES, (c + 1) * LANES))
                even, odd = dens[(slot, 0, *at)], dens[(slot, 1, *at)]
                d = even - odd if side else even + odd
                position = jnp.clip((d + SPREAD) * ((NCTRL - 1) / (2.0 * SPREAD)), 0.0, NCTRL - 1.0)
                index = position.astype(jnp.int32)
                frac = position - index.astype(jnp.float32)
                value = [
                    jnp.take_along_axis(maps[q], index, axis=1, mode="promise_in_bounds")
                    + frac * jnp.take_along_axis(maps[q + 4], index, axis=1, mode="promise_in_bounds")
                    for q in range(4)
                ]
                weight = clear[r, c] * value[3]
                colour[r, c] = [colour[r, c][q] + weight * value[q] for q in range(3)]
                clear[r, c] = clear[r, c] - weight
        for c in range(2):
            for q in range(4):
                both = jnp.concatenate(
                    [colour[r, c][q] if q < 3 else 1.0 - clear[r, c] for r in range(2)], axis=0
                )
                send2[chunk, x, half, q, :, c * LANES : (c + 1) * LANES] = both.astype(jnp.bfloat16)

    def slab(chunk, carry):
        if comm:
            pltpu.make_async_remote_copy(
                src_ref=recv1.at[chunk, pl.ds(0, 63)], dst_ref=recv1.at[chunk, pl.ds(0, 63)],
                send_sem=send_sem.at[chunk], recv_sem=recv1_sem.at[chunk],
                device_id=same_x((my_z + 1) % 8, my_j), device_id_type=MESH,
            ).wait_recv()
        for zl in range(4):
            for z in range(2):
                for pair in range(8):
                    first = recv1[chunk, zl * 16 + 2 * pair, :, z * LANES : (z + 1) * LANES]
                    second = recv1[chunk, zl * 16 + 2 * pair + 1, :, z * LANES : (z + 1) * LANES]
                    rows = slice((2 * zl + z) * FINE, (2 * zl + z + 1) * FINE)
                    cols = slice(pair * LANES, (pair + 1) * LANES)
                    lhs[0, rows, cols] = jnp.where(low, first, second)
                    lhs[1, rows, cols] = jnp.where(low, second, first)

        pairs = [(my_x + 1) % 2, (my_x + 1) % 2, my_x % 2, my_x % 2]
        for piece in range(8):
            transform_y(2 * pairs[0], 0, piece)
        for step in range(4):
            half = step % 2
            following = (2 * pairs[step + 1] + (step + 1) % 2, (step + 1) % 2) if step < 3 else None
            for side in range(2):
                shade(chunk, pairs[step] + 2 * side, half, step % 2, side, following)
            if comm:
                for side in range(2):
                    x = pairs[step] + 2 * side

                    @pl.when(x != my_x)
                    def _(x=x, half=half):
                        pltpu.make_async_remote_copy(
                            src_ref=send2.at[chunk, x, half], dst_ref=recv2.at[chunk, my_x, half],
                            send_sem=send_sem.at[CHUNKS + chunk], recv_sem=recv2_sem.at[chunk],
                            device_id=same_plane(x, my_zl), device_id_type=MESH,
                        ).start()

        recv2[chunk, my_x] = send2[chunk, my_x]
        if comm:
            pltpu.make_async_remote_copy(
                src_ref=recv2.at[chunk, pl.ds(0, 3)], dst_ref=recv2.at[chunk, pl.ds(0, 3)],
                send_sem=send_sem.at[CHUNKS + chunk], recv_sem=recv2_sem.at[chunk],
                device_id=same_plane((my_x + 1) % 4, my_zl), device_id_type=MESH,
            ).wait_recv()
        rows = pl.ds(pl.multiple_of(my_zl * 32 + chunk * FINE, FINE), FINE)
        for zl in range(4):
            half, cols = zl // 2, slice((zl % 2) * LANES, (zl % 2 + 1) * LANES)
            total = [recv2[chunk, 0, half, q, :, cols].astype(jnp.float32) for q in range(3)]
            clear = 1.0 - recv2[chunk, 0, half, 3, :, cols].astype(jnp.float32)
            for x in range(1, 4):
                for q in range(3):
                    total[q] = total[q] + clear * recv2[chunk, x, half, q, :, cols].astype(jnp.float32)
                clear = clear * (1.0 - recv2[chunk, x, half, 3, :, cols].astype(jnp.float32))
            for q in range(4):
                send3[chunk, zl, q] = total[q] if q < 3 else clear
            if comm:
                @pl.when(my_zl != zl)
                def _(zl=zl):
                    pltpu.make_async_remote_copy(
                        src_ref=send3.at[chunk, zl], dst_ref=out_ref.at[:, rows, :],
                        send_sem=send_sem.at[2 * CHUNKS + chunk], recv_sem=recv3_sem.at[chunk],
                        device_id=same_plane(my_x, zl), device_id_type=MESH,
                    ).start()
        out_ref[:, rows, :] = send3[chunk, my_zl]
        return carry

    lax.fori_loop(0, CHUNKS, slab, 0)

    if comm:
        for chunk in range(CHUNKS):
            pltpu.make_async_remote_copy(
                src_ref=recv1.at[chunk, pl.ds(0, 63)], dst_ref=recv1.at[chunk, pl.ds(0, 63)],
                send_sem=send_sem.at[chunk], recv_sem=recv1_sem.at[chunk],
                device_id=same_x((my_z + 1) % 8, my_j), device_id_type=MESH,
            ).wait_send()
            pltpu.make_async_remote_copy(
                src_ref=recv2.at[chunk, pl.ds(0, 3)], dst_ref=recv2.at[chunk, pl.ds(0, 3)],
                send_sem=send_sem.at[CHUNKS + chunk], recv_sem=recv2_sem.at[chunk],
                device_id=same_plane((my_x + 1) % 4, my_zl), device_id_type=MESH,
            ).wait_send()
            last = pltpu.make_async_remote_copy(
                src_ref=send3.at[chunk, pl.ds(0, 3)], dst_ref=send3.at[chunk, pl.ds(0, 3)],
                send_sem=send_sem.at[2 * CHUNKS + chunk], recv_sem=recv3_sem.at[chunk],
                device_id=same_plane(my_x, (my_zl + 1) % 4), device_id_type=MESH,
            )
            last.wait_send()
            last.wait_recv()
        pltpu.make_async_remote_copy(
            src_ref=ctab.at[pl.ds(0, 3)], dst_ref=ctab.at[pl.ds(0, 3)], send_sem=send_sem.at[3 * CHUNKS],
            recv_sem=tab_sem, device_id=same_plane(my_x, (my_zl + 1) % 4), device_id_type=MESH,
        ).wait_send()


def render(spectrum, colour_table, map_index, comm=True):
    fine_pair, fine_y, coarse_pair = base_tables()
    vmem = pl.BlockSpec(memory_space=pltpu.VMEM)
    bf16, f32 = jnp.bfloat16, jnp.float32
    return pl.pallas_call(
        functools.partial(kernel, comm=comm),
        out_shape=jax.ShapeDtypeStruct((4, 128, 128), f32),
        in_specs=[pl.BlockSpec(memory_space=pltpu.HBM)] * 6,
        out_specs=vmem,
        scratch_shapes=[
            pltpu.VMEM((2, 2, 64, NX), bf16),
            pltpu.VMEM((NMAPS, 4, NCTRL), f32),
            pltpu.SMEM((2,), jnp.int32),
            pltpu.VMEM((2, FINE, NX), f32),
            pltpu.VMEM((2, 2, FINE, NY // 2), f32),
            pltpu.VMEM((2, 128, LANES), f32),
            pltpu.VMEM((NX, 256), bf16),
            pltpu.VMEM((NX, 256), bf16),
            pltpu.VMEM((256, NX), bf16),
            pltpu.VMEM((256, NX), bf16),
            pltpu.VMEM((CHUNKS, 4, 2, 8, FINE, 256), bf16),
            pltpu.VMEM((CHUNKS, 64, FINE, 256), bf16),
            pltpu.VMEM((2, 4, NY // 2, 256), bf16),
            pltpu.VMEM((2, 128, NY // 2), bf16),
            pltpu.VMEM((4, 2, 8, LANES), f32),
            pltpu.VMEM((2, 2, 128, 256), f32),
            pltpu.VMEM((CHUNKS, 4, 2, 4, FINE, 2 * LANES), bf16),
            pltpu.VMEM((CHUNKS, 4, 2, 4, FINE, 2 * LANES), bf16),
            pltpu.VMEM((CHUNKS, 4, 4, FINE, LANES), f32),
            pltpu.SemaphoreType.DMA((6,)),
            pltpu.SemaphoreType.DMA((3 * CHUNKS + 1,)),
            pltpu.SemaphoreType.DMA((CHUNKS,)),
            pltpu.SemaphoreType.DMA((CHUNKS,)),
            pltpu.SemaphoreType.DMA((CHUNKS,)),
            pltpu.SemaphoreType.DMA,
        ],
        compiler_params=pltpu.CompilerParams(
            vmem_limit_bytes=60 << 20,
            **(dict(collective_id=0, has_side_effects=True) if comm else {}),
        ),
        name="render",
    )(spectrum, colour_table, map_index, jnp.asarray(fine_pair), jnp.asarray(fine_y), jnp.asarray(coarse_pair))


def solution(mesh):
    return jax.shard_map(
        render,
        mesh=mesh,
        in_specs=(P("depth", None, "plane", None), P(), P("depth")),
        out_specs=P(None, "plane", "depth"),
        check_vma=False,
    )
```

```python
import functools
import math

import jax
import jax.numpy as jnp
import numpy as np
from jax import lax
from jax.experimental import pallas as pl
from jax.experimental.pallas import tpu as pltpu
from jax.sharding import PartitionSpec as P

NX = 2048
NY = 2048
NCTRL = 16
NMAPS = 4
SPREAD = 3.0
OPACITY = 0.06
LANES = 128
FINE = 16
OCTETS = 4
OCT = 8
MESH = pl.DeviceIdType.MESH


def base_tables():
    fine = 2.0 * np.pi * np.outer(np.arange(FINE), np.arange(NX)) / NX
    coarse = 2.0 * np.pi * (np.outer(np.arange(128), np.arange(128)) % 128) / 128.0
    fine_pair = np.stack([np.cos(fine), np.sin(fine)]).astype(np.float32)
    odd_even = 2.0 * np.pi * np.outer(np.arange(2 * FINE), np.arange(NY // 2)) / NY
    fine_y = np.stack([np.cos(odd_even), np.sin(odd_even)]).reshape(2, FINE, 2, NY // 2)
    fine_y = np.ascontiguousarray(fine_y.transpose(2, 0, 1, 3)).astype(np.float32)
    coarse_pair = np.stack([np.cos(coarse), np.sin(coarse)]).astype(np.float32)
    return fine_pair, fine_y, coarse_pair


def kernel(
    spec_hbm, colour_hbm, map_hbm, fine_hbm, fine_y_hbm, coarse_hbm, out_ref,
    spec_ref, colour_ref, map_ref, fine_ref, fine_y_ref, coarse_ref,
    turned_ref, swapped_ref, cos_ref, sin_ref, send1, recv1, ytab, lhs, ctab, dens, send2, recv2, send3,
    in_sem, send_sem, recv1_sem, recv2_sem, recv3_sem, tab_sem, *, comm
):
    if comm:
        depth_id = lax.axis_index("depth")
        plane_id = lax.axis_index("plane")
    else:
        depth_id = jnp.int32(5)
        plane_id = jnp.int32(6)
    my_x, my_zl = depth_id // 4, depth_id % 4
    my_zh, my_j = plane_id // 8, plane_id % 8
    my_z = my_zh * 4 + my_zl

    fetches = [
        pltpu.make_async_copy(src, dst, in_sem.at[i])
        for i, (src, dst) in enumerate(
            [(spec_hbm, spec_ref), (fine_hbm, fine_ref), (coarse_hbm, coarse_ref),
             (colour_hbm, colour_ref), (map_hbm, map_ref), (fine_y_hbm, fine_y_ref)]
        )
    ]
    for fetch in fetches:
        fetch.start()

    def same_x(z, j):
        return {"depth": my_x * 4 + z % 4, "plane": (z // 4) * 8 + j}

    def same_plane(x, zl):
        return {"depth": x * 4 + zl, "plane": plane_id}

    if comm:
        barrier = pltpu.get_barrier_semaphore()

        def greet_gather(i, carry):
            z, j = (my_z + i // 8) % 8, (my_j + i % 8) % 8
            pl.semaphore_signal(barrier, inc=1, device_id=same_x(z, j), device_id_type=MESH)
            return carry

        def greet_depth(i, carry):
            pl.semaphore_signal(
                barrier, inc=1, device_id=same_plane((my_x + i) % 4, my_zl), device_id_type=MESH
            )
            return carry

        lax.fori_loop(1, 64, greet_gather, 0)
        lax.fori_loop(1, 4, greet_depth, 0)

    x_scale = 1.0 / math.sqrt(NX)
    y_scale = math.sqrt(2.0 / NY)

    def coarse_row(index, scale):
        bc = coarse_ref[0, pl.ds(index, 1), :] * scale
        bs = coarse_ref[1, pl.ds(index, 1), :] * scale
        return jnp.broadcast_to(bc, (FINE, LANES)), jnp.broadcast_to(bs, (FINE, LANES))

    def pair_z(k):
        return (my_z + 4 - k) % 8, (my_z + 4 + k + 4 * ((4 - k) // 4)) % 8

    def x_tables(chunk, k):
        for i, z in enumerate(pair_z(k)):
            first = (z // 4) * 64 + 2 * (z % 4) + chunk
            for j in range(8):
                bc, bs = coarse_row(first + 8 * j, x_scale)
                rows = slice((8 * i + j) * FINE, (8 * i + j + 1) * FINE)
                for b in range(NX // LANES):
                    cols = slice(b * LANES, (b + 1) * LANES)
                    ec, es = fine_ref[0, :, cols], fine_ref[1, :, cols]
                    cos_ref[rows, cols] = (bc * ec - bs * es).astype(jnp.bfloat16)
                    sin_ref[rows, cols] = (bs * ec + bc * es).astype(jnp.bfloat16)

    def x_rows(chunk, k):
        rows = jnp.dot(cos_ref[...], turned_ref[...], preferred_element_type=jnp.float32)
        rows += jnp.dot(sin_ref[...], swapped_ref[...], preferred_element_type=jnp.float32)
        send1[chunk, k] = rows.reshape(2, 8, 2, OCT, 256).astype(jnp.bfloat16)

    def send_x(k, part):
        zs = pair_z(k)
        if not comm:
            return

        def send(i, c):
            j = (my_j + i) % 8
            for side, z in enumerate(zs):
                if part == 0:
                    src, dst = send1.at[0, k, side, j], recv1.at[0, my_zl * 16 + plane_id]
                else:
                    src = send1.at[1, k, side, j, part - 1]
                    dst = recv1.at[1, my_zl * 16 + plane_id, part - 1]
                copy = pltpu.make_async_remote_copy(
                    src_ref=src, dst_ref=dst, send_sem=send_sem.at[0], recv_sem=recv1_sem.at[part],
                    device_id=same_x(z, j), device_id_type=MESH,
                )
                if side == 0:
                    copy.start()
                else:
                    pl.when(jnp.logical_or(k != 0, i != 0))(copy.start)
            return c

        lax.fori_loop(0, 8, send, 0)

    fetches[1].wait()
    fetches[2].wait()
    x_tables(0, 0)
    fetches[0].wait()

    source = lax.broadcasted_iota(jnp.int32, (256, 256), 0)
    column = lax.broadcasted_iota(jnp.int32, (256, 256), 1)
    part = (column // 32) % 2
    parity = (column // 64 + plane_id) % 2
    base = (column // 128) * 128 + (column % 32) * 2 + parity
    straight = jnp.where(source == base + 64 * part, 1.0, 0.0).astype(jnp.bfloat16)
    crossed = jnp.where(
        source == base + 64 * (1 - part), jnp.where(part == 0, -1.0, 1.0), 0.0
    ).astype(jnp.bfloat16)
    tn = (((0,), (0,)), ((), ()))
    spec = spec_ref[...].reshape(256, NX)
    turned_ref[...] = lax.dot_general(spec, straight, tn, preferred_element_type=jnp.float32).astype(jnp.bfloat16)
    swapped_ref[...] = lax.dot_general(spec, crossed, tn, preferred_element_type=jnp.float32).astype(jnp.bfloat16)

    x_rows(0, 0)
    fetches[3].wait()
    fetches[4].wait()

    for z in range(2):
        values = colour_ref[map_ref[z]]
        values = jnp.concatenate([values, jnp.zeros((4, LANES - NCTRL), jnp.float32)], axis=1)
        row = lax.broadcasted_iota(jnp.int32, (4, LANES), 0)
        values = jnp.where(row == 3, values * OPACITY, values)
        slopes = pltpu.roll(values, LANES - 1, 1) - values
        ctab[my_zl, z] = jnp.concatenate([values, slopes], axis=0)

    if comm:
        pl.semaphore_wait(barrier, 66)
    send_x(0, 0)
    if comm:
        for k in range(1, 4):
            pltpu.make_async_remote_copy(
                src_ref=ctab.at[my_zl], dst_ref=ctab.at[my_zl], send_sem=send_sem.at[3],
                recv_sem=tab_sem, device_id=same_plane(my_x, (my_zl + k) % 4), device_id_type=MESH,
            ).start()

    def first_half(k, carry):
        x_tables(0, k)
        x_rows(0, k)
        send_x(k, 0)
        return carry

    def second_half(k, carry):
        x_tables(1, k)
        x_rows(1, k)
        send_x(k, 1)
        return carry

    def last_part(k, carry):
        send_x(k, 2)
        return carry

    lax.fori_loop(1, 4, first_half, 0)
    lax.fori_loop(0, 4, second_half, 0)
    lax.fori_loop(0, 4, last_part, 0)
    for chunk in range(2):
        recv1[chunk, my_zl * 16 + plane_id] = send1[chunk, 0, 1, my_j]
    fetches[5].wait()

    def make_y(i, carry):
        parity, p, quarter = i // 32, (i % 32) // 2, i % 2
        bc, bs = coarse_row(4 * p + 2 * quarter, y_scale)
        base = (p // 2) * LANES + ((p + parity) % 2) * 64 + quarter * FINE
        base = pl.multiple_of(base, FINE)
        for b in range(NY // 2 // LANES):
            cols = slice(b * LANES, (b + 1) * LANES)
            ec, es = fine_y_ref[parity, 0, :, cols], fine_y_ref[parity, 1, :, cols]
            part = slice((b % 2) * LANES, (b % 2 + 1) * LANES)
            ytab[parity, b // 2, pl.ds(base, FINE), part] = (bc * ec - bs * es).astype(jnp.bfloat16)
            ytab[parity, b // 2, pl.ds(base + 32, FINE), part] = (-(bs * ec + bc * es)).astype(jnp.bfloat16)
        return carry

    lax.fori_loop(0, 64, make_y, 0)

    def table_copy():
        return pltpu.make_async_remote_copy(
            src_ref=ctab.at[pl.ds(0, 3)], dst_ref=ctab.at[pl.ds(0, 3)], send_sem=send_sem.at[3],
            recv_sem=tab_sem, device_id=same_plane(my_x, (my_zl + 1) % 4), device_id_type=MESH,
        )

    def waiting(ref, send_slot, recv, device):
        return pltpu.make_async_remote_copy(
            src_ref=ref, dst_ref=ref, send_sem=send_sem.at[send_slot], recv_sem=recv,
            device_id=device, device_id_type=MESH,
        )

    next_z = same_x((my_z + 1) % 8, my_j)
    next_x = same_plane((my_x + 1) % 4, my_zl)
    next_zl = same_plane(my_x, (my_zl + 1) % 4)
    if comm:
        table_copy().wait_recv()

    low = lax.broadcasted_iota(jnp.int32, (OCT, LANES), 1) < 64

    def transform_y(block, slot, piece):
        parity, depth = piece // 4, slice((piece % 4) * 256, (piece % 4 + 1) * 256)
        part = jnp.dot(lhs[parity, :, depth], ytab[parity, block, depth, :], preferred_element_type=jnp.float32)
        dens[slot, parity] = part if piece % 4 == 0 else dens[slot, parity] + part

    def shade(octet, xs, half, slot, following):
        tiles = [(i, c) for i in range(len(xs)) for c in range(2)]
        signs = [(1 - 2 * (x // 2)).astype(jnp.float32) for x in xs]
        colour = {t: [jnp.zeros((OCT, LANES), jnp.float32) for _ in range(3)] for t in tiles}
        clear = {t: jnp.ones((OCT, LANES), jnp.float32) for t in tiles}
        for z in range(8):
            if following is not None:
                transform_y(*following, z)
            maps = [jnp.broadcast_to(ctab[z // 2, z % 2, q : q + 1, :], (OCT, LANES)) for q in range(8)]
            for t in tiles:
                i, c = t
                at = (slice(z * OCT, (z + 1) * OCT), slice(c * LANES, (c + 1) * LANES))
                d = dens[(slot, 0, *at)] + signs[i] * dens[(slot, 1, *at)]
                position = jnp.clip((d + SPREAD) * ((NCTRL - 1) / (2.0 * SPREAD)), 0.0, NCTRL - 1.0)
                index = position.astype(jnp.int32)
                frac = position - index.astype(jnp.float32)
                value = [
                    jnp.take_along_axis(maps[q], index, axis=1, mode="promise_in_bounds")
                    + frac * jnp.take_along_axis(maps[q + 4], index, axis=1, mode="promise_in_bounds")
                    for q in range(4)
                ]
                weight = clear[t] * value[3]
                colour[t] = [colour[t][q] + weight * value[q] for q in range(3)]
                clear[t] = clear[t] - weight
        for i, c in tiles:
            for q in range(4):
                result = colour[i, c][q] if q < 3 else 1.0 - clear[i, c]
                send2[octet, xs[i], half, q, :, c * LANES : (c + 1) * LANES] = result.astype(jnp.bfloat16)

    def send_x_part(octet, x, half):
        if comm:
            pltpu.make_async_remote_copy(
                src_ref=send2.at[octet, x, half], dst_ref=recv2.at[octet, my_x, half],
                send_sem=send_sem.at[1], recv_sem=recv2_sem.at[octet],
                device_id=same_plane(x, my_zl), device_id_type=MESH,
            ).start()

    def combine(octet):
        if comm:
            waiting(recv2.at[octet, pl.ds(0, 3)], 1, recv2_sem.at[octet], next_x).wait_recv()
        rows = pl.ds(pl.multiple_of(my_zl * 32 + octet * OCT, OCT), OCT)
        for zl in range(4):
            half, cols = zl // 2, slice((zl % 2) * LANES, (zl % 2 + 1) * LANES)
            total = [recv2[octet, 0, half, q, :, cols].astype(jnp.float32) for q in range(3)]
            clear = 1.0 - recv2[octet, 0, half, 3, :, cols].astype(jnp.float32)
            for x in range(1, 4):
                for q in range(3):
                    total[q] = total[q] + clear * recv2[octet, x, half, q, :, cols].astype(jnp.float32)
                clear = clear * (1.0 - recv2[octet, x, half, 3, :, cols].astype(jnp.float32))
            for q in range(4):
                send3[octet, zl, q] = total[q] if q < 3 else clear
            if comm:
                @pl.when(my_zl != zl)
                def _(zl=zl):
                    pltpu.make_async_remote_copy(
                        src_ref=send3.at[octet, zl], dst_ref=out_ref.at[:, rows, :],
                        send_sem=send_sem.at[2], recv_sem=recv3_sem,
                        device_id=same_plane(my_x, zl), device_id_type=MESH,
                    ).start()
        out_ref[:, rows, :] = send3[octet, my_zl]

    def slab(octet, carry):
        chunk, part = octet // 2, octet % 2
        if comm:
            @pl.when(octet == 0)
            def _():
                waiting(recv1.at[0, pl.ds(0, 63)], 0, recv1_sem.at[0], next_z).wait_recv()

            for half in range(2):
                @pl.when(octet == 2 + half)
                def _(half=half):
                    waiting(recv1.at[1, pl.ds(0, 63), half], 0, recv1_sem.at[1 + half], next_z).wait_recv()

        for zl in range(4):
            for z in range(2):
                for pair in range(8):
                    first = recv1[chunk, zl * 16 + 2 * pair, part, :, z * LANES : (z + 1) * LANES]
                    second = recv1[chunk, zl * 16 + 2 * pair + 1, part, :, z * LANES : (z + 1) * LANES]
                    rows = slice((2 * zl + z) * OCT, (2 * zl + z + 1) * OCT)
                    cols = slice(pair * LANES, (pair + 1) * LANES)
                    lhs[0, rows, cols] = jnp.where(low, first, second)
                    lhs[1, rows, cols] = jnp.where(low, second, first)

        theirs = 2 * ((my_x + 1) % 2)
        ours = 2 * (my_x % 2)
        others = [(my_x + 1) % 4, (my_x + 3) % 4]
        across = (my_x + 2) % 4
        for piece in range(8):
            transform_y(theirs, 0, piece)
        shade(octet, others, 0, 0, (theirs + 1, 1))
        for x in others:
            send_x_part(octet, x, 0)
        shade(octet, others, 1, 1, (ours, 0))
        for x in others:
            send_x_part(octet, x, 1)
        shade(octet, [across], 0, 0, (ours + 1, 1))
        send_x_part(octet, across, 0)
        shade(octet, [across], 1, 1, None)
        send_x_part(octet, across, 1)
        shade(octet, [my_x], 0, 0, None)
        shade(octet, [my_x], 1, 1, None)
        recv2[octet, my_x] = send2[octet, my_x]

        @pl.when(octet > 0)
        def _():
            combine(octet - 1)

        return carry

    lax.fori_loop(0, OCTETS, slab, 0)
    combine(OCTETS - 1)

    if comm:
        waiting(recv1.at[:, pl.ds(0, 63)], 0, recv1_sem.at[0], next_z).wait_send()
        waiting(recv2.at[:, pl.ds(0, 3)], 1, recv2_sem.at[0], next_x).wait_send()
        last = waiting(send3.at[pl.ds(0, 3)], 2, recv3_sem, next_zl)
        last.wait_send()
        last.wait_recv()
        table_copy().wait_send()


def render(spectrum, colour_table, map_index, comm=True):
    fine_pair, fine_y, coarse_pair = base_tables()
    vmem = pl.BlockSpec(memory_space=pltpu.VMEM)
    bf16, f32 = jnp.bfloat16, jnp.float32
    return pl.pallas_call(
        functools.partial(kernel, comm=comm),
        out_shape=jax.ShapeDtypeStruct((4, 128, 128), f32),
        in_specs=[pl.BlockSpec(memory_space=pltpu.HBM)] * 6,
        out_specs=vmem,
        scratch_shapes=[
            pltpu.VMEM((2, 2, 64, NX), bf16),
            pltpu.VMEM((NMAPS, 4, NCTRL), f32),
            pltpu.SMEM((2,), jnp.int32),
            pltpu.VMEM((2, FINE, NX), f32),
            pltpu.VMEM((2, 2, FINE, NY // 2), f32),
            pltpu.VMEM((2, 128, LANES), f32),
            pltpu.VMEM((NX, 256), bf16),
            pltpu.VMEM((NX, 256), bf16),
            pltpu.VMEM((256, NX), bf16),
            pltpu.VMEM((256, NX), bf16),
            pltpu.VMEM((2, 4, 2, 8, 2, OCT, 256), bf16),
            pltpu.VMEM((2, 64, 2, OCT, 256), bf16),
            pltpu.VMEM((2, 4, NY // 2, 256), bf16),
            pltpu.VMEM((2, 8 * OCT, NY // 2), bf16),
            pltpu.VMEM((4, 2, 8, LANES), f32),
            pltpu.VMEM((2, 2, 8 * OCT, 256), f32),
            pltpu.VMEM((OCTETS, 4, 2, 4, OCT, 2 * LANES), bf16),
            pltpu.VMEM((OCTETS, 4, 2, 4, OCT, 2 * LANES), bf16),
            pltpu.VMEM((OCTETS, 4, 4, OCT, LANES), f32),
            pltpu.SemaphoreType.DMA((6,)),
            pltpu.SemaphoreType.DMA((4,)),
            pltpu.SemaphoreType.DMA((3,)),
            pltpu.SemaphoreType.DMA((OCTETS,)),
            pltpu.SemaphoreType.DMA,
            pltpu.SemaphoreType.DMA,
        ],
        compiler_params=pltpu.CompilerParams(
            vmem_limit_bytes=60 << 20,
            **(dict(collective_id=0, has_side_effects=True) if comm else {}),
        ),
        name="render",
    )(spectrum, colour_table, map_index, jnp.asarray(fine_pair), jnp.asarray(fine_y), jnp.asarray(coarse_pair))


def solution(mesh):
    return jax.shard_map(
        render,
        mesh=mesh,
        in_specs=(P("depth", None, "plane", None), P(), P("depth")),
        out_specs=P(None, "plane", "depth"),
        check_vma=False,
    )
```

```python
import functools
import math

import jax
import jax.numpy as jnp
import numpy as np
from jax import lax
from jax.experimental import pallas as pl
from jax.experimental.pallas import tpu as pltpu
from jax.sharding import PartitionSpec as P

NX = 2048
NY = 2048
NCTRL = 16
NMAPS = 4
SPREAD = 3.0
OPACITY = 0.06
LANES = 128
FINE = 16
OCTETS = 4
OCT = 8
MESH = pl.DeviceIdType.MESH


def base_tables():
    fine = 2.0 * np.pi * np.outer(np.arange(FINE), np.arange(NX)) / NX
    coarse = 2.0 * np.pi * (np.outer(np.arange(128), np.arange(128)) % 128) / 128.0
    fine_pair = np.stack([np.cos(fine), np.sin(fine)]).astype(np.float32)
    odd_even = 2.0 * np.pi * np.outer(np.arange(2 * FINE), np.arange(NY // 2)) / NY
    fine_y = np.stack([np.cos(odd_even), np.sin(odd_even)]).reshape(2, FINE, 2, NY // 2)
    fine_y = np.ascontiguousarray(fine_y.transpose(2, 0, 1, 3)).astype(np.float32)
    coarse_pair = np.stack([np.cos(coarse), np.sin(coarse)]).astype(np.float32)
    return fine_pair, fine_y, coarse_pair


def kernel(
    spec_hbm, colour_hbm, map_hbm, fine_hbm, fine_y_hbm, coarse_hbm, out_ref,
    spec_ref, colour_ref, map_ref, fine_ref, fine_y_ref, coarse_ref,
    turned_ref, swapped_ref, cos_ref, sin_ref, send1, recv1, ytab, lhs, ctab, dens, send2, recv2, send3, recv3,
    in_sem, send_sem, recv1_sem, recv2_sem, recv3_sem, tab_sem, *, comm
):
    if comm:
        depth_id = lax.axis_index("depth")
        plane_id = lax.axis_index("plane")
    else:
        depth_id = jnp.int32(5)
        plane_id = jnp.int32(6)
    my_x, my_zl = depth_id // 4, depth_id % 4
    my_zh, my_j = plane_id // 8, plane_id % 8
    my_z = my_zh * 4 + my_zl

    fetches = [
        pltpu.make_async_copy(src, dst, in_sem.at[i])
        for i, (src, dst) in enumerate(
            [(fine_hbm, fine_ref), (coarse_hbm, coarse_ref), (spec_hbm, spec_ref),
             (colour_hbm, colour_ref), (map_hbm, map_ref), (fine_y_hbm, fine_y_ref)]
        )
    ]
    for fetch in fetches:
        fetch.start()

    def same_x(z, j):
        return {"depth": my_x * 4 + z % 4, "plane": (z // 4) * 8 + j}

    def same_plane(x, zl):
        return {"depth": x * 4 + zl, "plane": plane_id}

    if comm:
        barrier = pltpu.get_barrier_semaphore()

        def greet_gather(i, carry):
            z, j = (my_z + i // 8) % 8, (my_j + i % 8) % 8
            pl.semaphore_signal(barrier, inc=1, device_id=same_x(z, j), device_id_type=MESH)
            return carry

        def greet_depth(i, carry):
            pl.semaphore_signal(
                barrier, inc=1, device_id=same_plane((my_x + i) % 4, my_zl), device_id_type=MESH
            )
            return carry

        lax.fori_loop(1, 64, greet_gather, 0)
        lax.fori_loop(1, 4, greet_depth, 0)

    x_scale = 1.0 / math.sqrt(NX)
    y_scale = math.sqrt(2.0 / NY)

    def coarse_row(index, scale):
        bc = coarse_ref[0, pl.ds(index, 1), :] * scale
        bs = coarse_ref[1, pl.ds(index, 1), :] * scale
        return jnp.broadcast_to(bc, (FINE, LANES)), jnp.broadcast_to(bs, (FINE, LANES))

    def pair_z(k):
        return (my_z + 4 - k) % 8, (my_z + 4 + k + 4 * ((4 - k) // 4)) % 8

    def x_tables(chunk, k):
        for i, z in enumerate(pair_z(k)):
            first = (z // 4) * 64 + 2 * (z % 4) + chunk
            for j in range(8):
                bc, bs = coarse_row(first + 8 * j, x_scale)
                rows = slice((8 * i + j) * FINE, (8 * i + j + 1) * FINE)
                for b in range(NX // LANES):
                    cols = slice(b * LANES, (b + 1) * LANES)
                    ec, es = fine_ref[0, :, cols], fine_ref[1, :, cols]
                    cos_ref[rows, cols] = (bc * ec - bs * es).astype(jnp.bfloat16)
                    sin_ref[rows, cols] = (bs * ec + bc * es).astype(jnp.bfloat16)

    def x_rows(chunk, k):
        rows = jnp.dot(cos_ref[...], turned_ref[...], preferred_element_type=jnp.float32)
        rows += jnp.dot(sin_ref[...], swapped_ref[...], preferred_element_type=jnp.float32)
        send1[chunk, k] = rows.reshape(2, 8, 2, OCT, 256).astype(jnp.bfloat16)

    def send_x(k, part):
        zs = pair_z(k)
        if not comm:
            return

        def send(i, c):
            j = (my_j + i) % 8
            for side, z in enumerate(zs):
                if part == 0:
                    src, dst = send1.at[0, k, side, j], recv1.at[0, my_zl * 16 + plane_id]
                else:
                    src = send1.at[1, k, side, j, part - 1]
                    dst = recv1.at[1, my_zl * 16 + plane_id, part - 1]
                copy = pltpu.make_async_remote_copy(
                    src_ref=src, dst_ref=dst, send_sem=send_sem.at[0], recv_sem=recv1_sem.at[part],
                    device_id=same_x(z, j), device_id_type=MESH,
                )
                if side == 0:
                    copy.start()
                else:
                    pl.when(jnp.logical_or(k != 0, i != 0))(copy.start)
            return c

        lax.fori_loop(0, 8, send, 0)

    fetches[0].wait()
    fetches[1].wait()
    x_tables(0, 0)
    fetches[2].wait()

    source = lax.broadcasted_iota(jnp.int32, (256, 256), 0)
    column = lax.broadcasted_iota(jnp.int32, (256, 256), 1)
    part = (column // 32) % 2
    parity = (column // 64 + plane_id) % 2
    base = (column // 128) * 128 + (column % 32) * 2 + parity
    straight = jnp.where(source == base + 64 * part, 1.0, 0.0).astype(jnp.bfloat16)
    crossed = jnp.where(
        source == base + 64 * (1 - part), jnp.where(part == 0, -1.0, 1.0), 0.0
    ).astype(jnp.bfloat16)
    tn = (((0,), (0,)), ((), ()))
    spec = spec_ref[...].reshape(256, NX)
    turned_ref[...] = lax.dot_general(spec, straight, tn, preferred_element_type=jnp.float32).astype(jnp.bfloat16)
    swapped_ref[...] = lax.dot_general(spec, crossed, tn, preferred_element_type=jnp.float32).astype(jnp.bfloat16)

    x_rows(0, 0)
    fetches[3].wait()
    fetches[4].wait()

    for z in range(2):
        values = colour_ref[map_ref[z]]
        values = jnp.concatenate([values, jnp.zeros((4, LANES - NCTRL), jnp.float32)], axis=1)
        row = lax.broadcasted_iota(jnp.int32, (4, LANES), 0)
        values = jnp.where(row == 3, values * OPACITY, values)
        slopes = pltpu.roll(values, LANES - 1, 1) - values
        ctab[my_zl, z] = jnp.concatenate([values, slopes], axis=0)

    if comm:
        pl.semaphore_wait(barrier, 66)
    send_x(0, 0)
    if comm:
        for k in range(1, 4):
            pltpu.make_async_remote_copy(
                src_ref=ctab.at[my_zl], dst_ref=ctab.at[my_zl], send_sem=send_sem.at[3],
                recv_sem=tab_sem, device_id=same_plane(my_x, (my_zl + k) % 4), device_id_type=MESH,
            ).start()

    def first_half(k, carry):
        x_tables(0, k)
        x_rows(0, k)
        send_x(k, 0)
        return carry

    def second_half(k, carry):
        x_tables(1, k)
        x_rows(1, k)
        send_x(k, 1)
        return carry

    def last_part(k, carry):
        send_x(k, 2)
        return carry

    lax.fori_loop(1, 4, first_half, 0)
    lax.fori_loop(0, 4, second_half, 0)
    lax.fori_loop(0, 4, last_part, 0)
    for chunk in range(2):
        recv1[chunk, my_zl * 16 + plane_id] = send1[chunk, 0, 1, my_j]
    fetches[5].wait()

    def make_y(i, carry):
        parity, p, quarter = i // 32, (i % 32) // 2, i % 2
        bc, bs = coarse_row(4 * p + 2 * quarter, y_scale)
        base = (p // 2) * LANES + ((p + parity) % 2) * 64 + quarter * FINE
        base = pl.multiple_of(base, FINE)
        for b in range(NY // 2 // LANES):
            cols = slice(b * LANES, (b + 1) * LANES)
            ec, es = fine_y_ref[parity, 0, :, cols], fine_y_ref[parity, 1, :, cols]
            part = slice((b % 2) * LANES, (b % 2 + 1) * LANES)
            ytab[parity, b // 2, pl.ds(base, FINE), part] = (bc * ec - bs * es).astype(jnp.bfloat16)
            ytab[parity, b // 2, pl.ds(base + 32, FINE), part] = (-(bs * ec + bc * es)).astype(jnp.bfloat16)
        return carry

    lax.fori_loop(0, 64, make_y, 0)

    def table_copy():
        return pltpu.make_async_remote_copy(
            src_ref=ctab.at[pl.ds(0, 3)], dst_ref=ctab.at[pl.ds(0, 3)], send_sem=send_sem.at[3],
            recv_sem=tab_sem, device_id=same_plane(my_x, (my_zl + 1) % 4), device_id_type=MESH,
        )

    def waiting(ref, send_slot, recv, device):
        return pltpu.make_async_remote_copy(
            src_ref=ref, dst_ref=ref, send_sem=send_sem.at[send_slot], recv_sem=recv,
            device_id=device, device_id_type=MESH,
        )

    next_z = same_x((my_z + 1) % 8, my_j)
    next_x = same_plane((my_x + 1) % 4, my_zl)
    next_zl = same_plane(my_x, (my_zl + 1) % 4)
    if comm:
        table_copy().wait_recv()

    low = lax.broadcasted_iota(jnp.int32, (OCT, LANES), 1) < 64

    def transform_y(block, slot, piece):
        parity, depth = piece // 4, slice((piece % 4) * 256, (piece % 4 + 1) * 256)
        part = jnp.dot(lhs[parity, :, depth], ytab[parity, block, depth, :], preferred_element_type=jnp.float32)
        dens[slot, parity] = part if piece % 4 == 0 else dens[slot, parity] + part

    def shade(octet, xs, half, slot, following):
        tiles = [(i, c) for i in range(len(xs)) for c in range(2)]
        signs = [(1 - 2 * (x // 2)).astype(jnp.float32) for x in xs]
        colour = {t: [jnp.zeros((OCT, LANES), jnp.float32) for _ in range(3)] for t in tiles}
        clear = {t: jnp.ones((OCT, LANES), jnp.float32) for t in tiles}
        for z in range(8):
            if following is not None:
                transform_y(*following, z)
            maps = [jnp.broadcast_to(ctab[z // 2, z % 2, q : q + 1, :], (OCT, LANES)) for q in range(8)]
            for t in tiles:
                i, c = t
                at = (slice(z * OCT, (z + 1) * OCT), slice(c * LANES, (c + 1) * LANES))
                d = dens[(slot, 0, *at)] + signs[i] * dens[(slot, 1, *at)]
                position = jnp.clip((d + SPREAD) * ((NCTRL - 1) / (2.0 * SPREAD)), 0.0, NCTRL - 1.0)
                index = position.astype(jnp.int32)
                frac = position - index.astype(jnp.float32)
                value = [
                    jnp.take_along_axis(maps[q], index, axis=1, mode="promise_in_bounds")
                    + frac * jnp.take_along_axis(maps[q + 4], index, axis=1, mode="promise_in_bounds")
                    for q in range(4)
                ]
                weight = clear[t] * value[3]
                colour[t] = [colour[t][q] + weight * value[q] for q in range(3)]
                clear[t] = clear[t] - weight
        for i, c in tiles:
            for q in range(4):
                result = colour[i, c][q] if q < 3 else 1.0 - clear[i, c]
                send2[octet, xs[i], half, q, :, c * LANES : (c + 1) * LANES] = result.astype(jnp.bfloat16)

    def send_x_part(octet, x, half):
        if comm:
            pltpu.make_async_remote_copy(
                src_ref=send2.at[octet, x, half], dst_ref=recv2.at[octet, my_x, half],
                send_sem=send_sem.at[1], recv_sem=recv2_sem.at[octet],
                device_id=same_plane(x, my_zl), device_id_type=MESH,
            ).start()

    def combine(octet):
        if comm:
            waiting(recv2.at[octet, pl.ds(0, 3)], 1, recv2_sem.at[octet], next_x).wait_recv()
        rows = pl.ds(pl.multiple_of(my_zl * 32 + octet * OCT, OCT), OCT)
        for zl in range(4):
            half, cols = zl // 2, slice((zl % 2) * LANES, (zl % 2 + 1) * LANES)
            total = [recv2[octet, 0, half, q, :, cols].astype(jnp.float32) for q in range(3)]
            clear = 1.0 - recv2[octet, 0, half, 3, :, cols].astype(jnp.float32)
            for x in range(1, 4):
                for q in range(3):
                    total[q] = total[q] + clear * recv2[octet, x, half, q, :, cols].astype(jnp.float32)
                clear = clear * (1.0 - recv2[octet, x, half, 3, :, cols].astype(jnp.float32))
            for q in range(4):
                result = total[q] if q < 3 else clear
                send3[octet, zl, q] = result.astype(jnp.bfloat16)

                @pl.when(my_zl == zl)
                def _(q=q, result=result):
                    out_ref[q, rows, :] = result

            if comm:
                @pl.when(my_zl != zl)
                def _(zl=zl):
                    pltpu.make_async_remote_copy(
                        src_ref=send3.at[octet, zl], dst_ref=recv3.at[octet, my_zl],
                        send_sem=send_sem.at[2], recv_sem=recv3_sem,
                        device_id=same_plane(my_x, zl), device_id_type=MESH,
                    ).start()

    def slab(octet, carry):
        chunk, part = octet // 2, octet % 2
        if comm:
            @pl.when(octet == 0)
            def _():
                waiting(recv1.at[0, pl.ds(0, 63)], 0, recv1_sem.at[0], next_z).wait_recv()

            for half in range(2):
                @pl.when(octet == 2 + half)
                def _(half=half):
                    waiting(recv1.at[1, pl.ds(0, 63), half], 0, recv1_sem.at[1 + half], next_z).wait_recv()

        for zl in range(4):
            for z in range(2):
                for pair in range(8):
                    first = recv1[chunk, zl * 16 + 2 * pair, part, :, z * LANES : (z + 1) * LANES]
                    second = recv1[chunk, zl * 16 + 2 * pair + 1, part, :, z * LANES : (z + 1) * LANES]
                    rows = slice((2 * zl + z) * OCT, (2 * zl + z + 1) * OCT)
                    cols = slice(pair * LANES, (pair + 1) * LANES)
                    lhs[0, rows, cols] = jnp.where(low, first, second)
                    lhs[1, rows, cols] = jnp.where(low, second, first)

        theirs = 2 * ((my_x + 1) % 2)
        ours = 2 * (my_x % 2)
        others = [(my_x + 1) % 4, (my_x + 3) % 4]
        across = (my_x + 2) % 4
        for piece in range(8):
            transform_y(theirs, 0, piece)
        shade(octet, others, 0, 0, (theirs + 1, 1))
        for x in others:
            send_x_part(octet, x, 0)
        shade(octet, others, 1, 1, (ours, 0))
        for x in others:
            send_x_part(octet, x, 1)
        shade(octet, [across], 0, 0, (ours + 1, 1))
        send_x_part(octet, across, 0)
        shade(octet, [across], 1, 1, None)
        send_x_part(octet, across, 1)
        shade(octet, [my_x], 0, 0, None)
        shade(octet, [my_x], 1, 1, None)
        recv2[octet, my_x] = send2[octet, my_x]

        @pl.when(octet > 0)
        def _():
            combine(octet - 1)

        return carry

    lax.fori_loop(0, OCTETS, slab, 0)
    combine(OCTETS - 1)

    if comm:
        waiting(recv1.at[:, pl.ds(0, 63)], 0, recv1_sem.at[0], next_z).wait_send()
        waiting(recv2.at[:, pl.ds(0, 3)], 1, recv2_sem.at[0], next_x).wait_send()
        last = waiting(send3.at[pl.ds(0, 3)], 2, recv3_sem, next_zl)
        last.wait_recv()
        for zl in range(4):
            @pl.when(my_zl != zl)
            def _(zl=zl):
                for octet in range(OCTETS):
                    rows = slice(zl * 32 + octet * OCT, zl * 32 + (octet + 1) * OCT)
                    out_ref[:, rows, :] = recv3[octet, zl].astype(jnp.float32)

        last.wait_send()
        table_copy().wait_send()


def render(spectrum, colour_table, map_index, comm=True):
    operands = [spectrum, colour_table, map_index, *map(jnp.asarray, base_tables())]
    vmem = pl.BlockSpec(memory_space=pltpu.VMEM)
    bf16, f32 = jnp.bfloat16, jnp.float32
    return pl.pallas_call(
        functools.partial(kernel, comm=comm),
        out_shape=jax.ShapeDtypeStruct((4, 128, 128), f32),
        in_specs=[pl.BlockSpec(memory_space=pltpu.HBM)] * 6,
        out_specs=vmem,
        scratch_shapes=[
            pltpu.VMEM((2, 2, 64, NX), bf16),
            pltpu.VMEM((NMAPS, 4, NCTRL), f32),
            pltpu.SMEM((2,), jnp.int32),
            pltpu.VMEM((2, FINE, NX), f32),
            pltpu.VMEM((2, 2, FINE, NY // 2), f32),
            pltpu.VMEM((2, 128, LANES), f32),
            pltpu.VMEM((NX, 256), bf16),
            pltpu.VMEM((NX, 256), bf16),
            pltpu.VMEM((256, NX), bf16),
            pltpu.VMEM((256, NX), bf16),
            pltpu.VMEM((2, 4, 2, 8, 2, OCT, 256), bf16),
            pltpu.VMEM((2, 64, 2, OCT, 256), bf16),
            pltpu.VMEM((2, 4, NY // 2, 256), bf16),
            pltpu.VMEM((2, 8 * OCT, NY // 2), bf16),
            pltpu.VMEM((4, 2, 8, LANES), f32),
            pltpu.VMEM((2, 2, 8 * OCT, 256), f32),
            pltpu.VMEM((OCTETS, 4, 2, 4, OCT, 2 * LANES), bf16),
            pltpu.VMEM((OCTETS, 4, 2, 4, OCT, 2 * LANES), bf16),
            pltpu.VMEM((OCTETS, 4, 4, OCT, LANES), bf16),
            pltpu.VMEM((OCTETS, 4, 4, OCT, LANES), bf16),
            pltpu.SemaphoreType.DMA((6,)),
            pltpu.SemaphoreType.DMA((4,)),
            pltpu.SemaphoreType.DMA((3,)),
            pltpu.SemaphoreType.DMA((OCTETS,)),
            pltpu.SemaphoreType.DMA,
            pltpu.SemaphoreType.DMA,
        ],
        compiler_params=pltpu.CompilerParams(
            vmem_limit_bytes=40 << 20,
            **(dict(collective_id=0, has_side_effects=True) if comm else {}),
        ),
        name="render",
    )(*[pltpu.with_memory_space_constraint(operand, pltpu.HBM) for operand in operands])


def solution(mesh):
    return jax.shard_map(
        render,
        mesh=mesh,
        in_specs=(P("depth", None, "plane", None), P(), P("depth")),
        out_specs=P(None, "plane", "depth"),
        check_vma=False,
    )
```

```python
import functools
import math

import jax
import jax.numpy as jnp
import numpy as np
from jax import lax
from jax.experimental import pallas as pl
from jax.experimental.pallas import tpu as pltpu
from jax.sharding import PartitionSpec as P

NX = 2048
NY = 2048
NCTRL = 16
NMAPS = 4
SPREAD = 3.0
OPACITY = 0.06
LANES = 128
FINE = 16
OCTETS = 4
OCT = 8
MESH = pl.DeviceIdType.MESH


def base_tables():
    fine = 2.0 * np.pi * np.outer(np.arange(FINE), np.arange(NX)) / NX
    coarse = 2.0 * np.pi * (np.outer(np.arange(128), np.arange(128)) % 128) / 128.0
    fine_pair = np.stack([np.cos(fine), np.sin(fine)]).astype(np.float32)
    odd_even = 2.0 * np.pi * np.outer(np.arange(2 * FINE), np.arange(NY // 2)) / NY
    fine_y = np.stack([np.cos(odd_even), np.sin(odd_even)]).reshape(2, FINE, 2, NY // 2)
    fine_y = np.ascontiguousarray(fine_y.transpose(2, 0, 1, 3)).astype(np.float32)
    coarse_pair = np.stack([np.cos(coarse), np.sin(coarse)]).astype(np.float32)
    return fine_pair, fine_y, coarse_pair


def kernel(
    spec_hbm, colour_hbm, map_hbm, fine_hbm, fine_y_hbm, coarse_hbm, out_ref,
    spec_ref, colour_ref, map_ref, fine_ref, fine_y_ref, coarse_ref,
    turned_ref, swapped_ref, cos_ref, sin_ref, send1, recv1, ytab, lhs, ctab, dens, send2, recv2, send3, recv3, direct,
    in_sem, send_sem, recv1_sem, recv2_sem, recv3_sem, direct_sem, tab_sem, *, comm
):
    if comm:
        depth_id = lax.axis_index("depth")
        plane_id = lax.axis_index("plane")
    else:
        depth_id = jnp.int32(5)
        plane_id = jnp.int32(6)
    my_x, my_zl = depth_id // 4, depth_id % 4
    my_zh, my_j = plane_id // 8, plane_id % 8
    my_z = my_zh * 4 + my_zl

    fetches = [
        pltpu.make_async_copy(src, dst, in_sem.at[i])
        for i, (src, dst) in enumerate(
            [(fine_hbm, fine_ref), (coarse_hbm, coarse_ref), (spec_hbm, spec_ref),
             (colour_hbm, colour_ref), (map_hbm, map_ref), (fine_y_hbm, fine_y_ref)]
        )
    ]
    for fetch in fetches:
        fetch.start()

    def same_x(z, j):
        return {"depth": my_x * 4 + z % 4, "plane": (z // 4) * 8 + j}

    def same_plane(x, zl):
        return {"depth": x * 4 + zl, "plane": plane_id}

    if comm:
        barrier = pltpu.get_barrier_semaphore()

        def greet_gather(i, carry):
            z, j = (my_z + i // 8) % 8, (my_j + i % 8) % 8
            pl.semaphore_signal(barrier, inc=1, device_id=same_x(z, j), device_id_type=MESH)
            return carry

        def greet_depth(i, carry):
            pl.semaphore_signal(
                barrier, inc=1, device_id=same_plane((my_x + 1 + i // 4) % 4, i % 4), device_id_type=MESH
            )
            return carry

        lax.fori_loop(1, 64, greet_gather, 0)
        lax.fori_loop(0, 12, greet_depth, 0)

    x_scale = 1.0 / math.sqrt(NX)
    y_scale = math.sqrt(2.0 / NY)

    def coarse_row(index, scale):
        bc = coarse_ref[0, pl.ds(index, 1), :] * scale
        bs = coarse_ref[1, pl.ds(index, 1), :] * scale
        return jnp.broadcast_to(bc, (FINE, LANES)), jnp.broadcast_to(bs, (FINE, LANES))

    def pair_z(k):
        return (my_z + 4 - k) % 8, (my_z + 4 + k + 4 * ((4 - k) // 4)) % 8

    def x_tables(chunk, k):
        for i, z in enumerate(pair_z(k)):
            first = (z // 4) * 64 + 2 * (z % 4) + chunk
            for j in range(8):
                bc, bs = coarse_row(first + 8 * j, x_scale)
                rows = slice((8 * i + j) * FINE, (8 * i + j + 1) * FINE)
                for b in range(NX // LANES):
                    cols = slice(b * LANES, (b + 1) * LANES)
                    ec, es = fine_ref[0, :, cols], fine_ref[1, :, cols]
                    cos_ref[rows, cols] = (bc * ec - bs * es).astype(jnp.bfloat16)
                    sin_ref[rows, cols] = (bs * ec + bc * es).astype(jnp.bfloat16)

    def x_rows(chunk, k):
        rows = jnp.dot(cos_ref[...], turned_ref[...], preferred_element_type=jnp.float32)
        rows += jnp.dot(sin_ref[...], swapped_ref[...], preferred_element_type=jnp.float32)
        send1[chunk, k] = rows.reshape(2, 8, 2, OCT, 256).astype(jnp.bfloat16)

    def send_x(k, part):
        zs = pair_z(k)
        if not comm:
            return

        def send(i, c):
            j = (my_j + i) % 8
            for side, z in enumerate(zs):
                if part == 0:
                    src, dst = send1.at[0, k, side, j], recv1.at[0, my_zl * 16 + plane_id]
                else:
                    src = send1.at[1, k, side, j, part - 1]
                    dst = recv1.at[1, my_zl * 16 + plane_id, part - 1]
                copy = pltpu.make_async_remote_copy(
                    src_ref=src, dst_ref=dst, send_sem=send_sem.at[0], recv_sem=recv1_sem.at[part],
                    device_id=same_x(z, j), device_id_type=MESH,
                )
                if side == 0:
                    copy.start()
                else:
                    pl.when(jnp.logical_or(k != 0, i != 0))(copy.start)
            return c

        lax.fori_loop(0, 8, send, 0)

    fetches[0].wait()
    fetches[1].wait()
    x_tables(0, 0)
    fetches[2].wait()

    source = lax.broadcasted_iota(jnp.int32, (256, 256), 0)
    column = lax.broadcasted_iota(jnp.int32, (256, 256), 1)
    part = (column // 32) % 2
    parity = (column // 64 + plane_id) % 2
    base = (column // 128) * 128 + (column % 32) * 2 + parity
    straight = jnp.where(source == base + 64 * part, 1.0, 0.0).astype(jnp.bfloat16)
    crossed = jnp.where(
        source == base + 64 * (1 - part), jnp.where(part == 0, -1.0, 1.0), 0.0
    ).astype(jnp.bfloat16)
    tn = (((0,), (0,)), ((), ()))
    spec = spec_ref[...].reshape(256, NX)
    turned_ref[...] = lax.dot_general(spec, straight, tn, preferred_element_type=jnp.float32).astype(jnp.bfloat16)
    swapped_ref[...] = lax.dot_general(spec, crossed, tn, preferred_element_type=jnp.float32).astype(jnp.bfloat16)

    x_rows(0, 0)
    fetches[3].wait()
    fetches[4].wait()

    for z in range(2):
        values = colour_ref[map_ref[z]]
        values = jnp.concatenate([values, jnp.zeros((4, LANES - NCTRL), jnp.float32)], axis=1)
        row = lax.broadcasted_iota(jnp.int32, (4, LANES), 0)
        values = jnp.where(row == 3, values * OPACITY, values)
        slopes = pltpu.roll(values, LANES - 1, 1) - values
        ctab[my_zl, z] = jnp.concatenate([values, slopes], axis=0)

    if comm:
        pl.semaphore_wait(barrier, 75)
    send_x(0, 0)
    if comm:
        for k in range(1, 4):
            pltpu.make_async_remote_copy(
                src_ref=ctab.at[my_zl], dst_ref=ctab.at[my_zl], send_sem=send_sem.at[3],
                recv_sem=tab_sem, device_id=same_plane(my_x, (my_zl + k) % 4), device_id_type=MESH,
            ).start()

    def first_half(k, carry):
        x_tables(0, k)
        x_rows(0, k)
        send_x(k, 0)
        return carry

    def second_half(k, carry):
        x_tables(1, k)
        x_rows(1, k)
        send_x(k, 1)
        return carry

    def last_part(k, carry):
        send_x(k, 2)
        return carry

    lax.fori_loop(1, 4, first_half, 0)
    lax.fori_loop(0, 4, second_half, 0)
    lax.fori_loop(0, 4, last_part, 0)
    for chunk in range(2):
        recv1[chunk, my_zl * 16 + plane_id] = send1[chunk, 0, 1, my_j]
    fetches[5].wait()

    def make_y(i, carry):
        parity, p, quarter = i // 32, (i % 32) // 2, i % 2
        bc, bs = coarse_row(4 * p + 2 * quarter, y_scale)
        base = (p // 2) * LANES + ((p + parity) % 2) * 64 + quarter * FINE
        base = pl.multiple_of(base, FINE)
        for b in range(NY // 2 // LANES):
            cols = slice(b * LANES, (b + 1) * LANES)
            ec, es = fine_y_ref[parity, 0, :, cols], fine_y_ref[parity, 1, :, cols]
            part = slice((b % 2) * LANES, (b % 2 + 1) * LANES)
            ytab[parity, b // 2, pl.ds(base, FINE), part] = (bc * ec - bs * es).astype(jnp.bfloat16)
            ytab[parity, b // 2, pl.ds(base + 32, FINE), part] = (-(bs * ec + bc * es)).astype(jnp.bfloat16)
        return carry

    lax.fori_loop(0, 64, make_y, 0)

    def table_copy():
        return pltpu.make_async_remote_copy(
            src_ref=ctab.at[pl.ds(0, 3)], dst_ref=ctab.at[pl.ds(0, 3)], send_sem=send_sem.at[3],
            recv_sem=tab_sem, device_id=same_plane(my_x, (my_zl + 1) % 4), device_id_type=MESH,
        )

    def waiting(ref, send_slot, recv, device):
        return pltpu.make_async_remote_copy(
            src_ref=ref, dst_ref=ref, send_sem=send_sem.at[send_slot], recv_sem=recv,
            device_id=device, device_id_type=MESH,
        )

    next_z = same_x((my_z + 1) % 8, my_j)
    next_x = same_plane((my_x + 1) % 4, my_zl)
    next_zl = same_plane(my_x, (my_zl + 1) % 4)
    if comm:
        table_copy().wait_recv()

    low = lax.broadcasted_iota(jnp.int32, (OCT, LANES), 1) < 64

    def transform_y(block, slot, piece):
        parity, depth = piece // 4, slice((piece % 4) * 256, (piece % 4 + 1) * 256)
        part = jnp.dot(lhs[parity, :, depth], ytab[parity, block, depth, :], preferred_element_type=jnp.float32)
        dens[slot, parity] = part if piece % 4 == 0 else dens[slot, parity] + part

    def shade(octet, xs, half, slot, following):
        tiles = [(i, c) for i in range(len(xs)) for c in range(2)]
        signs = [(1 - 2 * (x // 2)).astype(jnp.float32) for x in xs]
        colour = {t: [jnp.zeros((OCT, LANES), jnp.float32) for _ in range(3)] for t in tiles}
        clear = {t: jnp.ones((OCT, LANES), jnp.float32) for t in tiles}
        for z in range(8):
            if following is not None:
                transform_y(*following, z)
            maps = [jnp.broadcast_to(ctab[z // 2, z % 2, q : q + 1, :], (OCT, LANES)) for q in range(8)]
            for t in tiles:
                i, c = t
                at = (slice(z * OCT, (z + 1) * OCT), slice(c * LANES, (c + 1) * LANES))
                d = dens[(slot, 0, *at)] + signs[i] * dens[(slot, 1, *at)]
                position = jnp.clip((d + SPREAD) * ((NCTRL - 1) / (2.0 * SPREAD)), 0.0, NCTRL - 1.0)
                index = position.astype(jnp.int32)
                frac = position - index.astype(jnp.float32)
                value = [
                    jnp.take_along_axis(maps[q], index, axis=1, mode="promise_in_bounds")
                    + frac * jnp.take_along_axis(maps[q + 4], index, axis=1, mode="promise_in_bounds")
                    for q in range(4)
                ]
                weight = clear[t] * value[3]
                colour[t] = [colour[t][q] + weight * value[q] for q in range(3)]
                clear[t] = clear[t] - weight
        for i, c in tiles:
            for q in range(4):
                result = colour[i, c][q] if q < 3 else 1.0 - clear[i, c]
                send2[octet, xs[i], half, q, :, c * LANES : (c + 1) * LANES] = result.astype(jnp.bfloat16)

    def columns_of(c):
        return slice(c * LANES, (c + 1) * LANES)

    def send_part(octet, x, half, own=False):
        if not comm:
            return

        if not own:
            @pl.when(octet < OCTETS - 1)
            def _():
                pltpu.make_async_remote_copy(
                    src_ref=send2.at[octet, x, half], dst_ref=recv2.at[octet, my_x, half],
                    send_sem=send_sem.at[1], recv_sem=recv2_sem.at[octet],
                    device_id=same_plane(x, my_zl), device_id_type=MESH,
                ).start()

        @pl.when(octet == OCTETS - 1)
        def _():
            for c in range(2):
                zl = 2 * half + c
                copy = pltpu.make_async_remote_copy(
                    src_ref=send2.at[OCTETS - 1, x, half, :, :, columns_of(c)],
                    dst_ref=direct.at[my_x * 4 + my_zl], send_sem=send_sem.at[4], recv_sem=direct_sem,
                    device_id=same_plane(x, zl), device_id_type=MESH,
                )
                if own:
                    pl.when(zl != my_zl)(copy.start)
                else:
                    copy.start()

    def over(parts):
        total = [parts(0, q).astype(jnp.float32) for q in range(3)]
        clear = 1.0 - parts(0, 3).astype(jnp.float32)
        for x in range(1, 4):
            for q in range(3):
                total[q] = total[q] + clear * parts(x, q).astype(jnp.float32)
            clear = clear * (1.0 - parts(x, 3).astype(jnp.float32))
        return [*total, clear]

    def combine_last():
        if comm:
            waiting(direct.at[pl.ds(0, 15)], 4, direct_sem, next_x).wait_recv()
        for zl in range(4):
            rows = slice(zl * 32 + 3 * OCT, zl * 32 + 4 * OCT)
            result = over(lambda x, q, zl=zl: direct[x * 4 + zl, q])
            for q in range(4):
                out_ref[q, rows, :] = result[q]

    def combine(octet):
        if comm:
            waiting(recv2.at[octet, pl.ds(0, 3)], 1, recv2_sem.at[octet], next_x).wait_recv()
        rows = pl.ds(pl.multiple_of(my_zl * 32 + octet * OCT, OCT), OCT)
        for zl in range(4):
            half, cols = zl // 2, slice((zl % 2) * LANES, (zl % 2 + 1) * LANES)
            results = over(lambda x, q, half=half, cols=cols: recv2[octet, x, half, q, :, cols])
            for q in range(4):
                result = results[q]
                send3[octet, zl, q] = result.astype(jnp.bfloat16)

                @pl.when(my_zl == zl)
                def _(q=q, result=result):
                    out_ref[q, rows, :] = result

            if comm:
                @pl.when(my_zl != zl)
                def _(zl=zl):
                    pltpu.make_async_remote_copy(
                        src_ref=send3.at[octet, zl], dst_ref=recv3.at[octet, my_zl],
                        send_sem=send_sem.at[2], recv_sem=recv3_sem,
                        device_id=same_plane(my_x, zl), device_id_type=MESH,
                    ).start()

    def slab(octet, carry):
        chunk, part = octet // 2, octet % 2
        if comm:
            @pl.when(octet == 0)
            def _():
                waiting(recv1.at[0, pl.ds(0, 63)], 0, recv1_sem.at[0], next_z).wait_recv()

            for half in range(2):
                @pl.when(octet == 2 + half)
                def _(half=half):
                    waiting(recv1.at[1, pl.ds(0, 63), half], 0, recv1_sem.at[1 + half], next_z).wait_recv()

        for zl in range(4):
            for z in range(2):
                for pair in range(8):
                    first = recv1[chunk, zl * 16 + 2 * pair, part, :, z * LANES : (z + 1) * LANES]
                    second = recv1[chunk, zl * 16 + 2 * pair + 1, part, :, z * LANES : (z + 1) * LANES]
                    rows = slice((2 * zl + z) * OCT, (2 * zl + z + 1) * OCT)
                    cols = slice(pair * LANES, (pair + 1) * LANES)
                    lhs[0, rows, cols] = jnp.where(low, first, second)
                    lhs[1, rows, cols] = jnp.where(low, second, first)

        theirs = 2 * ((my_x + 1) % 2)
        ours = 2 * (my_x % 2)
        others = [(my_x + 1) % 4, (my_x + 3) % 4]
        across = (my_x + 2) % 4
        for piece in range(8):
            transform_y(theirs + 1 - my_zl // 2, 0, piece)
        far, near = 1 - my_zl // 2, my_zl // 2
        shade(octet, others, far, 0, (theirs + near, 1))
        for x in others:
            send_part(octet, x, far)
        shade(octet, others, near, 1, (ours + far, 0))
        for x in others:
            send_part(octet, x, near)
        shade(octet, [across], far, 0, (ours + near, 1))
        send_part(octet, across, far)
        shade(octet, [across], near, 1, None)
        send_part(octet, across, near)

        @pl.when(octet > 0)
        def _():
            combine(octet - 1)

        shade(octet, [my_x], far, 0, None)
        send_part(octet, my_x, far, own=True)
        shade(octet, [my_x], near, 1, None)
        send_part(octet, my_x, near, own=True)

        @pl.when(octet < OCTETS - 1)
        def _():
            recv2[octet, my_x] = send2[octet, my_x]

        return carry

    lax.fori_loop(0, OCTETS, slab, 0)
    for c in range(2):
        @pl.when(my_zl % 2 == c)
        def _(c=c):
            direct[depth_id] = send2[OCTETS - 1, my_x, my_zl // 2, :, :, columns_of(c)]

    combine_last()

    if comm:
        waiting(recv1.at[:, pl.ds(0, 63)], 0, recv1_sem.at[0], next_z).wait_send()
        waiting(recv2.at[pl.ds(0, 3), pl.ds(0, 3)], 1, recv2_sem.at[0], next_x).wait_send()
        waiting(direct.at[pl.ds(0, 15)], 4, direct_sem, next_x).wait_send()
        last = waiting(send3.at[:, pl.ds(0, 3)], 2, recv3_sem, next_zl)
        last.wait_recv()
        for zl in range(4):
            @pl.when(my_zl != zl)
            def _(zl=zl):
                for octet in range(OCTETS - 1):
                    rows = slice(zl * 32 + octet * OCT, zl * 32 + (octet + 1) * OCT)
                    out_ref[:, rows, :] = recv3[octet, zl].astype(jnp.float32)

        last.wait_send()
        table_copy().wait_send()


def render(spectrum, colour_table, map_index, comm=True):
    operands = [spectrum, colour_table, map_index, *map(jnp.asarray, base_tables())]
    vmem = pl.BlockSpec(memory_space=pltpu.VMEM)
    bf16, f32 = jnp.bfloat16, jnp.float32
    return pl.pallas_call(
        functools.partial(kernel, comm=comm),
        out_shape=jax.ShapeDtypeStruct((4, 128, 128), f32),
        in_specs=[pl.BlockSpec(memory_space=pltpu.HBM)] * 6,
        out_specs=vmem,
        scratch_shapes=[
            pltpu.VMEM((2, 2, 64, NX), bf16),
            pltpu.VMEM((NMAPS, 4, NCTRL), f32),
            pltpu.SMEM((2,), jnp.int32),
            pltpu.VMEM((2, FINE, NX), f32),
            pltpu.VMEM((2, 2, FINE, NY // 2), f32),
            pltpu.VMEM((2, 128, LANES), f32),
            pltpu.VMEM((NX, 256), bf16),
            pltpu.VMEM((NX, 256), bf16),
            pltpu.VMEM((256, NX), bf16),
            pltpu.VMEM((256, NX), bf16),
            pltpu.VMEM((2, 4, 2, 8, 2, OCT, 256), bf16),
            pltpu.VMEM((2, 64, 2, OCT, 256), bf16),
            pltpu.VMEM((2, 4, NY // 2, 256), bf16),
            pltpu.VMEM((2, 8 * OCT, NY // 2), bf16),
            pltpu.VMEM((4, 2, 8, LANES), f32),
            pltpu.VMEM((2, 2, 8 * OCT, 256), f32),
            pltpu.VMEM((OCTETS, 4, 2, 4, OCT, 2 * LANES), bf16),
            pltpu.VMEM((OCTETS - 1, 4, 2, 4, OCT, 2 * LANES), bf16),
            pltpu.VMEM((OCTETS - 1, 4, 4, OCT, LANES), bf16),
            pltpu.VMEM((OCTETS - 1, 4, 4, OCT, LANES), bf16),
            pltpu.VMEM((16, 4, OCT, LANES), bf16),
            pltpu.SemaphoreType.DMA((6,)),
            pltpu.SemaphoreType.DMA((5,)),
            pltpu.SemaphoreType.DMA((3,)),
            pltpu.SemaphoreType.DMA((OCTETS - 1,)),
            pltpu.SemaphoreType.DMA,
            pltpu.SemaphoreType.DMA,
            pltpu.SemaphoreType.DMA,
        ],
        compiler_params=pltpu.CompilerParams(
            vmem_limit_bytes=40 << 20,
            **(dict(collective_id=0, has_side_effects=True) if comm else {}),
        ),
        name="render",
    )(*[pltpu.with_memory_space_constraint(operand, pltpu.HBM) for operand in operands])


def solution(mesh):
    return jax.shard_map(
        render,
        mesh=mesh,
        in_specs=(P("depth", None, "plane", None), P(), P("depth")),
        out_specs=P(None, "plane", "depth"),
        check_vma=False,
    )
```

```python
import functools
import math

import jax
import jax.numpy as jnp
import numpy as np
from jax import lax
from jax.experimental import pallas as pl
from jax.experimental.pallas import tpu as pltpu
from jax.sharding import PartitionSpec as P

NX = 2048
NY = 2048
NCTRL = 16
NMAPS = 4
SPREAD = 3.0
OPACITY = 0.06
LANES = 128
FINE = 16
OCTETS = 4
OCT = 8
MESH = pl.DeviceIdType.MESH


def base_tables():
    fine = 2.0 * np.pi * np.outer(np.arange(FINE), np.arange(NX)) / NX
    coarse = 2.0 * np.pi * (np.outer(np.arange(128), np.arange(128)) % 128) / 128.0
    fine_pair = np.stack([np.cos(fine), np.sin(fine)]).astype(np.float32)
    odd_even = 2.0 * np.pi * np.outer(np.arange(2 * FINE), np.arange(NY // 2)) / NY
    fine_y = np.stack([np.cos(odd_even), np.sin(odd_even)]).reshape(2, FINE, 2, NY // 2)
    fine_y = np.ascontiguousarray(fine_y.transpose(2, 0, 1, 3)).astype(np.float32)
    coarse_pair = np.stack([np.cos(coarse), np.sin(coarse)]).astype(np.float32)
    return fine_pair, fine_y, coarse_pair


def kernel(
    spec_hbm, colour_hbm, map_hbm, fine_hbm, fine_y_hbm, coarse_hbm, out_ref,
    spec_ref, colour_ref, map_ref, fine_ref, fine_y_ref, coarse_ref,
    turned_ref, swapped_ref, cos_ref, sin_ref, send1, recv1, ytab, lhs, ctab, dens, send2, recv2, send3, recv3, direct,
    in_sem, send_sem, recv1_sem, recv2_sem, recv3_sem, direct_sem, tab_sem, *, comm
):
    if comm:
        depth_id = lax.axis_index("depth")
        plane_id = lax.axis_index("plane")
    else:
        depth_id = jnp.int32(5)
        plane_id = jnp.int32(6)
    my_x, my_zl = depth_id // 4, depth_id % 4
    my_zh, my_j = plane_id // 8, plane_id % 8
    my_z = my_zh * 4 + my_zl

    fetches = [
        pltpu.make_async_copy(src, dst, in_sem.at[i])
        for i, (src, dst) in enumerate(
            [(fine_hbm, fine_ref), (coarse_hbm, coarse_ref), (spec_hbm, spec_ref),
             (colour_hbm, colour_ref), (map_hbm, map_ref), (fine_y_hbm, fine_y_ref)]
        )
    ]
    for fetch in fetches:
        fetch.start()

    def same_x(z, j):
        return {"depth": my_x * 4 + z % 4, "plane": (z // 4) * 8 + j}

    def same_plane(x, zl):
        return {"depth": x * 4 + zl, "plane": plane_id}

    if comm:
        barrier = pltpu.get_barrier_semaphore()

        def greet_gather(i, carry):
            z, j = (my_z + i // 8) % 8, (my_j + i % 8) % 8
            pl.semaphore_signal(barrier, inc=1, device_id=same_x(z, j), device_id_type=MESH)
            return carry

        def greet_depth(i, carry):
            pl.semaphore_signal(
                barrier, inc=1, device_id=same_plane((my_x + 1 + i // 4) % 4, i % 4), device_id_type=MESH
            )
            return carry

        lax.fori_loop(1, 64, greet_gather, 0)
        lax.fori_loop(0, 12, greet_depth, 0)

    x_scale = 1.0 / math.sqrt(NX)
    y_scale = math.sqrt(2.0 / NY)

    def coarse_row(index, scale):
        bc = coarse_ref[0, pl.ds(index, 1), :] * scale
        bs = coarse_ref[1, pl.ds(index, 1), :] * scale
        return jnp.broadcast_to(bc, (FINE, LANES)), jnp.broadcast_to(bs, (FINE, LANES))

    def pair_z(k):
        return (my_z + 4 - k) % 8, (my_z + 4 + k + 4 * ((4 - k) // 4)) % 8

    def x_tables(chunk, k):
        for i, z in enumerate(pair_z(k)):
            first = (z // 4) * 64 + 2 * (z % 4) + chunk
            for j in range(8):
                bc, bs = coarse_row(first + 8 * j, x_scale)
                rows = slice((8 * i + j) * FINE, (8 * i + j + 1) * FINE)
                for b in range(NX // LANES):
                    cols = slice(b * LANES, (b + 1) * LANES)
                    ec, es = fine_ref[0, :, cols], fine_ref[1, :, cols]
                    cos_ref[rows, cols] = (bc * ec - bs * es).astype(jnp.bfloat16)
                    sin_ref[rows, cols] = (bs * ec + bc * es).astype(jnp.bfloat16)

    def x_rows(chunk, k):
        rows = jnp.dot(cos_ref[...], turned_ref[...], preferred_element_type=jnp.float32)
        rows += jnp.dot(sin_ref[...], swapped_ref[...], preferred_element_type=jnp.float32)
        send1[chunk, k] = rows.reshape(2, 8, 2, OCT, 256).astype(jnp.bfloat16)

    def x_side(side):
        half = slice(128 * side, 128 * (side + 1))
        rows = jnp.dot(cos_ref[half, :], turned_ref[...], preferred_element_type=jnp.float32)
        rows += jnp.dot(sin_ref[half, :], swapped_ref[...], preferred_element_type=jnp.float32)
        send1[0, 0, side] = rows.reshape(8, 2, OCT, 256).astype(jnp.bfloat16)

    def send_x(k, part, sides=(0, 1)):
        zs = pair_z(k)
        if not comm:
            return

        def send(i, c):
            j = (my_j + i) % 8
            for side in sides:
                z = zs[side]
                if part == 0:
                    src, dst = send1.at[0, k, side, j], recv1.at[0, my_zl * 16 + plane_id]
                else:
                    src = send1.at[1, k, side, j, part - 1]
                    dst = recv1.at[1, my_zl * 16 + plane_id, part - 1]
                copy = pltpu.make_async_remote_copy(
                    src_ref=src, dst_ref=dst, send_sem=send_sem.at[0], recv_sem=recv1_sem.at[part],
                    device_id=same_x(z, j), device_id_type=MESH,
                )
                if side == 0:
                    copy.start()
                else:
                    pl.when(jnp.logical_or(k != 0, i != 0))(copy.start)
            return c

        lax.fori_loop(0, 8, send, 0)

    fetches[0].wait()
    fetches[1].wait()
    x_tables(0, 0)
    fetches[2].wait()

    source = lax.broadcasted_iota(jnp.int32, (256, 256), 0)
    column = lax.broadcasted_iota(jnp.int32, (256, 256), 1)
    part = (column // 32) % 2
    parity = (column // 64 + plane_id) % 2
    base = (column // 128) * 128 + (column % 32) * 2 + parity
    straight = jnp.where(source == base + 64 * part, 1.0, 0.0).astype(jnp.bfloat16)
    crossed = jnp.where(
        source == base + 64 * (1 - part), jnp.where(part == 0, -1.0, 1.0), 0.0
    ).astype(jnp.bfloat16)
    tn = (((0,), (0,)), ((), ()))
    spec = spec_ref[...].reshape(256, NX)
    both = lax.dot_general(
        spec, jnp.concatenate([straight, crossed], axis=1), tn, preferred_element_type=jnp.float32
    ).astype(jnp.bfloat16)
    turned_ref[...] = both[:, :256]
    swapped_ref[...] = both[:, 256:]

    x_side(0)
    if comm:
        pl.semaphore_wait(barrier, 75)
    send_x(0, 0, sides=(0,))
    x_side(1)
    send_x(0, 0, sides=(1,))
    fetches[3].wait()
    fetches[4].wait()

    for z in range(2):
        values = colour_ref[map_ref[z]]
        values = jnp.concatenate([values, jnp.zeros((4, LANES - NCTRL), jnp.float32)], axis=1)
        row = lax.broadcasted_iota(jnp.int32, (4, LANES), 0)
        values = jnp.where(row == 3, values * OPACITY, values)
        slopes = pltpu.roll(values, LANES - 1, 1) - values
        ctab[my_zl, z] = jnp.concatenate([values, slopes], axis=0)

    if comm:
        for k in range(1, 4):
            pltpu.make_async_remote_copy(
                src_ref=ctab.at[my_zl], dst_ref=ctab.at[my_zl], send_sem=send_sem.at[3],
                recv_sem=tab_sem, device_id=same_plane(my_x, (my_zl + k) % 4), device_id_type=MESH,
            ).start()

    def first_half(k, carry):
        x_tables(0, k)
        x_rows(0, k)
        send_x(k, 0)
        return carry

    def second_half(k, carry):
        x_tables(1, k)
        x_rows(1, k)
        send_x(k, 1)
        return carry

    def last_part(k, carry):
        send_x(k, 2)
        return carry

    lax.fori_loop(1, 4, first_half, 0)
    lax.fori_loop(0, 4, second_half, 0)
    lax.fori_loop(0, 4, last_part, 0)
    for chunk in range(2):
        recv1[chunk, my_zl * 16 + plane_id] = send1[chunk, 0, 1, my_j]
    fetches[5].wait()

    def make_y(i, carry):
        parity, p, quarter = i // 32, (i % 32) // 2, i % 2
        bc, bs = coarse_row(4 * p + 2 * quarter, y_scale)
        base = (p // 2) * LANES + ((p + parity) % 2) * 64 + quarter * FINE
        base = pl.multiple_of(base, FINE)
        for b in range(NY // 2 // LANES):
            cols = slice(b * LANES, (b + 1) * LANES)
            ec, es = fine_y_ref[parity, 0, :, cols], fine_y_ref[parity, 1, :, cols]
            part = slice((b % 2) * LANES, (b % 2 + 1) * LANES)
            ytab[parity, b // 2, pl.ds(base, FINE), part] = (bc * ec - bs * es).astype(jnp.bfloat16)
            ytab[parity, b // 2, pl.ds(base + 32, FINE), part] = (-(bs * ec + bc * es)).astype(jnp.bfloat16)
        return carry

    lax.fori_loop(0, 64, make_y, 0)

    def table_copy():
        return pltpu.make_async_remote_copy(
            src_ref=ctab.at[pl.ds(0, 3)], dst_ref=ctab.at[pl.ds(0, 3)], send_sem=send_sem.at[3],
            recv_sem=tab_sem, device_id=same_plane(my_x, (my_zl + 1) % 4), device_id_type=MESH,
        )

    def waiting(ref, send_slot, recv, device):
        return pltpu.make_async_remote_copy(
            src_ref=ref, dst_ref=ref, send_sem=send_sem.at[send_slot], recv_sem=recv,
            device_id=device, device_id_type=MESH,
        )

    next_z = same_x((my_z + 1) % 8, my_j)
    next_x = same_plane((my_x + 1) % 4, my_zl)
    next_zl = same_plane(my_x, (my_zl + 1) % 4)
    if comm:
        table_copy().wait_recv()

    low = lax.broadcasted_iota(jnp.int32, (OCT, LANES), 1) < 64

    def transform_y(block, slot, piece):
        parity, depth = piece // 4, slice((piece % 4) * 256, (piece % 4 + 1) * 256)
        part = jnp.dot(lhs[parity, :, depth], ytab[parity, block, depth, :], preferred_element_type=jnp.float32)
        dens[slot, parity] = part if piece % 4 == 0 else dens[slot, parity] + part

    def shade(octet, xs, half, slot, following):
        tiles = [(i, c) for i in range(len(xs)) for c in range(2)]
        signs = [(1 - 2 * (x // 2)).astype(jnp.float32) for x in xs]
        colour = {t: [jnp.zeros((OCT, LANES), jnp.float32) for _ in range(3)] for t in tiles}
        clear = {t: jnp.ones((OCT, LANES), jnp.float32) for t in tiles}
        for z in range(8):
            if following is not None:
                transform_y(*following, z)
            maps = [jnp.broadcast_to(ctab[z // 2, z % 2, q : q + 1, :], (OCT, LANES)) for q in range(8)]
            for t in tiles:
                i, c = t
                at = (slice(z * OCT, (z + 1) * OCT), slice(c * LANES, (c + 1) * LANES))
                d = dens[(slot, 0, *at)] + signs[i] * dens[(slot, 1, *at)]
                position = jnp.clip((d + SPREAD) * ((NCTRL - 1) / (2.0 * SPREAD)), 0.0, NCTRL - 1.0)
                index = position.astype(jnp.int32)
                frac = position - index.astype(jnp.float32)
                value = [
                    jnp.take_along_axis(maps[q], index, axis=1, mode="promise_in_bounds")
                    + frac * jnp.take_along_axis(maps[q + 4], index, axis=1, mode="promise_in_bounds")
                    for q in range(4)
                ]
                weight = clear[t] * value[3]
                colour[t] = [colour[t][q] + weight * value[q] for q in range(3)]
                clear[t] = clear[t] - weight
        for i, c in tiles:
            for q in range(4):
                result = colour[i, c][q] if q < 3 else 1.0 - clear[i, c]
                send2[octet, xs[i], half, q, :, c * LANES : (c + 1) * LANES] = result.astype(jnp.bfloat16)

    def columns_of(c):
        return slice(c * LANES, (c + 1) * LANES)

    def send_part(octet, x, half, own=False):
        if not comm:
            return

        if not own:
            @pl.when(octet < OCTETS - 1)
            def _():
                pltpu.make_async_remote_copy(
                    src_ref=send2.at[octet, x, half], dst_ref=recv2.at[octet, my_x, half],
                    send_sem=send_sem.at[1], recv_sem=recv2_sem.at[octet],
                    device_id=same_plane(x, my_zl), device_id_type=MESH,
                ).start()

        @pl.when(octet == OCTETS - 1)
        def _():
            for c in range(2):
                zl = 2 * half + c
                copy = pltpu.make_async_remote_copy(
                    src_ref=send2.at[OCTETS - 1, x, half, :, :, columns_of(c)],
                    dst_ref=direct.at[my_x * 4 + my_zl], send_sem=send_sem.at[4], recv_sem=direct_sem,
                    device_id=same_plane(x, zl), device_id_type=MESH,
                )
                if own:
                    pl.when(zl != my_zl)(copy.start)
                else:
                    copy.start()

    def over(parts):
        total = [parts(0, q).astype(jnp.float32) for q in range(3)]
        clear = 1.0 - parts(0, 3).astype(jnp.float32)
        for x in range(1, 4):
            for q in range(3):
                total[q] = total[q] + clear * parts(x, q).astype(jnp.float32)
            clear = clear * (1.0 - parts(x, 3).astype(jnp.float32))
        return [*total, clear]

    def combine_last():
        if comm:
            waiting(direct.at[pl.ds(0, 15)], 4, direct_sem, next_x).wait_recv()
        for zl in range(4):
            rows = slice(zl * 32 + 3 * OCT, zl * 32 + 4 * OCT)
            result = over(lambda x, q, zl=zl: direct[x * 4 + zl, q])
            for q in range(4):
                out_ref[q, rows, :] = result[q]

    def combine(octet):
        if comm:
            waiting(recv2.at[octet, pl.ds(0, 3)], 1, recv2_sem.at[octet], next_x).wait_recv()
        rows = pl.ds(pl.multiple_of(my_zl * 32 + octet * OCT, OCT), OCT)
        for zl in range(4):
            half, cols = zl // 2, slice((zl % 2) * LANES, (zl % 2 + 1) * LANES)
            results = over(lambda x, q, half=half, cols=cols: recv2[octet, x, half, q, :, cols])
            for q in range(4):
                result = results[q]
                send3[octet, zl, q] = result.astype(jnp.bfloat16)

                @pl.when(my_zl == zl)
                def _(q=q, result=result):
                    out_ref[q, rows, :] = result

            if comm:
                @pl.when(my_zl != zl)
                def _(zl=zl):
                    pltpu.make_async_remote_copy(
                        src_ref=send3.at[octet, zl], dst_ref=recv3.at[octet, my_zl],
                        send_sem=send_sem.at[2], recv_sem=recv3_sem,
                        device_id=same_plane(my_x, zl), device_id_type=MESH,
                    ).start()

    def slab(octet, carry):
        chunk, part = octet // 2, octet % 2
        if comm:
            @pl.when(octet == 0)
            def _():
                waiting(recv1.at[0, pl.ds(0, 63)], 0, recv1_sem.at[0], next_z).wait_recv()

            for half in range(2):
                @pl.when(octet == 2 + half)
                def _(half=half):
                    waiting(recv1.at[1, pl.ds(0, 63), half], 0, recv1_sem.at[1 + half], next_z).wait_recv()

        for zl in range(4):
            for z in range(2):
                for pair in range(8):
                    first = recv1[chunk, zl * 16 + 2 * pair, part, :, z * LANES : (z + 1) * LANES]
                    second = recv1[chunk, zl * 16 + 2 * pair + 1, part, :, z * LANES : (z + 1) * LANES]
                    rows = slice((2 * zl + z) * OCT, (2 * zl + z + 1) * OCT)
                    cols = slice(pair * LANES, (pair + 1) * LANES)
                    lhs[0, rows, cols] = jnp.where(low, first, second)
                    lhs[1, rows, cols] = jnp.where(low, second, first)

        theirs = 2 * ((my_x + 1) % 2)
        ours = 2 * (my_x % 2)
        others = [(my_x + 1) % 4, (my_x + 3) % 4]
        across = (my_x + 2) % 4
        for piece in range(8):
            transform_y(theirs + 1 - my_zl // 2, 0, piece)
        far, near = 1 - my_zl // 2, my_zl // 2
        shade(octet, others, far, 0, (theirs + near, 1))
        for x in others:
            send_part(octet, x, far)
        shade(octet, others, near, 1, (ours + far, 0))
        for x in others:
            send_part(octet, x, near)
        shade(octet, [across], far, 0, (ours + near, 1))
        send_part(octet, across, far)
        shade(octet, [across], near, 1, None)
        send_part(octet, across, near)

        @pl.when(octet > 0)
        def _():
            combine(octet - 1)

        shade(octet, [my_x], far, 0, None)
        send_part(octet, my_x, far, own=True)
        shade(octet, [my_x], near, 1, None)
        send_part(octet, my_x, near, own=True)

        @pl.when(octet < OCTETS - 1)
        def _():
            recv2[octet, my_x] = send2[octet, my_x]

        return carry

    lax.fori_loop(0, OCTETS, slab, 0)
    for c in range(2):
        @pl.when(my_zl % 2 == c)
        def _(c=c):
            direct[depth_id] = send2[OCTETS - 1, my_x, my_zl // 2, :, :, columns_of(c)]

    if comm:
        waiting(send3.at[:, pl.ds(0, 3)], 2, recv3_sem, next_zl).wait_recv()
        for zl in range(4):
            @pl.when(my_zl != zl)
            def _(zl=zl):
                for octet in range(OCTETS - 1):
                    rows = slice(zl * 32 + octet * OCT, zl * 32 + (octet + 1) * OCT)
                    out_ref[:, rows, :] = recv3[octet, zl].astype(jnp.float32)

    combine_last()

    if comm:
        waiting(recv1.at[:, pl.ds(0, 63)], 0, recv1_sem.at[0], next_z).wait_send()
        waiting(recv2.at[pl.ds(0, 3), pl.ds(0, 3)], 1, recv2_sem.at[0], next_x).wait_send()
        waiting(direct.at[pl.ds(0, 15)], 4, direct_sem, next_x).wait_send()
        waiting(send3.at[:, pl.ds(0, 3)], 2, recv3_sem, next_zl).wait_send()
        table_copy().wait_send()


def render(spectrum, colour_table, map_index, comm=True):
    operands = [spectrum, colour_table, map_index, *map(jnp.asarray, base_tables())]
    vmem = pl.BlockSpec(memory_space=pltpu.VMEM)
    bf16, f32 = jnp.bfloat16, jnp.float32
    return pl.pallas_call(
        functools.partial(kernel, comm=comm),
        out_shape=jax.ShapeDtypeStruct((4, 128, 128), f32),
        in_specs=[pl.BlockSpec(memory_space=pltpu.HBM)] * 6,
        out_specs=vmem,
        scratch_shapes=[
            pltpu.VMEM((2, 2, 64, NX), bf16),
            pltpu.VMEM((NMAPS, 4, NCTRL), f32),
            pltpu.SMEM((2,), jnp.int32),
            pltpu.VMEM((2, FINE, NX), f32),
            pltpu.VMEM((2, 2, FINE, NY // 2), f32),
            pltpu.VMEM((2, 128, LANES), f32),
            pltpu.VMEM((NX, 256), bf16),
            pltpu.VMEM((NX, 256), bf16),
            pltpu.VMEM((256, NX), bf16),
            pltpu.VMEM((256, NX), bf16),
            pltpu.VMEM((2, 4, 2, 8, 2, OCT, 256), bf16),
            pltpu.VMEM((2, 64, 2, OCT, 256), bf16),
            pltpu.VMEM((2, 4, NY // 2, 256), bf16),
            pltpu.VMEM((2, 8 * OCT, NY // 2), bf16),
            pltpu.VMEM((4, 2, 8, LANES), f32),
            pltpu.VMEM((2, 2, 8 * OCT, 256), f32),
            pltpu.VMEM((OCTETS, 4, 2, 4, OCT, 2 * LANES), bf16),
            pltpu.VMEM((OCTETS - 1, 4, 2, 4, OCT, 2 * LANES), bf16),
            pltpu.VMEM((OCTETS - 1, 4, 4, OCT, LANES), bf16),
            pltpu.VMEM((OCTETS - 1, 4, 4, OCT, LANES), bf16),
            pltpu.VMEM((16, 4, OCT, LANES), bf16),
            pltpu.SemaphoreType.DMA((6,)),
            pltpu.SemaphoreType.DMA((5,)),
            pltpu.SemaphoreType.DMA((3,)),
            pltpu.SemaphoreType.DMA((OCTETS - 1,)),
            pltpu.SemaphoreType.DMA,
            pltpu.SemaphoreType.DMA,
            pltpu.SemaphoreType.DMA,
        ],
        compiler_params=pltpu.CompilerParams(
            vmem_limit_bytes=40 << 20,
            **(dict(collective_id=0, has_side_effects=True) if comm else {}),
        ),
        name="render",
    )(*[pltpu.with_memory_space_constraint(operand, pltpu.HBM) for operand in operands])


def solution(mesh):
    return jax.shard_map(
        render,
        mesh=mesh,
        in_specs=(P("depth", None, "plane", None), P(), P("depth")),
        out_specs=P(None, "plane", "depth"),
        check_vma=False,
    )
```

```python
import functools
import math

import jax
import jax.numpy as jnp
import numpy as np
from jax import lax
from jax.experimental import pallas as pl
from jax.experimental.pallas import tpu as pltpu
from jax.sharding import PartitionSpec as P

NX = 2048
NY = 2048
NCTRL = 16
NMAPS = 4
SPREAD = 3.0
OPACITY = 0.06
LANES = 128
FINE = 16
OCTETS = 4
OCT = 8
MESH = pl.DeviceIdType.MESH


def base_tables():
    fine = 2.0 * np.pi * np.outer(np.arange(FINE), np.arange(NX)) / NX
    coarse = 2.0 * np.pi * (np.outer(np.arange(128), np.arange(128)) % 128) / 128.0
    fine_pair = np.stack([np.cos(fine), np.sin(fine)]).astype(np.float32)
    odd_even = 2.0 * np.pi * np.outer(np.arange(2 * FINE), np.arange(NY // 2)) / NY
    fine_y = np.stack([np.cos(odd_even), np.sin(odd_even)]).reshape(2, FINE, 2, NY // 2)
    fine_y = np.ascontiguousarray(fine_y.transpose(2, 0, 1, 3)).astype(np.float32)
    coarse_pair = np.stack([np.cos(coarse), np.sin(coarse)]).astype(np.float32)
    return fine_pair, fine_y, coarse_pair


def quotient(a, b):
    return a // b if isinstance(a, int) else lax.div(a, jnp.int32(b))


def remainder(a, b):
    return a % b if isinstance(a, int) else lax.rem(a, jnp.int32(b))


def kernel(
    spec_hbm, colour_hbm, map_hbm, fine_hbm, fine_y_hbm, coarse_hbm, out_ref,
    spec_ref, colour_ref, map_ref, fine_ref, fine_y_ref, coarse_ref,
    turned_ref, swapped_ref, cos_ref, sin_ref, send1, recv1, ytab, lhs, ctab, dens, send2, recv2, send3, recv3, direct,
    in_sem, send_sem, recv1_sem, recv2_sem, recv3_sem, direct_sem, tab_sem, *, comm
):
    if comm:
        depth_id = lax.axis_index("depth")
        plane_id = lax.axis_index("plane")
    else:
        depth_id = jnp.int32(5)
        plane_id = jnp.int32(6)
    my_x, my_zl = depth_id // 4, depth_id % 4
    my_zh, my_j = plane_id // 8, plane_id % 8
    my_z = my_zh * 4 + my_zl

    fetches = [
        pltpu.make_async_copy(src, dst, in_sem.at[i])
        for i, (src, dst) in enumerate(
            [(fine_hbm, fine_ref), (coarse_hbm, coarse_ref), (spec_hbm, spec_ref),
             (colour_hbm, colour_ref), (map_hbm, map_ref), (fine_y_hbm, fine_y_ref)]
        )
    ]
    for fetch in fetches:
        fetch.start()

    def same_x(z, j):
        return {"depth": my_x * 4 + remainder(z, 4), "plane": quotient(z, 4) * 8 + j}

    def same_plane(x, zl):
        return {"depth": x * 4 + zl, "plane": plane_id}

    if comm:
        barrier = pltpu.get_barrier_semaphore()

        def greet_gather(i, carry):
            z, j = remainder(my_z + quotient(i, 8), 8), remainder(my_j + remainder(i, 8), 8)
            pl.semaphore_signal(barrier, inc=1, device_id=same_x(z, j), device_id_type=MESH)
            return carry

        def greet_depth(i, carry):
            pl.semaphore_signal(
                barrier, inc=1, device_id=same_plane(remainder(my_x + 1 + quotient(i, 4), 4), remainder(i, 4)), device_id_type=MESH
            )
            return carry

        lax.fori_loop(1, 64, greet_gather, 0)
        lax.fori_loop(0, 12, greet_depth, 0)

    x_scale = 1.0 / math.sqrt(NX)
    y_scale = math.sqrt(2.0 / NY)

    def coarse_row(index, scale):
        bc = coarse_ref[0, pl.ds(index, 1), :] * scale
        bs = coarse_ref[1, pl.ds(index, 1), :] * scale
        return jnp.broadcast_to(bc, (FINE, LANES)), jnp.broadcast_to(bs, (FINE, LANES))

    def pair_z(k):
        return remainder(my_z + 4 - k, 8), remainder(my_z + 4 + k + 4 * quotient(4 - k, 4), 8)

    def x_tables(chunk, k):
        for i, z in enumerate(pair_z(k)):
            first = quotient(z, 4) * 64 + 2 * remainder(z, 4) + chunk
            for j in range(8):
                bc, bs = coarse_row(first + 8 * j, x_scale)
                rows = slice((8 * i + j) * FINE, (8 * i + j + 1) * FINE)
                for b in range(NX // LANES):
                    cols = slice(b * LANES, (b + 1) * LANES)
                    ec, es = fine_ref[0, :, cols], fine_ref[1, :, cols]
                    cos_ref[rows, cols] = (bc * ec - bs * es).astype(jnp.bfloat16)
                    sin_ref[rows, cols] = (bs * ec + bc * es).astype(jnp.bfloat16)

    def x_rows(chunk, k):
        rows = jnp.dot(cos_ref[...], turned_ref[...], preferred_element_type=jnp.float32)
        rows += jnp.dot(sin_ref[...], swapped_ref[...], preferred_element_type=jnp.float32)
        send1[chunk, k] = rows.reshape(2, 8, 2, OCT, 256).astype(jnp.bfloat16)

    def x_side(side):
        half = slice(128 * side, 128 * (side + 1))
        rows = jnp.dot(cos_ref[half, :], turned_ref[...], preferred_element_type=jnp.float32)
        rows += jnp.dot(sin_ref[half, :], swapped_ref[...], preferred_element_type=jnp.float32)
        send1[0, 0, side] = rows.reshape(8, 2, OCT, 256).astype(jnp.bfloat16)

    def send_x(k, part, sides=(0, 1)):
        zs = pair_z(k)
        if not comm:
            return

        def send(i, c):
            j = remainder(my_j + i, 8)
            for side in sides:
                z = zs[side]
                if part == 0:
                    src, dst = send1.at[0, k, side, j], recv1.at[0, my_zl * 16 + plane_id]
                else:
                    src = send1.at[1, k, side, j, part - 1]
                    dst = recv1.at[1, my_zl * 16 + plane_id, part - 1]
                copy = pltpu.make_async_remote_copy(
                    src_ref=src, dst_ref=dst, send_sem=send_sem.at[0], recv_sem=recv1_sem.at[part],
                    device_id=same_x(z, j), device_id_type=MESH,
                )
                if side == 0:
                    copy.start()
                else:
                    pl.when(jnp.logical_or(k != 0, i != 0))(copy.start)
            return c

        lax.fori_loop(0, 8, send, 0)

    fetches[0].wait()
    fetches[1].wait()
    x_tables(0, 0)
    fetches[2].wait()

    source = lax.broadcasted_iota(jnp.int32, (256, 256), 0)
    column = lax.broadcasted_iota(jnp.int32, (256, 256), 1)
    part = (column // 32) % 2
    parity = (column // 64 + plane_id) % 2
    base = (column // 128) * 128 + (column % 32) * 2 + parity
    straight = jnp.where(source == base + 64 * part, 1.0, 0.0).astype(jnp.bfloat16)
    crossed = jnp.where(
        source == base + 64 * (1 - part), jnp.where(part == 0, -1.0, 1.0), 0.0
    ).astype(jnp.bfloat16)
    tn = (((0,), (0,)), ((), ()))
    spec = spec_ref[...].reshape(256, NX)
    both = lax.dot_general(
        spec, jnp.concatenate([straight, crossed], axis=1), tn, preferred_element_type=jnp.float32
    ).astype(jnp.bfloat16)
    turned_ref[...] = both[:, :256]
    swapped_ref[...] = both[:, 256:]

    x_side(0)
    if comm:
        pl.semaphore_wait(barrier, 75)
    send_x(0, 0, sides=(0,))
    x_side(1)
    send_x(0, 0, sides=(1,))
    fetches[3].wait()
    fetches[4].wait()

    for z in range(2):
        values = colour_ref[map_ref[z]]
        values = jnp.concatenate([values, jnp.zeros((4, LANES - NCTRL), jnp.float32)], axis=1)
        row = lax.broadcasted_iota(jnp.int32, (4, LANES), 0)
        values = jnp.where(row == 3, values * OPACITY, values)
        slopes = pltpu.roll(values, LANES - 1, 1) - values
        ctab[my_zl, z] = jnp.concatenate([values, slopes], axis=0)

    if comm:
        for k in range(1, 4):
            pltpu.make_async_remote_copy(
                src_ref=ctab.at[my_zl], dst_ref=ctab.at[my_zl], send_sem=send_sem.at[3],
                recv_sem=tab_sem, device_id=same_plane(my_x, (my_zl + k) % 4), device_id_type=MESH,
            ).start()

    def first_half(k, carry):
        x_tables(0, k)
        x_rows(0, k)
        send_x(k, 0)
        return carry

    def second_half(k, carry):
        x_tables(1, k)
        x_rows(1, k)
        send_x(k, 1)
        return carry

    def last_part(k, carry):
        send_x(k, 2)
        return carry

    lax.fori_loop(1, 4, first_half, 0)
    lax.fori_loop(0, 4, second_half, 0)
    lax.fori_loop(0, 4, last_part, 0)
    for chunk in range(2):
        recv1[chunk, my_zl * 16 + plane_id] = send1[chunk, 0, 1, my_j]
    fetches[5].wait()

    def make_y(i, carry):
        parity, p, quarter = i // 32, (i % 32) // 2, i % 2
        bc, bs = coarse_row(4 * p + 2 * quarter, y_scale)
        base = (p // 2) * LANES + ((p + parity) % 2) * 64 + quarter * FINE
        base = pl.multiple_of(base, FINE)
        for b in range(NY // 2 // LANES):
            cols = slice(b * LANES, (b + 1) * LANES)
            ec, es = fine_y_ref[parity, 0, :, cols], fine_y_ref[parity, 1, :, cols]
            part = slice((b % 2) * LANES, (b % 2 + 1) * LANES)
            ytab[parity, b // 2, pl.ds(base, FINE), part] = (bc * ec - bs * es).astype(jnp.bfloat16)
            ytab[parity, b // 2, pl.ds(base + 32, FINE), part] = (-(bs * ec + bc * es)).astype(jnp.bfloat16)
        return carry

    lax.fori_loop(0, 64, make_y, 0)

    def table_copy():
        return pltpu.make_async_remote_copy(
            src_ref=ctab.at[pl.ds(0, 3)], dst_ref=ctab.at[pl.ds(0, 3)], send_sem=send_sem.at[3],
            recv_sem=tab_sem, device_id=same_plane(my_x, (my_zl + 1) % 4), device_id_type=MESH,
        )

    def waiting(ref, send_slot, recv, device):
        return pltpu.make_async_remote_copy(
            src_ref=ref, dst_ref=ref, send_sem=send_sem.at[send_slot], recv_sem=recv,
            device_id=device, device_id_type=MESH,
        )

    next_z = same_x((my_z + 1) % 8, my_j)
    next_x = same_plane((my_x + 1) % 4, my_zl)
    next_zl = same_plane(my_x, (my_zl + 1) % 4)
    if comm:
        table_copy().wait_recv()

    low = lax.broadcasted_iota(jnp.int32, (OCT, LANES), 1) < 64

    def transform_y(block, slot, piece):
        parity, depth = piece // 4, slice((piece % 4) * 256, (piece % 4 + 1) * 256)
        part = jnp.dot(lhs[parity, :, depth], ytab[parity, block, depth, :], preferred_element_type=jnp.float32)
        dens[slot, parity] = part if piece % 4 == 0 else dens[slot, parity] + part

    def shade(octet, xs, half, slot, following):
        tiles = [(i, c) for i in range(len(xs)) for c in range(2)]
        signs = [(1 - 2 * (x // 2)).astype(jnp.float32) for x in xs]
        colour = {t: [jnp.zeros((OCT, LANES), jnp.float32) for _ in range(3)] for t in tiles}
        clear = {t: jnp.ones((OCT, LANES), jnp.float32) for t in tiles}
        for z in range(8):
            if following is not None:
                transform_y(*following, z)
            maps = [jnp.broadcast_to(ctab[z // 2, z % 2, q : q + 1, :], (OCT, LANES)) for q in range(8)]
            for t in tiles:
                i, c = t
                at = (slice(z * OCT, (z + 1) * OCT), slice(c * LANES, (c + 1) * LANES))
                d = dens[(slot, 0, *at)] + signs[i] * dens[(slot, 1, *at)]
                position = jnp.clip((d + SPREAD) * ((NCTRL - 1) / (2.0 * SPREAD)), 0.0, NCTRL - 1.0)
                index = position.astype(jnp.int32)
                frac = position - index.astype(jnp.float32)
                value = [
                    jnp.take_along_axis(maps[q], index, axis=1, mode="promise_in_bounds")
                    + frac * jnp.take_along_axis(maps[q + 4], index, axis=1, mode="promise_in_bounds")
                    for q in range(4)
                ]
                weight = clear[t] * value[3]
                colour[t] = [colour[t][q] + weight * value[q] for q in range(3)]
                clear[t] = clear[t] - weight
        for i, c in tiles:
            for q in range(4):
                result = colour[i, c][q] if q < 3 else 1.0 - clear[i, c]
                send2[octet, xs[i], half, q, :, c * LANES : (c + 1) * LANES] = result.astype(jnp.bfloat16)

    def columns_of(c):
        return slice(c * LANES, (c + 1) * LANES)

    def send_part(octet, x, half, own=False):
        if not comm:
            return

        if not own:
            @pl.when(octet < OCTETS - 1)
            def _():
                pltpu.make_async_remote_copy(
                    src_ref=send2.at[octet, x, half], dst_ref=recv2.at[octet, my_x, half],
                    send_sem=send_sem.at[1], recv_sem=recv2_sem.at[octet],
                    device_id=same_plane(x, my_zl), device_id_type=MESH,
                ).start()

        @pl.when(octet == OCTETS - 1)
        def _():
            for c in range(2):
                zl = 2 * half + c
                copy = pltpu.make_async_remote_copy(
                    src_ref=send2.at[OCTETS - 1, x, half, :, :, columns_of(c)],
                    dst_ref=direct.at[my_x * 4 + my_zl], send_sem=send_sem.at[4], recv_sem=direct_sem,
                    device_id=same_plane(x, zl), device_id_type=MESH,
                )
                if own:
                    pl.when(zl != my_zl)(copy.start)
                else:
                    copy.start()

    def over(parts):
        total = [parts(0, q).astype(jnp.float32) for q in range(3)]
        clear = 1.0 - parts(0, 3).astype(jnp.float32)
        for x in range(1, 4):
            for q in range(3):
                total[q] = total[q] + clear * parts(x, q).astype(jnp.float32)
            clear = clear * (1.0 - parts(x, 3).astype(jnp.float32))
        return [*total, clear]

    def combine_last():
        if comm:
            waiting(direct.at[pl.ds(0, 15)], 4, direct_sem, next_x).wait_recv()
        for zl in range(4):
            rows = slice(zl * 32 + 3 * OCT, zl * 32 + 4 * OCT)
            result = over(lambda x, q, zl=zl: direct[x * 4 + zl, q])
            for q in range(4):
                out_ref[q, rows, :] = result[q]

    def combine(octet):
        if comm:
            waiting(recv2.at[octet, pl.ds(0, 3)], 1, recv2_sem.at[octet], next_x).wait_recv()
        rows = pl.ds(pl.multiple_of(my_zl * 32 + octet * OCT, OCT), OCT)
        for zl in range(4):
            half, cols = zl // 2, slice((zl % 2) * LANES, (zl % 2 + 1) * LANES)
            results = over(lambda x, q, half=half, cols=cols: recv2[octet, x, half, q, :, cols])
            for q in range(4):
                result = results[q]
                send3[octet, zl, q] = result.astype(jnp.bfloat16)

                @pl.when(my_zl == zl)
                def _(q=q, result=result):
                    out_ref[q, rows, :] = result

            if comm:
                @pl.when(my_zl != zl)
                def _(zl=zl):
                    pltpu.make_async_remote_copy(
                        src_ref=send3.at[octet, zl], dst_ref=recv3.at[octet, my_zl],
                        send_sem=send_sem.at[2], recv_sem=recv3_sem,
                        device_id=same_plane(my_x, zl), device_id_type=MESH,
                    ).start()

    def slab(octet, carry):
        chunk, part = octet // 2, octet % 2
        if comm:
            @pl.when(octet == 0)
            def _():
                waiting(recv1.at[0, pl.ds(0, 63)], 0, recv1_sem.at[0], next_z).wait_recv()

            for half in range(2):
                @pl.when(octet == 2 + half)
                def _(half=half):
                    waiting(recv1.at[1, pl.ds(0, 63), half], 0, recv1_sem.at[1 + half], next_z).wait_recv()

        for zl in range(4):
            for z in range(2):
                for pair in range(8):
                    first = recv1[chunk, zl * 16 + 2 * pair, part, :, z * LANES : (z + 1) * LANES]
                    second = recv1[chunk, zl * 16 + 2 * pair + 1, part, :, z * LANES : (z + 1) * LANES]
                    rows = slice((2 * zl + z) * OCT, (2 * zl + z + 1) * OCT)
                    cols = slice(pair * LANES, (pair + 1) * LANES)
                    lhs[0, rows, cols] = jnp.where(low, first, second)
                    lhs[1, rows, cols] = jnp.where(low, second, first)

        theirs = 2 * ((my_x + 1) % 2)
        ours = 2 * (my_x % 2)
        others = [(my_x + 1) % 4, (my_x + 3) % 4]
        across = (my_x + 2) % 4
        for piece in range(8):
            transform_y(theirs + 1 - my_zl // 2, 0, piece)
        far, near = 1 - my_zl // 2, my_zl // 2
        shade(octet, others, far, 0, (theirs + near, 1))
        for x in others:
            send_part(octet, x, far)
        shade(octet, others, near, 1, (ours + far, 0))
        for x in others:
            send_part(octet, x, near)
        shade(octet, [across], far, 0, (ours + near, 1))
        send_part(octet, across, far)
        shade(octet, [across], near, 1, None)
        send_part(octet, across, near)

        @pl.when(octet > 0)
        def _():
            combine(octet - 1)

        shade(octet, [my_x], far, 0, None)
        send_part(octet, my_x, far, own=True)
        shade(octet, [my_x], near, 1, None)
        send_part(octet, my_x, near, own=True)

        @pl.when(octet < OCTETS - 1)
        def _():
            recv2[octet, my_x] = send2[octet, my_x]

        return carry

    lax.fori_loop(0, OCTETS, slab, 0)
    for c in range(2):
        @pl.when(my_zl % 2 == c)
        def _(c=c):
            direct[depth_id] = send2[OCTETS - 1, my_x, my_zl // 2, :, :, columns_of(c)]

    if comm:
        waiting(send3.at[:, pl.ds(0, 3)], 2, recv3_sem, next_zl).wait_recv()
        for zl in range(4):
            @pl.when(my_zl != zl)
            def _(zl=zl):
                for octet in range(OCTETS - 1):
                    rows = slice(zl * 32 + octet * OCT, zl * 32 + (octet + 1) * OCT)
                    out_ref[:, rows, :] = recv3[octet, zl].astype(jnp.float32)

    combine_last()

    if comm:
        waiting(recv1.at[:, pl.ds(0, 63)], 0, recv1_sem.at[0], next_z).wait_send()
        waiting(recv2.at[pl.ds(0, 3), pl.ds(0, 3)], 1, recv2_sem.at[0], next_x).wait_send()
        waiting(direct.at[pl.ds(0, 15)], 4, direct_sem, next_x).wait_send()
        waiting(send3.at[:, pl.ds(0, 3)], 2, recv3_sem, next_zl).wait_send()
        table_copy().wait_send()


def render(spectrum, colour_table, map_index, comm=True):
    operands = [spectrum, colour_table, map_index, *map(jnp.asarray, base_tables())]
    vmem = pl.BlockSpec(memory_space=pltpu.VMEM)
    bf16, f32 = jnp.bfloat16, jnp.float32
    return pl.pallas_call(
        functools.partial(kernel, comm=comm),
        out_shape=jax.ShapeDtypeStruct((4, 128, 128), f32),
        in_specs=[pl.BlockSpec(memory_space=pltpu.HBM)] * 6,
        out_specs=vmem,
        scratch_shapes=[
            pltpu.VMEM((2, 2, 64, NX), bf16),
            pltpu.VMEM((NMAPS, 4, NCTRL), f32),
            pltpu.SMEM((2,), jnp.int32),
            pltpu.VMEM((2, FINE, NX), f32),
            pltpu.VMEM((2, 2, FINE, NY // 2), f32),
            pltpu.VMEM((2, 128, LANES), f32),
            pltpu.VMEM((NX, 256), bf16),
            pltpu.VMEM((NX, 256), bf16),
            pltpu.VMEM((256, NX), bf16),
            pltpu.VMEM((256, NX), bf16),
            pltpu.VMEM((2, 4, 2, 8, 2, OCT, 256), bf16),
            pltpu.VMEM((2, 64, 2, OCT, 256), bf16),
            pltpu.VMEM((2, 4, NY // 2, 256), bf16),
            pltpu.VMEM((2, 8 * OCT, NY // 2), bf16),
            pltpu.VMEM((4, 2, 8, LANES), f32),
            pltpu.VMEM((2, 2, 8 * OCT, 256), f32),
            pltpu.VMEM((OCTETS, 4, 2, 4, OCT, 2 * LANES), bf16),
            pltpu.VMEM((OCTETS - 1, 4, 2, 4, OCT, 2 * LANES), bf16),
            pltpu.VMEM((OCTETS - 1, 4, 4, OCT, LANES), bf16),
            pltpu.VMEM((OCTETS - 1, 4, 4, OCT, LANES), bf16),
            pltpu.VMEM((16, 4, OCT, LANES), bf16),
            pltpu.SemaphoreType.DMA((6,)),
            pltpu.SemaphoreType.DMA((5,)),
            pltpu.SemaphoreType.DMA((3,)),
            pltpu.SemaphoreType.DMA((OCTETS - 1,)),
            pltpu.SemaphoreType.DMA,
            pltpu.SemaphoreType.DMA,
            pltpu.SemaphoreType.DMA,
        ],
        compiler_params=pltpu.CompilerParams(
            vmem_limit_bytes=40 << 20,
            **(dict(collective_id=0, has_side_effects=True) if comm else {}),
        ),
        name="render",
    )(*[pltpu.with_memory_space_constraint(operand, pltpu.HBM) for operand in operands])


def solution(mesh):
    return jax.shard_map(
        render,
        mesh=mesh,
        in_specs=(P("depth", None, "plane", None), P(), P("depth")),
        out_specs=P(None, "plane", "depth"),
        check_vma=False,
    )
```

```python
import functools
import math

import jax
import jax.numpy as jnp
import numpy as np
from jax import lax
from jax.experimental import pallas as pl
from jax.experimental.pallas import tpu as pltpu
from jax.sharding import PartitionSpec as P

NX = 2048
NY = 2048
NCTRL = 16
NMAPS = 4
SPREAD = 3.0
OPACITY = 0.06
LANES = 128
FINE = 16
OCTETS = 4
OCT = 8
MESH = pl.DeviceIdType.MESH


def base_tables():
    fine = 2.0 * np.pi * np.outer(np.arange(FINE), np.arange(NX)) / NX
    coarse = 2.0 * np.pi * (np.outer(np.arange(128), np.arange(128)) % 128) / 128.0
    fine_pair = np.stack([np.cos(fine), np.sin(fine)]).astype(np.float32)
    odd_even = 2.0 * np.pi * np.outer(np.arange(2 * FINE), np.arange(NY // 2)) / NY
    fine_y = np.stack([np.cos(odd_even), np.sin(odd_even)]).reshape(2, FINE, 2, NY // 2)
    fine_y = np.ascontiguousarray(fine_y.transpose(2, 0, 1, 3)).astype(np.float32)
    coarse_pair = np.stack([np.cos(coarse), np.sin(coarse)]).astype(np.float32)
    return fine_pair, fine_y, coarse_pair


def kernel(
    spec_hbm, colour_hbm, map_hbm, fine_hbm, fine_y_hbm, coarse_hbm, out_ref,
    spec_ref, colour_ref, map_ref, fine_ref, fine_y_ref, coarse_ref,
    turned_ref, swapped_ref, cos_ref, sin_ref, send1, recv1, ytab, lhs, ctab, dens, send2, recv2, send3, recv3, direct,
    in_sem, send_sem, recv1_sem, recv2_sem, recv3_sem, direct_sem, tab_sem, *, comm
):
    if comm:
        depth_id = lax.axis_index("depth")
        plane_id = lax.axis_index("plane")
    else:
        depth_id = jnp.int32(5)
        plane_id = jnp.int32(6)
    my_x, my_zl = depth_id // 4, depth_id % 4
    my_zh, my_j = plane_id // 8, plane_id % 8
    my_z = my_zh * 4 + my_zl

    fetches = [
        pltpu.make_async_copy(src, dst, in_sem.at[i])
        for i, (src, dst) in enumerate(
            [(fine_hbm, fine_ref), (coarse_hbm, coarse_ref), (spec_hbm, spec_ref),
             (colour_hbm, colour_ref), (map_hbm, map_ref), (fine_y_hbm, fine_y_ref)]
        )
    ]
    for fetch in fetches:
        fetch.start()

    def same_x(z, j):
        return {"depth": my_x * 4 + z % 4, "plane": (z // 4) * 8 + j}

    def same_plane(x, zl):
        return {"depth": x * 4 + zl, "plane": plane_id}

    if comm:
        barrier = pltpu.get_barrier_semaphore()

        def greet_gather(i, carry):
            z, j = (my_z + i // 8) % 8, (my_j + i % 8) % 8
            pl.semaphore_signal(barrier, inc=1, device_id=same_x(z, j), device_id_type=MESH)
            return carry

        def greet_depth(i, carry):
            pl.semaphore_signal(
                barrier, inc=1, device_id=same_plane((my_x + 1 + i // 4) % 4, i % 4), device_id_type=MESH
            )
            return carry

        lax.fori_loop(1, 64, greet_gather, 0)
        lax.fori_loop(0, 12, greet_depth, 0)

    x_scale = 1.0 / math.sqrt(NX)
    y_scale = math.sqrt(2.0 / NY)

    def coarse_row(index, scale):
        bc = coarse_ref[0, pl.ds(index, 1), :] * scale
        bs = coarse_ref[1, pl.ds(index, 1), :] * scale
        return jnp.broadcast_to(bc, (FINE, LANES)), jnp.broadcast_to(bs, (FINE, LANES))

    def pair_z(k):
        return (my_z + 4 - k) % 8, (my_z + 4 + k + 4 * ((4 - k) // 4)) % 8

    def x_tables(chunk, k):
        for i, z in enumerate(pair_z(k)):
            first = (z // 4) * 64 + 2 * (z % 4) + chunk
            for j in range(8):
                bc, bs = coarse_row(first + 8 * j, x_scale)
                rows = slice((8 * i + j) * FINE, (8 * i + j + 1) * FINE)
                for b in range(NX // LANES):
                    cols = slice(b * LANES, (b + 1) * LANES)
                    ec, es = fine_ref[0, :, cols], fine_ref[1, :, cols]
                    cos_ref[rows, cols] = (bc * ec - bs * es).astype(jnp.bfloat16)
                    sin_ref[rows, cols] = (bs * ec + bc * es).astype(jnp.bfloat16)

    def x_rows(chunk, k):
        rows = jnp.dot(cos_ref[...], turned_ref[...], preferred_element_type=jnp.float32)
        rows += jnp.dot(sin_ref[...], swapped_ref[...], preferred_element_type=jnp.float32)
        send1[chunk, k] = rows.reshape(2, 8, 2, OCT, 256).astype(jnp.bfloat16)

    def x_side(side):
        half = slice(128 * side, 128 * (side + 1))
        rows = jnp.dot(cos_ref[half, :], turned_ref[...], preferred_element_type=jnp.float32)
        rows += jnp.dot(sin_ref[half, :], swapped_ref[...], preferred_element_type=jnp.float32)
        send1[0, 0, side] = rows.reshape(8, 2, OCT, 256).astype(jnp.bfloat16)

    def send_x(k, part, sides=(0, 1)):
        zs = pair_z(k)
        if not comm:
            return

        def send(i, c):
            j = (my_j + i) % 8
            for side in sides:
                z = zs[side]
                if part == 0:
                    src, dst = send1.at[0, k, side, j], recv1.at[0, my_zl * 16 + plane_id]
                else:
                    src = send1.at[1, k, side, j, part - 1]
                    dst = recv1.at[1, my_zl * 16 + plane_id, part - 1]
                copy = pltpu.make_async_remote_copy(
                    src_ref=src, dst_ref=dst, send_sem=send_sem.at[0], recv_sem=recv1_sem.at[part],
                    device_id=same_x(z, j), device_id_type=MESH,
                )
                if side == 0:
                    copy.start()
                else:
                    pl.when(jnp.logical_or(k != 0, i != 0))(copy.start)
            return c

        lax.fori_loop(0, 8, send, 0)

    fetches[0].wait()
    fetches[1].wait()
    x_tables(0, 0)
    fetches[2].wait()

    source = lax.broadcasted_iota(jnp.int32, (256, 256), 0)
    column = lax.broadcasted_iota(jnp.int32, (256, 256), 1)
    part = (column // 32) % 2
    parity = (column // 64 + plane_id) % 2
    base = (column // 128) * 128 + (column % 32) * 2 + parity
    straight = jnp.where(source == base + 64 * part, 1.0, 0.0).astype(jnp.bfloat16)
    crossed = jnp.where(
        source == base + 64 * (1 - part), jnp.where(part == 0, -1.0, 1.0), 0.0
    ).astype(jnp.bfloat16)
    tn = (((0,), (0,)), ((), ()))
    spec = spec_ref[...].reshape(256, NX)
    both = lax.dot_general(
        spec, jnp.concatenate([straight, crossed], axis=1), tn, preferred_element_type=jnp.float32
    ).astype(jnp.bfloat16)
    turned_ref[...] = both[:, :256]
    swapped_ref[...] = both[:, 256:]

    x_side(0)
    if comm:
        pl.semaphore_wait(barrier, 75)
    send_x(0, 0, sides=(0,))
    x_side(1)
    send_x(0, 0, sides=(1,))
    fetches[3].wait()
    fetches[4].wait()

    for z in range(2):
        values = colour_ref[map_ref[z]]
        values = jnp.concatenate([values, jnp.zeros((4, LANES - NCTRL), jnp.float32)], axis=1)
        row = lax.broadcasted_iota(jnp.int32, (4, LANES), 0)
        values = jnp.where(row == 3, values * OPACITY, values)
        slopes = pltpu.roll(values, LANES - 1, 1) - values
        ctab[my_zl, z] = jnp.concatenate([values, slopes], axis=0)

    if comm:
        for k in range(1, 4):
            pltpu.make_async_remote_copy(
                src_ref=ctab.at[my_zl], dst_ref=ctab.at[my_zl], send_sem=send_sem.at[3],
                recv_sem=tab_sem, device_id=same_plane(my_x, (my_zl + k) % 4), device_id_type=MESH,
            ).start()

    def first_half(k, carry):
        x_tables(0, k)
        x_rows(0, k)
        send_x(k, 0)
        return carry

    def second_half(k, carry):
        x_tables(1, k)
        x_rows(1, k)
        send_x(k, 1)
        return carry

    def last_part(k, carry):
        send_x(k, 2)
        return carry

    lax.fori_loop(1, 4, first_half, 0)
    lax.fori_loop(0, 4, second_half, 0)
    lax.fori_loop(0, 4, last_part, 0)
    for chunk in range(2):
        recv1[chunk, my_zl * 16 + plane_id] = send1[chunk, 0, 1, my_j]
    fetches[5].wait()

    def make_y(i, carry):
        parity, p, quarter = i // 32, (i % 32) // 2, i % 2
        bc, bs = coarse_row(4 * p + 2 * quarter, y_scale)
        base = (p // 2) * LANES + ((p + parity) % 2) * 64 + quarter * FINE
        base = pl.multiple_of(base, FINE)
        for b in range(NY // 2 // LANES):
            cols = slice(b * LANES, (b + 1) * LANES)
            ec, es = fine_y_ref[parity, 0, :, cols], fine_y_ref[parity, 1, :, cols]
            part = slice((b % 2) * LANES, (b % 2 + 1) * LANES)
            ytab[parity, b // 2, pl.ds(base, FINE), part] = (bc * ec - bs * es).astype(jnp.bfloat16)
            ytab[parity, b // 2, pl.ds(base + 32, FINE), part] = (-(bs * ec + bc * es)).astype(jnp.bfloat16)
        return carry

    lax.fori_loop(0, 64, make_y, 0)

    def table_copy():
        return pltpu.make_async_remote_copy(
            src_ref=ctab.at[pl.ds(0, 3)], dst_ref=ctab.at[pl.ds(0, 3)], send_sem=send_sem.at[3],
            recv_sem=tab_sem, device_id=same_plane(my_x, (my_zl + 1) % 4), device_id_type=MESH,
        )

    def waiting(ref, send_slot, recv, device):
        return pltpu.make_async_remote_copy(
            src_ref=ref, dst_ref=ref, send_sem=send_sem.at[send_slot], recv_sem=recv,
            device_id=device, device_id_type=MESH,
        )

    next_z = same_x((my_z + 1) % 8, my_j)
    next_x = same_plane((my_x + 1) % 4, my_zl)
    next_zl = same_plane(my_x, (my_zl + 1) % 4)
    if comm:
        table_copy().wait_recv()

    low = lax.broadcasted_iota(jnp.int32, (OCT, LANES), 1) < 64

    def transform_y(block, slot, parity):
        dens[slot, parity] = jnp.dot(lhs[parity], ytab[parity, block], preferred_element_type=jnp.float32)

    def shade(octet, xs, half, slot, following):
        tiles = [(i, c) for i in range(len(xs)) for c in range(2)]
        signs = [(1 - 2 * (x // 2)).astype(jnp.float32) for x in xs]
        colour = {t: [jnp.zeros((OCT, LANES), jnp.float32) for _ in range(3)] for t in tiles}
        clear = {t: jnp.ones((OCT, LANES), jnp.float32) for t in tiles}
        for z in range(8):
            if following is not None and z % 4 == 0:
                transform_y(*following, z // 4)
            maps = [jnp.broadcast_to(ctab[z // 2, z % 2, q : q + 1, :], (OCT, LANES)) for q in range(8)]
            for t in tiles:
                i, c = t
                at = (slice(z * OCT, (z + 1) * OCT), slice(c * LANES, (c + 1) * LANES))
                d = dens[(slot, 0, *at)] + signs[i] * dens[(slot, 1, *at)]
                position = jnp.clip((d + SPREAD) * ((NCTRL - 1) / (2.0 * SPREAD)), 0.0, NCTRL - 1.0)
                index = position.astype(jnp.int32)
                frac = position - index.astype(jnp.float32)
                value = [
                    jnp.take_along_axis(maps[q], index, axis=1, mode="promise_in_bounds")
                    + frac * jnp.take_along_axis(maps[q + 4], index, axis=1, mode="promise_in_bounds")
                    for q in range(4)
                ]
                weight = clear[t] * value[3]
                colour[t] = [colour[t][q] + weight * value[q] for q in range(3)]
                clear[t] = clear[t] - weight
        for i, c in tiles:
            for q in range(4):
                result = colour[i, c][q] if q < 3 else 1.0 - clear[i, c]
                send2[octet, xs[i], half, q, :, c * LANES : (c + 1) * LANES] = result.astype(jnp.bfloat16)

    def columns_of(c):
        return slice(c * LANES, (c + 1) * LANES)

    def send_part(octet, x, half, own=False):
        if not comm:
            return

        if not own:
            @pl.when(octet < OCTETS - 1)
            def _():
                pltpu.make_async_remote_copy(
                    src_ref=send2.at[octet, x, half], dst_ref=recv2.at[octet, my_x, half],
                    send_sem=send_sem.at[1], recv_sem=recv2_sem.at[octet],
                    device_id=same_plane(x, my_zl), device_id_type=MESH,
                ).start()

        @pl.when(octet == OCTETS - 1)
        def _():
            for c in range(2):
                zl = 2 * half + c
                copy = pltpu.make_async_remote_copy(
                    src_ref=send2.at[OCTETS - 1, x, half, :, :, columns_of(c)],
                    dst_ref=direct.at[my_x * 4 + my_zl], send_sem=send_sem.at[4], recv_sem=direct_sem,
                    device_id=same_plane(x, zl), device_id_type=MESH,
                )
                if own:
                    pl.when(zl != my_zl)(copy.start)
                else:
                    copy.start()

    def over(parts):
        total = [parts(0, q).astype(jnp.float32) for q in range(3)]
        clear = 1.0 - parts(0, 3).astype(jnp.float32)
        for x in range(1, 4):
            for q in range(3):
                total[q] = total[q] + clear * parts(x, q).astype(jnp.float32)
            clear = clear * (1.0 - parts(x, 3).astype(jnp.float32))
        return [*total, clear]

    def combine_last():
        if comm:
            waiting(direct.at[pl.ds(0, 15)], 4, direct_sem, next_x).wait_recv()
        for zl in range(4):
            rows = slice(zl * 32 + 3 * OCT, zl * 32 + 4 * OCT)
            result = over(lambda x, q, zl=zl: direct[x * 4 + zl, q])
            for q in range(4):
                out_ref[q, rows, :] = result[q]

    def combine(octet):
        if comm:
            waiting(recv2.at[octet, pl.ds(0, 3)], 1, recv2_sem.at[octet], next_x).wait_recv()
        rows = pl.ds(pl.multiple_of(my_zl * 32 + octet * OCT, OCT), OCT)
        for zl in range(4):
            half, cols = zl // 2, slice((zl % 2) * LANES, (zl % 2 + 1) * LANES)
            results = over(lambda x, q, half=half, cols=cols: recv2[octet, x, half, q, :, cols])
            for q in range(4):
                result = results[q]
                send3[octet, zl, q] = result.astype(jnp.bfloat16)

                @pl.when(my_zl == zl)
                def _(q=q, result=result):
                    out_ref[q, rows, :] = result

            if comm:
                @pl.when(my_zl != zl)
                def _(zl=zl):
                    pltpu.make_async_remote_copy(
                        src_ref=send3.at[octet, zl], dst_ref=recv3.at[octet, my_zl],
                        send_sem=send_sem.at[2], recv_sem=recv3_sem,
                        device_id=same_plane(my_x, zl), device_id_type=MESH,
                    ).start()

    def slab(octet, carry):
        chunk, part = octet // 2, octet % 2
        if comm:
            @pl.when(octet == 0)
            def _():
                waiting(recv1.at[0, pl.ds(0, 63)], 0, recv1_sem.at[0], next_z).wait_recv()

            for half in range(2):
                @pl.when(octet == 2 + half)
                def _(half=half):
                    waiting(recv1.at[1, pl.ds(0, 63), half], 0, recv1_sem.at[1 + half], next_z).wait_recv()

        for zl in range(4):
            for z in range(2):
                for pair in range(8):
                    first = recv1[chunk, zl * 16 + 2 * pair, part, :, z * LANES : (z + 1) * LANES]
                    second = recv1[chunk, zl * 16 + 2 * pair + 1, part, :, z * LANES : (z + 1) * LANES]
                    rows = slice((2 * zl + z) * OCT, (2 * zl + z + 1) * OCT)
                    cols = slice(pair * LANES, (pair + 1) * LANES)
                    lhs[0, rows, cols] = jnp.where(low, first, second)
                    lhs[1, rows, cols] = jnp.where(low, second, first)

        theirs = 2 * ((my_x + 1) % 2)
        ours = 2 * (my_x % 2)
        others = [(my_x + 1) % 4, (my_x + 3) % 4]
        across = (my_x + 2) % 4
        for parity in range(2):
            transform_y(theirs + 1 - my_zl // 2, 0, parity)
        far, near = 1 - my_zl // 2, my_zl // 2
        shade(octet, others, far, 0, (theirs + near, 1))
        for x in others:
            send_part(octet, x, far)
        shade(octet, others, near, 1, (ours + far, 0))
        for x in others:
            send_part(octet, x, near)
        shade(octet, [across], far, 0, (ours + near, 1))
        send_part(octet, across, far)
        shade(octet, [across], near, 1, None)
        send_part(octet, across, near)

        @pl.when(octet > 0)
        def _():
            combine(octet - 1)

        shade(octet, [my_x], far, 0, None)
        send_part(octet, my_x, far, own=True)
        shade(octet, [my_x], near, 1, None)
        send_part(octet, my_x, near, own=True)

        @pl.when(octet < OCTETS - 1)
        def _():
            recv2[octet, my_x] = send2[octet, my_x]

        return carry

    lax.fori_loop(0, OCTETS, slab, 0)
    for c in range(2):
        @pl.when(my_zl % 2 == c)
        def _(c=c):
            direct[depth_id] = send2[OCTETS - 1, my_x, my_zl // 2, :, :, columns_of(c)]

    if comm:
        waiting(send3.at[:, pl.ds(0, 3)], 2, recv3_sem, next_zl).wait_recv()
        for zl in range(4):
            @pl.when(my_zl != zl)
            def _(zl=zl):
                for octet in range(OCTETS - 1):
                    rows = slice(zl * 32 + octet * OCT, zl * 32 + (octet + 1) * OCT)
                    out_ref[:, rows, :] = recv3[octet, zl].astype(jnp.float32)

    combine_last()

    if comm:
        waiting(recv1.at[:, pl.ds(0, 63)], 0, recv1_sem.at[0], next_z).wait_send()
        waiting(recv2.at[pl.ds(0, 3), pl.ds(0, 3)], 1, recv2_sem.at[0], next_x).wait_send()
        waiting(direct.at[pl.ds(0, 15)], 4, direct_sem, next_x).wait_send()
        waiting(send3.at[:, pl.ds(0, 3)], 2, recv3_sem, next_zl).wait_send()
        table_copy().wait_send()


def render(spectrum, colour_table, map_index, comm=True):
    operands = [spectrum, colour_table, map_index, *map(jnp.asarray, base_tables())]
    vmem = pl.BlockSpec(memory_space=pltpu.VMEM)
    bf16, f32 = jnp.bfloat16, jnp.float32
    return pl.pallas_call(
        functools.partial(kernel, comm=comm),
        out_shape=jax.ShapeDtypeStruct((4, 128, 128), f32),
        in_specs=[pl.BlockSpec(memory_space=pltpu.HBM)] * 6,
        out_specs=vmem,
        scratch_shapes=[
            pltpu.VMEM((2, 2, 64, NX), bf16),
            pltpu.VMEM((NMAPS, 4, NCTRL), f32),
            pltpu.SMEM((2,), jnp.int32),
            pltpu.VMEM((2, FINE, NX), f32),
            pltpu.VMEM((2, 2, FINE, NY // 2), f32),
            pltpu.VMEM((2, 128, LANES), f32),
            pltpu.VMEM((NX, 256), bf16),
            pltpu.VMEM((NX, 256), bf16),
            pltpu.VMEM((256, NX), bf16),
            pltpu.VMEM((256, NX), bf16),
            pltpu.VMEM((2, 4, 2, 8, 2, OCT, 256), bf16),
            pltpu.VMEM((2, 64, 2, OCT, 256), bf16),
            pltpu.VMEM((2, 4, NY // 2, 256), bf16),
            pltpu.VMEM((2, 8 * OCT, NY // 2), bf16),
            pltpu.VMEM((4, 2, 8, LANES), f32),
            pltpu.VMEM((2, 2, 8 * OCT, 256), f32),
            pltpu.VMEM((OCTETS, 4, 2, 4, OCT, 2 * LANES), bf16),
            pltpu.VMEM((OCTETS - 1, 4, 2, 4, OCT, 2 * LANES), bf16),
            pltpu.VMEM((OCTETS - 1, 4, 4, OCT, LANES), bf16),
            pltpu.VMEM((OCTETS - 1, 4, 4, OCT, LANES), bf16),
            pltpu.VMEM((16, 4, OCT, LANES), bf16),
            pltpu.SemaphoreType.DMA((6,)),
            pltpu.SemaphoreType.DMA((5,)),
            pltpu.SemaphoreType.DMA((3,)),
            pltpu.SemaphoreType.DMA((OCTETS - 1,)),
            pltpu.SemaphoreType.DMA,
            pltpu.SemaphoreType.DMA,
            pltpu.SemaphoreType.DMA,
        ],
        compiler_params=pltpu.CompilerParams(
            vmem_limit_bytes=40 << 20,
            **(dict(collective_id=0, has_side_effects=True) if comm else {}),
        ),
        name="render",
    )(*[pltpu.with_memory_space_constraint(operand, pltpu.HBM) for operand in operands])


def solution(mesh):
    return jax.shard_map(
        render,
        mesh=mesh,
        in_specs=(P("depth", None, "plane", None), P(), P("depth")),
        out_specs=P(None, "plane", "depth"),
        check_vma=False,
    )
```
